512 devices in a mesh: band: 16 (over x, y_hi), grid: 32 (over y_lo, z, core).
Axes of the slice: x: 4, y: 8 (y_hi: 4, y_lo: 2; y = y_hi * 2 + y_lo), z: 8, core: 2. Of those that a mesh axis runs over, the one named last changes fastest.
Arguments:
- waves: bfloat16 [32, 192, 192, 192], P('band', 'grid'), may hold values from -6 to 6
- potential: bfloat16 [192, 192, 192], P(None, 'grid'), may hold values from -3 to 1
- block_index: int32 [16384], P('grid'), may hold values from 0 to 1727
- atom_of_slot: int32 [16384], P('grid'), may hold values from 0 to 1023, as said below
- projectors: bfloat16 [16384, 8, 128], P('grid'), may hold values from -0.5 to 0.5
- coupling: float32 [1024, 8, 8], P('grid'), may hold values from -8 to 8
Outputs:
- applied: bfloat16 [32, 192, 192, 192], P('band', 'grid')
The draws below stay inside these ranges and needn't reach their ends.
Inputs may be any that keep to these rules, and one draw needn't show every extreme that they name: `atom_of_slot`: atom a has its home slab a // 32; the atom of slot s has its home in slab s // 512 or in one of the two slabs beside it, counted cyclically.
All inputs are finite; a program needn't handle non-finite values.
Results may differ from the reference program's by a relative error of at most 0.015.
Values may be sent and summed in bfloat16 or wider, within the bound.
A program may use at most 64 MiB of HBM per device.

```python
import math
import jax
import jax.numpy as jnp
from jax import lax

N = 192
BANDS = 32
RADIUS = 48
BLOCK = 128
NPROJ = 8
SLAB_BLOCKS = 1728
SLOTS_DEV = 512
SLOTS = 16384
ATOM_SLAB = 32
ATOMS = 1024
N_GRID = 32


def draw_atom_of_slot(key, part):
    slot_ids = jnp.arange(SLOTS, dtype=jnp.int32)
    groups = ATOMS // ATOM_SLAB
    home = slot_ids // SLOTS_DEV
    first_key, second_key = jax.random.split(jax.random.fold_in(key, 7))
    offset = jax.random.randint(first_key, (SLOTS,), -1, 2, dtype=jnp.int32)
    member = jax.random.randint(second_key, (SLOTS,), 0, ATOM_SLAB, dtype=jnp.int32)
    return ((home + offset + groups) % groups * ATOM_SLAB + member).astype(jnp.int32)


def with_ends(result, stream_key, low, largest):
    longest = result.shape.index(max(result.shape))
    spots = []
    for shift in (0, 1):
        where = [jax.random.randint(jax.random.fold_in(stream_key, axis), (), 0, length) for axis, length in enumerate(result.shape)]
        where[longest] = (where[longest] + shift) % result.shape[longest]
        spots.append(tuple(where))
    return result.at[spots[0]].set(low).at[spots[1]].set(largest)


def level_of(rng, dims, cuts, low, largest):
    level = 1.0
    for axis_at, parts in cuts:
        heights = jax.random.uniform(jax.random.fold_in(jax.random.fold_in(rng, 6), axis_at), (parts,), jnp.float32, low / len(cuts), largest / len(cuts))
        level = level * jnp.repeat(jnp.exp(heights), dims[axis_at] // parts).reshape((-1,) + (1,) * (len(dims) - 1 - axis_at))
    return level


def noise(rng, shape, spread, limit, pieces=(), held_as=jnp.bfloat16):
    gain = level_of(rng, shape, pieces, -0.22, 0.18) if pieces else 1.0
    result = jax.random.normal(rng, shape, jnp.float32) * spread * gain
    return jnp.minimum(jnp.maximum(result, -limit), limit).astype(held_as)


def setup_inputs(seed: int = 0) -> dict:
    splits = jax.random.split(jax.random.key(seed), 7)
    waves = noise(splits[0], (BANDS, N, N, N), 1.0, 6.0, ((0, 16), (1, 32)))
    potential = jnp.clip(-3.0 + 4.0 * jax.random.uniform(splits[1], (N, N, N), jnp.float32) ** level_of(splits[1], (N, N, N), ((1, 32),), -0.2, 0.2), -3.0, 1.0).astype(jnp.bfloat16)
    block_index = with_ends(jax.random.randint(splits[2], (SLOTS,), 0, SLAB_BLOCKS), jax.random.fold_in(splits[2], 1), 0, SLAB_BLOCKS - 1).astype(jnp.int32)
    atom_of_slot = draw_atom_of_slot(jax.random.fold_in(splits[6], 71), 0)
    projectors = noise(splits[4], (SLOTS, NPROJ, BLOCK), BLOCK ** -0.5, 0.5, ((0, 32),))
    coupling = noise(splits[5], (ATOMS, NPROJ, NPROJ), 2.0, 8.0, ((0, 32),), jnp.float32)
    return dict(waves=waves, potential=potential, block_index=block_index, atom_of_slot=atom_of_slot, projectors=projectors, coupling=coupling)


def hartley(size):
    counter = jnp.arange(size, dtype=jnp.int32)
    product = counter[:, None] * counter[None, :] % size
    angles = 2.0 * math.pi / size * product.astype(jnp.float32)
    return ((jnp.cos(angles) + jnp.sin(angles)) / math.sqrt(size)).astype(jnp.bfloat16)

def folded_squares(counter, size):
    folded = jnp.minimum(counter, size - counter)
    return (folded * folded).astype(jnp.float32)

def reference(waves, potential, block_index, atom_of_slot, projectors, coupling):
    size = N
    transform = hartley(size).astype(jnp.float32)
    squares = folded_squares(jnp.arange(size, dtype=jnp.int32), size)
    wave_sq = squares[:, None, None] + squares[None, :, None] + squares[None, None, :]
    inside = wave_sq < RADIUS * RADIUS
    kinetic = wave_sq / (RADIUS * RADIUS)
    thick = size // N_GRID
    global_block = jnp.arange(SLOTS, dtype=jnp.int32) // SLOTS_DEV * SLAB_BLOCKS + block_index
    proj_wide = projectors.astype(jnp.float32)
    pot_wide = potential.astype(jnp.float32)
    highest = lax.Precision.HIGHEST

    def apply_one(wave):
        plane_wave = jnp.where(inside, wave, jnp.zeros_like(wave))
        first = jnp.einsum('xyz,kz->xyk', plane_wave.astype(jnp.float32), transform).astype(jnp.bfloat16)
        second = jnp.einsum('xyz,ky->xkz', first.astype(jnp.float32), transform).astype(jnp.bfloat16)
        real_space = jnp.einsum('kx,xyz->kyz', transform, second.astype(jnp.float32)).astype(jnp.bfloat16)
        slabs = real_space.reshape(size, N_GRID, thick, size).transpose(1, 0, 2, 3).reshape(-1, BLOCK)
        rows = slabs[global_block].astype(jnp.float32)
        intersection = jnp.einsum('spq,sq->sp', proj_wide, rows)
        coef = jax.ops.segment_sum(intersection, atom_of_slot, num_segments=ATOMS)
        coupled = jnp.einsum('apq,aq->ap', coupling, coef, precision=highest)
        coupled = lax.optimization_barrier(coupled.astype(jnp.bfloat16)).astype(jnp.float32)
        selected = coupled[atom_of_slot]
        back = jnp.einsum('spq,sp->sq', proj_wide, selected)
        spread_back = jnp.zeros((N_GRID * SLAB_BLOCKS, BLOCK), jnp.float32).at[global_block].add(back)
        spread_back = spread_back.reshape(N_GRID, size, thick, size).transpose(1, 0, 2, 3).reshape(size, size, size)
        mixed = (pot_wide * real_space.astype(jnp.float32) + spread_back).astype(jnp.bfloat16)
        third = jnp.einsum('kx,xyz->kyz', transform, mixed.astype(jnp.float32)).astype(jnp.bfloat16)
        fourth = jnp.einsum('xyz,ky->xkz', third.astype(jnp.float32), transform).astype(jnp.bfloat16)
        fifth = jnp.einsum('xyz,kz->xyk', fourth.astype(jnp.float32), transform)
        total = kinetic * plane_wave.astype(jnp.float32) + fifth
        return jnp.where(inside, total, jnp.zeros_like(total)).astype(jnp.bfloat16)
    return lax.map(apply_one, waves)
```

```python
import functools
import math

import jax
import jax.numpy as jnp
import ml_dtypes
import numpy as np
from jax import lax
from jax.experimental import pallas as pl
from jax.experimental.pallas import tpu as pltpu
from jax.sharding import PartitionSpec as P

MESH = pl.DeviceIdType.MESH
F32, BF16 = jnp.float32, jnp.bfloat16
N, G, T = 192, 32, 6
A = 16
RAD2 = 48 * 48
KEEP = np.concatenate([np.arange(48), np.arange(144, 192)])
OFFSETS = (1, -1, 2, -2)


def tables():
    k = np.arange(N)
    angles = np.float32(2.0 * math.pi / N) * ((k[:, None] * k[None, :]) % N).astype(np.float32)
    c = ((np.cos(angles) + np.sin(angles)) / np.float32(math.sqrt(N))).astype(ml_dtypes.bfloat16)
    c = c.astype(np.float32)
    cy = np.zeros((G, 2, 8, 2, 96), np.float32)
    for par in range(2):
        cy[:, par, :T, par, :] = c[:, KEEP].reshape(G, T, 96)
    cy = cy.reshape(512, 192)
    lx = np.zeros((T, N, 96, 8), np.float32)
    for y in range(T):
        lx[y, :, :, y] = c[:, KEEP]
    lx = lx.reshape(T * N, 768)
    lane = np.arange(128)
    kz = np.where(lane < 64, lane, lane + 64)
    half = c[kz, :] * ((lane < 48) | (lane >= 80))[:, None]
    wz = np.zeros((2, 128, 2, N), np.float32)
    wz[0, :, 0, :] = half
    wz[1, :, 1, :] = half
    wz = wz.reshape(256, 384)
    out = [cy, np.ascontiguousarray(cy.T), lx, np.ascontiguousarray(lx.T), wz, np.ascontiguousarray(wz.T)]
    return [x.astype(ml_dtypes.bfloat16) for x in out]


def dot(a, b):
    return jnp.dot(a, b, preferred_element_type=F32)


def folded_sq(k):
    f = jnp.minimum(k, N - k)
    return f * f


def sphere_sq(kx):
    row = lax.broadcasted_iota(jnp.int32, (96, 128), 0)
    lane = lax.broadcasted_iota(jnp.int32, (96, 128), 1)
    ky = jnp.where(row < 48, row, row + 96)
    kz = jnp.where(lane < 64, lane, lane + 64)
    return folded_sq(kx) + folded_sq(ky) + folded_sq(kz)


def squeeze_z(w):
    return jnp.concatenate([w[:, :64], w[:, 128:]], axis=1)


def main_kernel(
    waves, pot, idx_ref, atom_ref, proj, coup_ref, cy, lx, lxt, wz_ref, wzt_ref, out,
    wlo, whi, cyv, lxv, lxtv, potv, projv, projt, potc, oh1, oh2, oha, exp_up,
    send1, recv1, xbuf, rs, mx, send2, coef_out, coef_in, coup_in,
    load_sem, s1, r1, s2, r2, self_sem, cs, cr, ks, kr,
):
    g = lax.axis_index("grid")
    active = jnp.logical_or(g < 8, g >= 24)
    ai = jnp.where(g < 8, g, g - 16)

    def peer(d):
        return lax.rem(g + d + G, G)

    loads = [
        pltpu.make_async_copy(lx, lxv, load_sem.at[0]),
        pltpu.make_async_copy(lxt, lxtv, load_sem.at[1]),
        pltpu.make_async_copy(pot, potv, load_sem.at[2]),
        pltpu.make_async_copy(proj, projv, load_sem.at[3]),
    ]
    wave_loads = [
        pltpu.make_async_copy(waves.at[:, :, 0:48, :], wlo, load_sem.at[4]),
        pltpu.make_async_copy(waves.at[:, :, 144:192, :], whi, load_sem.at[5]),
        pltpu.make_async_copy(cy, cyv, load_sem.at[6]),
    ]

    @pl.when(active)
    def _():
        for copy in wave_loads:
            copy.start()

    for copy in loads:
        copy.start()

    barrier = pltpu.get_barrier_semaphore()

    def greet(d, carry):
        pl.semaphore_signal(barrier, inc=1, device_id={"grid": peer(d)}, device_id_type=MESH)
        return carry

    lax.fori_loop(1, G, greet, 0)

    @pl.when(active)
    def _():
        for copy in wave_loads:
            copy.wait()
        for kp in range(3):
            parts = []
            for par in range(2):
                kx = g * T + 2 * kp + par
                inside = sphere_sq(kx) < RAD2
                cols = []
                for b in range(2):
                    w = jnp.concatenate([wlo[b, 2 * kp + par], whi[b, 2 * kp + par]], axis=0)
                    w = squeeze_z(w.astype(F32))
                    cols.append(jnp.where(inside, w, 0.0).astype(BF16))
                parts.append(jnp.concatenate(cols, axis=1))
            rhs = jnp.concatenate(parts, axis=0)
            send1[:, kp] = dot(cyv[...], rhs).astype(BF16).reshape(G, 16, 256)

    pl.semaphore_wait(barrier, G - 1)

    def first_copy(d):
        to = peer(d)
        return pltpu.make_async_remote_copy(
            src_ref=send1.at[to], dst_ref=recv1.at[ai], send_sem=s1.at[d], recv_sem=r1.at[ai],
            device_id={"grid": to}, device_id_type=MESH,
        )

    @pl.when(active)
    def _():
        def go(d, carry):
            first_copy(d).start()
            return carry

        lax.fori_loop(1, G, go, 0)
        recv1[ai] = send1[g]

    coup_copies = [
        pltpu.make_async_remote_copy(
            src_ref=coup_ref, dst_ref=coup_in.at[n], send_sem=ks.at[n], recv_sem=kr.at[n],
            device_id={"grid": peer(d)}, device_id_type=MESH,
        )
        for n, d in enumerate(OFFSETS[:2])
    ]
    for copy in coup_copies:
        copy.start()

    idx_row = idx_ref[...]
    atom_row = atom_ref[...]
    atom_row = ((lax.shift_right_logical(atom_row, 5) - g + 33) & 31) * 32 + (atom_row & 31)

    def column(row):
        return jnp.transpose(jnp.broadcast_to(row.astype(F32), (128, 512))).astype(jnp.int32)

    idx_col = column(idx_row)
    idx_col = jnp.concatenate([idx_col, idx_col[:, :64]], axis=1)
    lane192 = lax.broadcasted_iota(jnp.int32, (512, N), 1) * 9
    row192 = lax.broadcasted_iota(jnp.int32, (N, 512), 0) * 9
    for c in range(9):
        oh1[c] = jnp.where(lane192 + c == idx_col, 1.0, 0.0).astype(BF16)
        oh2[c] = jnp.where(row192 + c == idx_row, 1.0, 0.0).astype(BF16)
    lane128 = lax.broadcasted_iota(jnp.int32, (512, 128), 1)
    oha[...] = jnp.where(column(atom_row) == lane128, 1.0, 0.0).astype(BF16)
    up_row = lax.broadcasted_iota(jnp.int32, (128, 2048), 0)
    up_lane = lax.broadcasted_iota(jnp.int32, (128, 2048), 1)
    exp_up[...] = jnp.where(lax.shift_right_logical(up_lane, 7) == up_row, 1.0, 0.0).astype(BF16)
    for copy in loads:
        copy.wait()
    projt[...] = jnp.swapaxes(projv[...].astype(F32), 0, 1)
    pt = jnp.swapaxes(potv[...].astype(F32), 0, 1)
    for j in range(3):
        e, o = pt[2 * j], pt[2 * j + 1]
        potc[3 * j] = e[:, :128]
        potc[3 * j + 1] = jnp.concatenate([e[:, 128:], o[:, :64]], axis=1)
        potc[3 * j + 2] = o[:, 64:]

    def wait_first(i, carry):
        src = jnp.where(i < 8, i, i + 16)

        @pl.when(src != g)
        def _():
            pltpu.make_async_remote_copy(
                src_ref=send1.at[0], dst_ref=recv1.at[i], send_sem=s1.at[0], recv_sem=r1.at[i],
                device_id={"grid": src}, device_id_type=MESH,
            ).wait_recv()

        return carry

    lax.fori_loop(0, A, wait_first, 0)

    for y in range(T):
        xbuf[y] = dot(lxv[y * N : (y + 1) * N, :], recv1[...].reshape(768, 256)).astype(BF16)
    for j in range(3):
        for b in range(2):
            cut = slice(b * 128, (b + 1) * 128)
            eo = jnp.concatenate([xbuf[2 * j, :, cut], xbuf[2 * j + 1, :, cut]], axis=1)
            real = dot(eo, wz_ref[...]).astype(BF16)
            for t in range(3):
                rs[3 * j + t, :, cut] = real[:, t * 128 : (t + 1) * 128]

    rows = dot(oh1[0], rs[0])
    for c in range(1, 9):
        rows = rows + dot(oh1[c], rs[c])
    inter = None
    for b in range(2):
        prod = jnp.concatenate(
            [(projt[p] * rows[:, b * 128 : (b + 1) * 128]).astype(BF16) for p in range(8)], axis=1
        )
        term = lax.dot_general(
            prod, exp_up[:, b * 1024 : (b + 1) * 1024], (((1,), (1,)), ((), ())), preferred_element_type=F32
        )
        inter = term if inter is None else inter + term
    inter_t = jnp.transpose(inter)[:16]
    high = inter_t.astype(BF16)
    low = (inter_t - high.astype(F32)).astype(BF16)
    coef_out[...] = dot(high, oha[...]) + dot(low, oha[...])
    coef_copies = [
        pltpu.make_async_remote_copy(
            src_ref=coef_out, dst_ref=coef_in.at[n], send_sem=cs.at[n], recv_sem=cr.at[n],
            device_id={"grid": peer(d)}, device_id_type=MESH,
        )
        for n, d in enumerate(OFFSETS)
    ]
    for copy in coef_copies:
        copy.start()
    for copy in coup_copies:
        copy.wait()
    coup = coup_in[0] + pltpu.roll(coup_ref[...], 32, 1) + pltpu.roll(coup_in[1], 64, 1)
    for copy in coef_copies:
        copy.wait()
    lane16 = lax.broadcasted_iota(jnp.int32, (16, 128), 1)
    coef = coef_out[...] + pltpu.roll(coef_in[0], 96, 1) + pltpu.roll(coef_in[1], 32, 1)
    coef = coef + jnp.where(lane16 < 32, pltpu.roll(coef_in[2], 64, 1), 0.0)
    coef = coef + jnp.where(
        jnp.logical_and(lane16 >= 64, lane16 < 96), pltpu.roll(coef_in[3], 64, 1), 0.0
    )
    mixed_rows = []
    for b in range(2):
        for p in range(8):
            mixed_rows.append(
                jnp.sum(coup[8 * p : 8 * p + 8] * coef[8 * b : 8 * b + 8], axis=0, keepdims=True)
            )
    coupled = jnp.concatenate(mixed_rows, axis=0).astype(BF16)
    coupled = jnp.concatenate([coupled, jnp.zeros((112, 128), BF16)], axis=0)
    chosen = lax.dot_general(
        oha[...], coupled, (((1,), (1,)), ((), ())), preferred_element_type=F32
    ).astype(BF16)
    backs = []
    for b in range(2):
        back = None
        for p in range(8):
            n = (b * 8 + p) * 128
            term = projt[p] * dot(chosen, exp_up[:, n : n + 128])
            back = term if back is None else back + term
        backs.append(back)
    back = jnp.concatenate(backs, axis=1)
    high = back.astype(BF16)
    low = (back - high.astype(F32)).astype(BF16)

    for c in range(9):
        spread = dot(oh2[c], high) + dot(oh2[c], low)
        local = potc[c]
        local = jnp.concatenate([local, local], axis=1)
        mx[c] = (local * rs[c].astype(F32) + spread).astype(BF16)
    for j in range(3):
        for b in range(2):
            cut = slice(b * 128, (b + 1) * 128)
            row = jnp.concatenate([mx[3 * j + t, :, cut] for t in range(3)], axis=1)
            eo = dot(row, wzt_ref[...]).astype(BF16)
            xbuf[2 * j, :, cut] = eo[:, :128]
            xbuf[2 * j + 1, :, cut] = eo[:, 128:]
    xall = xbuf[...].reshape(T * N, 256)
    for n in range(4):
        send2[4 * n : 4 * n + 4] = (
            dot(lxtv[n * N : (n + 1) * N, :], xall).astype(BF16).reshape(4, 3, 16, 256)
        )

    def second_copy(i):
        to = jnp.where(i < 8, i, i + 16)
        return to, pltpu.make_async_remote_copy(
            src_ref=send2.at[i], dst_ref=out.at[g], send_sem=s2.at[i], recv_sem=r2.at[g],
            device_id={"grid": to}, device_id_type=MESH,
        )

    def go_back(n, carry):
        i = lax.rem(n + g, A)
        to, copy = second_copy(i)

        @pl.when(to != g)
        def _():
            copy.start()

        return carry

    lax.fori_loop(0, A, go_back, 0)

    @pl.when(active)
    def _():
        own = pltpu.make_async_copy(send2.at[ai], out.at[g], self_sem)
        own.start()
        own.wait()

        def wait_sent(d, carry):
            first_copy(d).wait_send()
            return carry

        lax.fori_loop(1, G, wait_sent, 0)

        def wait_second(src, carry):
            @pl.when(src != g)
            def _():
                pltpu.make_async_remote_copy(
                    src_ref=send2.at[0], dst_ref=out.at[src], send_sem=s2.at[0], recv_sem=r2.at[src],
                    device_id={"grid": src}, device_id_type=MESH,
                ).wait_recv()

            return carry

        lax.fori_loop(0, G, wait_second, 0)

    def wait_back(i, carry):
        to, copy = second_copy(i)

        @pl.when(to != g)
        def _():
            copy.wait_send()

        return carry

    lax.fori_loop(0, A, wait_back, 0)


def last_kernel(cyi, recv, waves, out):
    kp = pl.program_id(0)
    g = lax.axis_index("grid")
    active = jnp.logical_or(g < 8, g >= 24)

    @pl.when(active)
    def _():
        f = dot(cyi[...], recv[...].reshape(512, 256))
        for par in range(2):
            ksq = sphere_sq(g * T + 2 * kp + par)
            inside = ksq < RAD2
            kinetic = ksq.astype(F32) / RAD2
            for b in range(2):
                w = jnp.concatenate([waves[b, par, 0:48, :], waves[b, par, 144:192, :]], axis=0)
                w = squeeze_z(w.astype(F32))
                part = f[par * 96 : (par + 1) * 96, b * 128 : (b + 1) * 128]
                total = jnp.where(inside, kinetic * w + part, 0.0)
                wide = jnp.concatenate([total[:, :64], jnp.zeros((96, 64), F32), total[:, 64:]], axis=1)
                wide = wide.astype(BF16)
                out[b, par, 0:48, :] = wide[:48]
                out[b, par, 48:144, :] = jnp.zeros((96, N), BF16)
                out[b, par, 144:192, :] = wide[48:]

    @pl.when(jnp.logical_not(active))
    def _():
        out[...] = jnp.zeros(out.shape, BF16)


def shards(waves, potential, block_index, atom_of_slot, projectors, coupling):
    cy, cyi, lx, lxt, wz, wzt = (jnp.asarray(x) for x in tables())
    coup = jnp.transpose(coupling, (1, 2, 0)).reshape(64, 32)
    coup = jnp.pad(coup, ((0, 0), (0, 96)))
    any_spec = pl.BlockSpec(memory_space=pl.ANY)
    vmem = pl.BlockSpec(memory_space=pltpu.VMEM)
    dma = pltpu.SemaphoreType.DMA
    recv = pl.pallas_call(
        main_kernel,
        name="exchange_and_apply",
        out_shape=jax.ShapeDtypeStruct((G, 3, 16, 256), BF16),
        in_specs=[any_spec, any_spec, vmem, vmem, any_spec, vmem, any_spec, any_spec, any_spec, vmem, vmem],
        out_specs=any_spec,
        scratch_shapes=[
            pltpu.VMEM((2, T, 48, N), BF16),
            pltpu.VMEM((2, T, 48, N), BF16),
            pltpu.VMEM((512, 192), BF16),
            pltpu.VMEM((T * N, 768), BF16),
            pltpu.VMEM((768, T * N), BF16),
            pltpu.VMEM((N, T, N), BF16),
            pltpu.VMEM((512, 8, 128), BF16),
            pltpu.VMEM((8, 512, 128), F32),
            pltpu.VMEM((9, N, 128), F32),
            pltpu.VMEM((9, 512, N), BF16),
            pltpu.VMEM((9, N, 512), BF16),
            pltpu.VMEM((512, 128), BF16),
            pltpu.VMEM((128, 2048), BF16),
            pltpu.VMEM((G, 3, 16, 256), BF16),
            pltpu.VMEM((A, 3, 16, 256), BF16),
            pltpu.VMEM((T, N, 256), BF16),
            pltpu.VMEM((9, N, 256), BF16),
            pltpu.VMEM((9, N, 256), BF16),
            pltpu.VMEM((A, 3, 16, 256), BF16),
            pltpu.VMEM((16, 128), F32),
            pltpu.VMEM((4, 16, 128), F32),
            pltpu.VMEM((2, 64, 128), F32),
            dma((7,)),
            dma((G,)),
            dma((A,)),
            dma((A,)),
            dma((G,)),
            dma,
            dma((4,)),
            dma((4,)),
            dma((2,)),
            dma((2,)),
        ],
        compiler_params=pltpu.CompilerParams(
            collective_id=0, has_side_effects=True, vmem_limit_bytes=48 << 20
        ),
    )(
        waves, potential, block_index.reshape(1, -1), atom_of_slot.reshape(1, -1), projectors, coup,
        cy, lx, lxt, wz, wzt,
    )
    return pl.pallas_call(
        last_kernel,
        name="finish",
        grid=(3,),
        out_shape=jax.ShapeDtypeStruct(waves.shape, BF16),
        in_specs=[
            pl.BlockSpec((192, 512), lambda k: (0, 0)),
            pl.BlockSpec((G, 1, 16, 256), lambda k: (0, k, 0, 0)),
            pl.BlockSpec((2, 2, N, N), lambda k: (0, k, 0, 0)),
        ],
        out_specs=pl.BlockSpec((2, 2, N, N), lambda k: (0, k, 0, 0)),
        compiler_params=pltpu.CompilerParams(vmem_limit_bytes=32 << 20),
    )(cyi, recv, waves)


def solution(mesh):
    in_specs = (
        P("band", "grid", None, None),
        P(None, "grid", None),
        P("grid"),
        P("grid"),
        P("grid", None, None),
        P("grid", None, None),
    )
    out_specs = P("band", "grid", None, None)
    return jax.shard_map(shards, mesh=mesh, in_specs=in_specs, out_specs=out_specs, check_vma=False)
```

```python
import functools
import math

import jax
import jax.numpy as jnp
import ml_dtypes
import numpy as np
from jax import lax
from jax.experimental import pallas as pl
from jax.experimental.pallas import tpu as pltpu
from jax.sharding import PartitionSpec as P

MESH = pl.DeviceIdType.MESH
F32, BF16 = jnp.float32, jnp.bfloat16
N, G, T = 192, 32, 6
A = 16
RAD2 = 48 * 48
KEEP = np.concatenate([np.arange(48), np.arange(144, 192)])
OFFSETS = (1, -1, 2, -2)


def tables():
    k = np.arange(N)
    angles = np.float32(2.0 * math.pi / N) * ((k[:, None] * k[None, :]) % N).astype(np.float32)
    c = ((np.cos(angles) + np.sin(angles)) / np.float32(math.sqrt(N))).astype(ml_dtypes.bfloat16)
    c = c.astype(np.float32)
    cy = np.zeros((G, 2, 8, 2, 96), np.float32)
    for par in range(2):
        cy[:, par, :T, par, :] = c[:, KEEP].reshape(G, T, 96)
    cy = cy.reshape(512, 192)
    cx = c[:, KEEP]
    lane = np.arange(128)
    kz = np.where(lane < 64, lane, lane + 64)
    half = c[kz, :] * ((lane < 48) | (lane >= 80))[:, None]
    wz = np.zeros((2, 128, 2, N), np.float32)
    wz[0, :, 0, :] = half
    wz[1, :, 1, :] = half
    wz = wz.reshape(256, 384)
    out = [cy, cy.T, cx, cx.T, wz, wz.T]
    return [np.ascontiguousarray(x).astype(ml_dtypes.bfloat16) for x in out]


def dot(a, b):
    return jnp.dot(a, b, preferred_element_type=F32)


def folded_sq(k):
    f = jnp.minimum(k, N - k)
    return f * f


def sphere_sq(kx):
    row = lax.broadcasted_iota(jnp.int32, (96, 128), 0)
    lane = lax.broadcasted_iota(jnp.int32, (96, 128), 1)
    ky = jnp.where(row < 48, row, row + 96)
    kz = jnp.where(lane < 64, lane, lane + 64)
    return folded_sq(kx) + folded_sq(ky) + folded_sq(kz)


def squeeze_z(w):
    return jnp.concatenate([w[:, :64], w[:, 128:]], axis=1)


def main_kernel(
    waves, pot, idx, atom, proj, coup, cy, cx, cxt, wz, wzt, out,
    wlo, whi, cyv, cxv, cxtv, wzv, wztv, potv, idxv, atomv, projv, coupv,
    projt, potc, oh1, oh2, oha, exp_up,
    send1, recv1, xbuf, rs, mx, send2, coup_out, coup_in, coef_out, coef_in,
    load_sem, s1, r1, s2, r2, self_sem, cs, cr, ks, kr,
):
    g = lax.axis_index("grid")
    active = jnp.logical_or(g < 8, g >= 24)
    ai = jnp.where(g < 8, g, g - 16)

    def peer(d):
        return lax.rem(g + d + G, G)

    wave_loads = [
        pltpu.make_async_copy(waves.at[:, :, 0:48, :], wlo, load_sem.at[0]),
        pltpu.make_async_copy(waves.at[:, :, 144:192, :], whi, load_sem.at[1]),
        pltpu.make_async_copy(cy, cyv, load_sem.at[2]),
    ]
    pairs = (
        (coup, coupv), (idx, idxv), (atom, atomv), (proj, projv), (pot, potv),
        (cx, cxv), (wz, wzv), (wzt, wztv), (cxt, cxtv),
    )
    loads = [pltpu.make_async_copy(a, b, load_sem.at[3 + n]) for n, (a, b) in enumerate(pairs)]

    @pl.when(active)
    def _():
        for copy in wave_loads:
            copy.start()

    for copy in loads:
        copy.start()

    barrier = pltpu.get_barrier_semaphore()

    def greet(d, carry):
        pl.semaphore_signal(barrier, inc=1, device_id={"grid": peer(d)}, device_id_type=MESH)
        return carry

    lax.fori_loop(1, G, greet, 0)

    @pl.when(active)
    def _():
        for copy in wave_loads:
            copy.wait()
        for kp in range(3):
            parts = []
            for par in range(2):
                kx = g * T + 2 * kp + par
                inside = sphere_sq(kx) < RAD2
                cols = []
                for b in range(2):
                    w = jnp.concatenate([wlo[b, 2 * kp + par], whi[b, 2 * kp + par]], axis=0)
                    w = squeeze_z(w.astype(F32))
                    cols.append(jnp.where(inside, w, 0.0).astype(BF16))
                parts.append(jnp.concatenate(cols, axis=1))
            rhs = jnp.concatenate(parts, axis=0)
            send1[:, kp] = dot(cyv[...], rhs).astype(BF16).reshape(G, 16, 256)

    pl.semaphore_wait(barrier, G - 1)

    def first_copy(d):
        to = peer(d)
        return pltpu.make_async_remote_copy(
            src_ref=send1.at[to], dst_ref=recv1.at[ai], send_sem=s1.at[d], recv_sem=r1.at[ai],
            device_id={"grid": to}, device_id_type=MESH,
        )

    @pl.when(active)
    def _():
        def go(d, carry):
            first_copy(d).start()
            return carry

        lax.fori_loop(1, G, go, 0)
        recv1[ai] = send1[g]

    for copy in loads:
        copy.wait()
    coup_out[...] = jnp.concatenate([coupv[...], jnp.zeros((64, 96), F32)], axis=1)
    coup_copies = [
        pltpu.make_async_remote_copy(
            src_ref=coup_out, dst_ref=coup_in.at[n], send_sem=ks.at[n], recv_sem=kr.at[n],
            device_id={"grid": peer(d)}, device_id_type=MESH,
        )
        for n, d in enumerate(OFFSETS[:2])
    ]
    for copy in coup_copies:
        copy.start()

    idx_row = idxv[...]
    atom_row = atomv[...]
    atom_row = ((lax.shift_right_logical(atom_row, 5) - g + 33) & 31) * 32 + (atom_row & 31)

    def column(row):
        return jnp.transpose(jnp.broadcast_to(row.astype(F32), (128, 512))).astype(jnp.int32)

    idx_col = column(idx_row)
    idx_col = jnp.concatenate([idx_col, idx_col[:, :64]], axis=1)
    lane192 = lax.broadcasted_iota(jnp.int32, (512, N), 1) * 9
    row192 = lax.broadcasted_iota(jnp.int32, (N, 512), 0) * 9
    for c in range(9):
        oh1[c] = jnp.where(lane192 + c == idx_col, 1.0, 0.0).astype(BF16)
        oh2[c] = jnp.where(row192 + c == idx_row, 1.0, 0.0).astype(BF16)
    lane128 = lax.broadcasted_iota(jnp.int32, (512, 128), 1)
    oha[...] = jnp.where(column(atom_row) == lane128, 1.0, 0.0).astype(BF16)
    up_row = lax.broadcasted_iota(jnp.int32, (128, 2048), 0)
    up_lane = lax.broadcasted_iota(jnp.int32, (128, 2048), 1)
    exp_up[...] = jnp.where(lax.shift_right_logical(up_lane, 7) == up_row, 1.0, 0.0).astype(BF16)
    projt[...] = jnp.swapaxes(projv[...].astype(F32), 0, 1)
    pt = potv[...].astype(F32)
    for j in range(3):
        e, o = pt[2 * j], pt[2 * j + 1]
        potc[3 * j] = e[:, :128]
        potc[3 * j + 1] = jnp.concatenate([e[:, 128:], o[:, :64]], axis=1)
        potc[3 * j + 2] = o[:, 64:]

    def wait_first(i, carry):
        src = jnp.where(i < 8, i, i + 16)

        @pl.when(src != g)
        def _():
            pltpu.make_async_remote_copy(
                src_ref=send1.at[0], dst_ref=recv1.at[i], send_sem=s1.at[0], recv_sem=r1.at[i],
                device_id={"grid": src}, device_id_type=MESH,
            ).wait_recv()

        return carry

    lax.fori_loop(0, A, wait_first, 0)

    planes = jnp.swapaxes(recv1[...].reshape(768, 256).astype(F32).reshape(96, 8, 256), 0, 1)
    for y in range(T):
        xbuf[y] = dot(cxv[...], planes[y].astype(BF16)).astype(BF16)
    for j in range(3):
        for b in range(2):
            cut = slice(b * 128, (b + 1) * 128)
            eo = jnp.concatenate([xbuf[2 * j, :, cut], xbuf[2 * j + 1, :, cut]], axis=1)
            real = dot(eo, wzv[...]).astype(BF16)
            for t in range(3):
                rs[3 * j + t, :, cut] = real[:, t * 128 : (t + 1) * 128]

    rows = dot(oh1[0], rs[0])
    for c in range(1, 9):
        rows = rows + dot(oh1[c], rs[c])
    inter = None
    for b in range(2):
        prod = jnp.concatenate(
            [(projt[p] * rows[:, b * 128 : (b + 1) * 128]).astype(BF16) for p in range(8)], axis=1
        )
        term = lax.dot_general(
            prod, exp_up[:, b * 1024 : (b + 1) * 1024], (((1,), (1,)), ((), ())), preferred_element_type=F32
        )
        inter = term if inter is None else inter + term
    inter_t = jnp.transpose(inter)[:16]
    high = inter_t.astype(BF16)
    low = (inter_t - high.astype(F32)).astype(BF16)
    coef_out[...] = dot(high, oha[...]) + dot(low, oha[...])
    coef_copies = [
        pltpu.make_async_remote_copy(
            src_ref=coef_out, dst_ref=coef_in.at[n], send_sem=cs.at[n], recv_sem=cr.at[n],
            device_id={"grid": peer(d)}, device_id_type=MESH,
        )
        for n, d in enumerate(OFFSETS)
    ]
    for copy in coef_copies:
        copy.start()
    for copy in coup_copies:
        copy.wait()
    coup = coup_in[0] + pltpu.roll(coup_out[...], 32, 1) + pltpu.roll(coup_in[1], 64, 1)
    for copy in coef_copies:
        copy.wait()
    lane16 = lax.broadcasted_iota(jnp.int32, (16, 128), 1)
    coef = coef_out[...] + pltpu.roll(coef_in[0], 96, 1) + pltpu.roll(coef_in[1], 32, 1)
    coef = coef + jnp.where(lane16 < 32, pltpu.roll(coef_in[2], 64, 1), 0.0)
    coef = coef + jnp.where(
        jnp.logical_and(lane16 >= 64, lane16 < 96), pltpu.roll(coef_in[3], 64, 1), 0.0
    )
    mixed_rows = []
    for b in range(2):
        for p in range(8):
            mixed_rows.append(
                jnp.sum(coup[8 * p : 8 * p + 8] * coef[8 * b : 8 * b + 8], axis=0, keepdims=True)
            )
    coupled = jnp.concatenate(mixed_rows, axis=0).astype(BF16)
    coupled = jnp.concatenate([coupled, jnp.zeros((112, 128), BF16)], axis=0)
    chosen = lax.dot_general(
        oha[...], coupled, (((1,), (1,)), ((), ())), preferred_element_type=F32
    ).astype(BF16)
    backs = []
    for b in range(2):
        back = None
        for p in range(8):
            n = (b * 8 + p) * 128
            term = projt[p] * dot(chosen, exp_up[:, n : n + 128])
            back = term if back is None else back + term
        backs.append(back)
    back = jnp.concatenate(backs, axis=1)
    high = back.astype(BF16)
    low = (back - high.astype(F32)).astype(BF16)

    for c in range(9):
        spread = dot(oh2[c], high) + dot(oh2[c], low)
        local = potc[c]
        local = jnp.concatenate([local, local], axis=1)
        mx[c] = (local * rs[c].astype(F32) + spread).astype(BF16)
    for j in range(3):
        for b in range(2):
            cut = slice(b * 128, (b + 1) * 128)
            row = jnp.concatenate([mx[3 * j + t, :, cut] for t in range(3)], axis=1)
            eo = dot(row, wztv[...]).astype(BF16)
            xbuf[2 * j, :, cut] = eo[:, :128]
            xbuf[2 * j + 1, :, cut] = eo[:, 128:]
    planes = [dot(cxtv[...], xbuf[y])[None] for y in range(T)] + [jnp.zeros((2, 96, 256), F32)]
    planes = jnp.swapaxes(jnp.concatenate(planes, axis=0), 0, 1)
    send2[...] = planes.reshape(768, 256).astype(BF16).reshape(A, 3, 16, 256)

    def second_copy(i):
        to = jnp.where(i < 8, i, i + 16)
        return to, pltpu.make_async_remote_copy(
            src_ref=send2.at[i], dst_ref=out.at[g], send_sem=s2.at[i], recv_sem=r2.at[g],
            device_id={"grid": to}, device_id_type=MESH,
        )

    def go_back(n, carry):
        i = lax.rem(n + g, A)
        to, copy = second_copy(i)

        @pl.when(to != g)
        def _():
            copy.start()

        return carry

    lax.fori_loop(0, A, go_back, 0)

    @pl.when(active)
    def _():
        own = pltpu.make_async_copy(send2.at[ai], out.at[g], self_sem)
        own.start()
        own.wait()

        def wait_sent(d, carry):
            first_copy(d).wait_send()
            return carry

        lax.fori_loop(1, G, wait_sent, 0)

        def wait_second(src, carry):
            @pl.when(src != g)
            def _():
                pltpu.make_async_remote_copy(
                    src_ref=send2.at[0], dst_ref=out.at[src], send_sem=s2.at[0], recv_sem=r2.at[src],
                    device_id={"grid": src}, device_id_type=MESH,
                ).wait_recv()

            return carry

        lax.fori_loop(0, G, wait_second, 0)

    def wait_back(i, carry):
        to, copy = second_copy(i)

        @pl.when(to != g)
        def _():
            copy.wait_send()

        return carry

    lax.fori_loop(0, A, wait_back, 0)


def last_kernel(cyi, recv, waves, out):
    kp = pl.program_id(0)
    g = lax.axis_index("grid")
    active = jnp.logical_or(g < 8, g >= 24)

    @pl.when(active)
    def _():
        f = dot(cyi[...], recv[...].reshape(512, 256))
        for par in range(2):
            ksq = sphere_sq(g * T + 2 * kp + par)
            inside = ksq < RAD2
            kinetic = ksq.astype(F32) / RAD2
            for b in range(2):
                w = jnp.concatenate([waves[b, par, 0:48, :], waves[b, par, 144:192, :]], axis=0)
                w = squeeze_z(w.astype(F32))
                part = f[par * 96 : (par + 1) * 96, b * 128 : (b + 1) * 128]
                total = jnp.where(inside, kinetic * w + part, 0.0)
                wide = jnp.concatenate([total[:, :64], jnp.zeros((96, 64), F32), total[:, 64:]], axis=1)
                wide = wide.astype(BF16)
                out[b, par, 0:48, :] = wide[:48]
                out[b, par, 48:144, :] = jnp.zeros((96, N), BF16)
                out[b, par, 144:192, :] = wide[48:]

    @pl.when(jnp.logical_not(active))
    def _():
        out[...] = jnp.zeros(out.shape, BF16)


def shards(waves, potential, block_index, atom_of_slot, projectors, coupling):
    cy, cyi, cx, cxt, wz, wzt = (jnp.asarray(x) for x in tables())
    coup = jnp.transpose(coupling, (1, 2, 0)).reshape(64, 32)
    hbm = pl.BlockSpec(memory_space=pltpu.HBM)
    dma = pltpu.SemaphoreType.DMA
    recv = pl.pallas_call(
        main_kernel,
        name="exchange_and_apply",
        out_shape=jax.ShapeDtypeStruct((G, 3, 16, 256), BF16),
        in_specs=[hbm] * 11,
        out_specs=hbm,
        scratch_shapes=[
            pltpu.VMEM((2, T, 48, N), BF16),
            pltpu.VMEM((2, T, 48, N), BF16),
            pltpu.VMEM((512, 192), BF16),
            pltpu.VMEM((N, 96), BF16),
            pltpu.VMEM((96, N), BF16),
            pltpu.VMEM((256, 384), BF16),
            pltpu.VMEM((384, 256), BF16),
            pltpu.VMEM((T, N, N), BF16),
            pltpu.VMEM((1, 512), jnp.int32),
            pltpu.VMEM((1, 512), jnp.int32),
            pltpu.VMEM((512, 8, 128), BF16),
            pltpu.VMEM((64, 32), F32),
            pltpu.VMEM((8, 512, 128), F32),
            pltpu.VMEM((9, N, 128), F32),
            pltpu.VMEM((9, 512, N), BF16),
            pltpu.VMEM((9, N, 512), BF16),
            pltpu.VMEM((512, 128), BF16),
            pltpu.VMEM((128, 2048), BF16),
            pltpu.VMEM((G, 3, 16, 256), BF16),
            pltpu.VMEM((A, 3, 16, 256), BF16),
            pltpu.VMEM((T, N, 256), BF16),
            pltpu.VMEM((9, N, 256), BF16),
            pltpu.VMEM((9, N, 256), BF16),
            pltpu.VMEM((A, 3, 16, 256), BF16),
            pltpu.VMEM((64, 128), F32),
            pltpu.VMEM((2, 64, 128), F32),
            pltpu.VMEM((16, 128), F32),
            pltpu.VMEM((4, 16, 128), F32),
            dma((12,)),
            dma((G,)),
            dma((A,)),
            dma((A,)),
            dma((G,)),
            dma,
            dma((4,)),
            dma((4,)),
            dma((2,)),
            dma((2,)),
        ],
        compiler_params=pltpu.CompilerParams(
            collective_id=0, has_side_effects=True, vmem_limit_bytes=60 << 20
        ),
    )(
        waves, jnp.transpose(potential, (1, 0, 2)), block_index.reshape(1, -1), atom_of_slot.reshape(1, -1),
        projectors, coup, cy, cx, cxt, wz, wzt,
    )
    return pl.pallas_call(
        last_kernel,
        name="finish",
        grid=(3,),
        out_shape=jax.ShapeDtypeStruct(waves.shape, BF16),
        in_specs=[
            pl.BlockSpec((192, 512), lambda k: (0, 0)),
            pl.BlockSpec((G, 1, 16, 256), lambda k: (0, k, 0, 0)),
            pl.BlockSpec((2, 2, N, N), lambda k: (0, k, 0, 0)),
        ],
        out_specs=pl.BlockSpec((2, 2, N, N), lambda k: (0, k, 0, 0)),
        compiler_params=pltpu.CompilerParams(vmem_limit_bytes=60 << 20),
    )(cyi, recv, waves)


def solution(mesh):
    in_specs = (
        P("band", "grid", None, None),
        P(None, "grid", None),
        P("grid"),
        P("grid"),
        P("grid", None, None),
        P("grid", None, None),
    )
    out_specs = P("band", "grid", None, None)
    return jax.shard_map(shards, mesh=mesh, in_specs=in_specs, out_specs=out_specs, check_vma=False)
```

```python
import functools
import math

import jax
import jax.numpy as jnp
import ml_dtypes
import numpy as np
from jax import lax
from jax.experimental import pallas as pl
from jax.experimental.pallas import tpu as pltpu
from jax.sharding import PartitionSpec as P

MESH = pl.DeviceIdType.MESH
F32, BF16 = jnp.float32, jnp.bfloat16
N, G, T = 192, 32, 6
A = 16
RAD2 = 48 * 48
KEEP = np.concatenate([np.arange(48), np.arange(144, 192)])
OFFSETS = (1, -1, 2, -2)


def tables():
    k = np.arange(N)
    angles = np.float32(2.0 * math.pi / N) * ((k[:, None] * k[None, :]) % N).astype(np.float32)
    c = ((np.cos(angles) + np.sin(angles)) / np.float32(math.sqrt(N))).astype(ml_dtypes.bfloat16)
    c = c.astype(np.float32)
    cy = np.zeros((G, 8, 96), np.float32)
    cy[:, :T] = c[:, KEEP].reshape(G, T, 96)
    cy = cy.reshape(256, 96)
    cx = c[:, KEEP].reshape(N, A, T).transpose(0, 2, 1).reshape(N, 96)
    wz = np.zeros((2, 2, 96, 2, 2, N), np.float32)
    for par in range(2):
        for b in range(2):
            wz[par, b, :, b, par, :] = c[KEEP]
    wz = wz.reshape(384, 768)
    out = [cy, cy.T, cx, cx.T, wz, wz.T]
    return [np.ascontiguousarray(x).astype(ml_dtypes.bfloat16) for x in out]


def dot(a, b):
    return jnp.dot(a, b, preferred_element_type=F32)


def folded_sq(k):
    f = jnp.minimum(k, N - k)
    return f * f


def sphere_sq(kx):
    row = lax.broadcasted_iota(jnp.int32, (96, 96), 0)
    lane = lax.broadcasted_iota(jnp.int32, (96, 96), 1)
    ky = jnp.where(row < 48, row, row + 96)
    kz = jnp.where(lane < 48, lane, lane + 96)
    return folded_sq(kx) + folded_sq(ky) + folded_sq(kz)


def kept(low, high):
    w = jnp.concatenate([low, high], axis=0).astype(F32)
    return jnp.concatenate([w[:, :48], w[:, 144:]], axis=1)


def tile(x, n):
    return x[..., n * 128 : (n + 1) * 128]


def main_kernel(
    waves, pot, idx, atom, proj, coup, cy, cx, cxt, wz, wzt, out,
    wlo, whi, cyv, cxv, cxtv, wzv, wztv, potv, idxv, atomv, projv, coupv,
    projt, potc, oh1, oh2, oha, exp_up,
    send1, recv1, rs, mx, send2, coup_out, coup_in, coef_out, coef_in,
    load_sem, s1, r1, s2, r2, self_sem, cs, cr, ks, kr,
):
    g = lax.axis_index("grid")
    active = jnp.logical_or(g < 8, g >= 24)
    ai = jnp.where(g < 8, g, g - 16)

    def peer(d):
        return lax.rem(g + d + G, G)

    wave_loads = [
        pltpu.make_async_copy(waves.at[:, :, 0:48, :], wlo, load_sem.at[0]),
        pltpu.make_async_copy(waves.at[:, :, 144:192, :], whi, load_sem.at[1]),
        pltpu.make_async_copy(cy, cyv, load_sem.at[2]),
    ]
    pairs = (
        (coup, coupv), (idx, idxv), (atom, atomv), (proj, projv), (pot, potv),
        (cx, cxv), (wz, wzv), (wzt, wztv), (cxt, cxtv),
    )
    loads = [pltpu.make_async_copy(a, b, load_sem.at[3 + n]) for n, (a, b) in enumerate(pairs)]

    @pl.when(active)
    def _():
        for copy in wave_loads:
            copy.start()

    for copy in loads:
        copy.start()

    barrier = pltpu.get_barrier_semaphore()

    def greet(d, carry):
        pl.semaphore_signal(barrier, inc=1, device_id={"grid": peer(d)}, device_id_type=MESH)
        return carry

    lax.fori_loop(1, G, greet, 0)

    @pl.when(active)
    def _():
        for copy in wave_loads:
            copy.wait()
        parts = []
        for k in range(T):
            inside = sphere_sq(g * T + k) < RAD2
            for b in range(2):
                parts.append(jnp.where(inside, kept(wlo[b, k], whi[b, k]), 0.0))
        rhs = jnp.concatenate(parts, axis=1).astype(BF16)
        spare = [dot(cyv[...], tile(rhs, n)).reshape(G, 8, 128) for n in (7, 8)]
        sub = lax.broadcasted_iota(jnp.int32, (G, 8, 128), 1)
        for t in range(7):
            plane = dot(cyv[...], tile(rhs, t)).reshape(G, 8, 128)
            if t < T:
                plane = jnp.where(sub == 6, spare[0][:, t : t + 1, :], plane)
                plane = jnp.where(sub == 7, spare[1][:, t : t + 1, :], plane)
            send1[:, :, t * 128 : (t + 1) * 128] = plane.astype(BF16)

    pl.semaphore_wait(barrier, G - 1)

    def first_copy(d):
        to = peer(d)
        return pltpu.make_async_remote_copy(
            src_ref=send1.at[to], dst_ref=recv1.at[ai], send_sem=s1.at[d], recv_sem=r1.at[ai],
            device_id={"grid": to}, device_id_type=MESH,
        )

    @pl.when(active)
    def _():
        def go(d, carry):
            first_copy(d).start()
            return carry

        lax.fori_loop(1, G, go, 0)
        recv1[ai] = send1[g]

    for copy in loads:
        copy.wait()
    coup_out[...] = jnp.concatenate([coupv[...], jnp.zeros((64, 96), F32)], axis=1)
    coup_copies = [
        pltpu.make_async_remote_copy(
            src_ref=coup_out, dst_ref=coup_in.at[n], send_sem=ks.at[n], recv_sem=kr.at[n],
            device_id={"grid": peer(d)}, device_id_type=MESH,
        )
        for n, d in enumerate(OFFSETS[:2])
    ]
    for copy in coup_copies:
        copy.start()

    idx_row = idxv[...]
    atom_row = atomv[...]
    atom_row = ((lax.shift_right_logical(atom_row, 5) - g + 33) & 31) * 32 + (atom_row & 31)

    def column(row):
        return jnp.transpose(jnp.broadcast_to(row.astype(F32), (128, 512))).astype(jnp.int32)

    idx_col = column(idx_row)
    idx_col = jnp.concatenate([idx_col, idx_col[:, :64]], axis=1)
    lane192 = lax.broadcasted_iota(jnp.int32, (512, N), 1) * 9
    row192 = lax.broadcasted_iota(jnp.int32, (N, 512), 0) * 9
    for c in range(9):
        oh1[c] = jnp.where(lane192 + c == idx_col, 1.0, 0.0).astype(BF16)
        oh2[c] = jnp.where(row192 + c == idx_row, 1.0, 0.0).astype(BF16)
    lane128 = lax.broadcasted_iota(jnp.int32, (512, 128), 1)
    oha[...] = jnp.where(column(atom_row) == lane128, 1.0, 0.0).astype(BF16)
    up_row = lax.broadcasted_iota(jnp.int32, (128, 2048), 0)
    up_lane = lax.broadcasted_iota(jnp.int32, (128, 2048), 1)
    exp_up[...] = jnp.where(lax.shift_right_logical(up_lane, 7) == up_row, 1.0, 0.0).astype(BF16)
    projt[...] = jnp.swapaxes(projv[...].astype(F32), 0, 1)
    pt = potv[...].astype(F32)
    for j in range(3):
        e, o = pt[2 * j], pt[2 * j + 1]
        potc[3 * j] = e[:, :128]
        potc[3 * j + 1] = jnp.concatenate([e[:, 128:], o[:, :64]], axis=1)
        potc[3 * j + 2] = o[:, 64:]

    def wait_first(i, carry):
        src = jnp.where(i < 8, i, i + 16)

        @pl.when(src != g)
        def _():
            pltpu.make_async_remote_copy(
                src_ref=send1.at[0], dst_ref=recv1.at[i], send_sem=s1.at[0], recv_sem=r1.at[i],
                device_id={"grid": src}, device_id_type=MESH,
            ).wait_recv()

        return carry

    lax.fori_loop(0, A, wait_first, 0)

    got = jnp.swapaxes(recv1[...].astype(F32), 0, 1)
    stacks = []
    for y in range(T):
        line = jnp.concatenate([got[y], tile(got[6], y), tile(got[7], y)], axis=1)
        stacks.append(jnp.concatenate([line[:, k * N : (k + 1) * N] for k in range(T)], axis=0))
    for j in range(3):
        rhs = jnp.concatenate([stacks[2 * j], stacks[2 * j + 1]], axis=1).astype(BF16)
        part = dot(cxv[...], rhs).astype(BF16)
        real = dot(part, wzv[...]).astype(BF16)
        for t in range(3):
            rs[3 * j + t] = jnp.concatenate([tile(real, t), tile(real, 3 + t)], axis=1)

    rows = dot(oh1[0], rs[0])
    for c in range(1, 9):
        rows = rows + dot(oh1[c], rs[c])
    inter = None
    for b in range(2):
        prod = jnp.concatenate(
            [(projt[p] * rows[:, b * 128 : (b + 1) * 128]).astype(BF16) for p in range(8)], axis=1
        )
        term = lax.dot_general(
            prod, exp_up[:, b * 1024 : (b + 1) * 1024], (((1,), (1,)), ((), ())), preferred_element_type=F32
        )
        inter = term if inter is None else inter + term
    inter_t = jnp.transpose(inter)[:16]
    high = inter_t.astype(BF16)
    low = (inter_t - high.astype(F32)).astype(BF16)
    coef_out[...] = dot(high, oha[...]) + dot(low, oha[...])
    coef_copies = [
        pltpu.make_async_remote_copy(
            src_ref=coef_out, dst_ref=coef_in.at[n], send_sem=cs.at[n], recv_sem=cr.at[n],
            device_id={"grid": peer(d)}, device_id_type=MESH,
        )
        for n, d in enumerate(OFFSETS)
    ]
    for copy in coef_copies:
        copy.start()
    for copy in coup_copies:
        copy.wait()
    coup = coup_in[0] + pltpu.roll(coup_out[...], 32, 1) + pltpu.roll(coup_in[1], 64, 1)
    for copy in coef_copies:
        copy.wait()
    lane16 = lax.broadcasted_iota(jnp.int32, (16, 128), 1)
    coef = coef_out[...] + pltpu.roll(coef_in[0], 96, 1) + pltpu.roll(coef_in[1], 32, 1)
    coef = coef + jnp.where(lane16 < 32, pltpu.roll(coef_in[2], 64, 1), 0.0)
    coef = coef + jnp.where(
        jnp.logical_and(lane16 >= 64, lane16 < 96), pltpu.roll(coef_in[3], 64, 1), 0.0
    )
    mixed_rows = []
    for b in range(2):
        for p in range(8):
            mixed_rows.append(
                jnp.sum(coup[8 * p : 8 * p + 8] * coef[8 * b : 8 * b + 8], axis=0, keepdims=True)
            )
    coupled = jnp.concatenate(mixed_rows, axis=0).astype(BF16)
    coupled = jnp.concatenate([coupled, jnp.zeros((112, 128), BF16)], axis=0)
    chosen = lax.dot_general(
        oha[...], coupled, (((1,), (1,)), ((), ())), preferred_element_type=F32
    ).astype(BF16)
    backs = []
    for b in range(2):
        back = None
        for p in range(8):
            n = (b * 8 + p) * 128
            term = projt[p] * dot(chosen, exp_up[:, n : n + 128])
            back = term if back is None else back + term
        backs.append(back)
    back = jnp.concatenate(backs, axis=1)
    high = back.astype(BF16)
    low = (back - high.astype(F32)).astype(BF16)

    for c in range(9):
        spread = dot(oh2[c], high) + dot(oh2[c], low)
        local = potc[c]
        local = jnp.concatenate([local, local], axis=1)
        mx[c] = (local * rs[c].astype(F32) + spread).astype(BF16)
    lines = []
    for j in range(3):
        row = jnp.concatenate([tile(mx[3 * j + t], b) for b in range(2) for t in range(3)], axis=1)
        part = dot(row, wztv[...]).astype(BF16)
        back = dot(cxtv[...], part)
        for par in range(2):
            lines.append(
                jnp.concatenate(
                    [back[k * A : (k + 1) * A, par * N : (par + 1) * N] for k in range(T)], axis=1
                )
            )
    spare = [
        jnp.concatenate([tile(line, n) for line in lines] + [jnp.zeros((A, 128), F32)], axis=1)
        for n in (7, 8)
    ]
    lines = jnp.concatenate([line[None, :, :896] for line in lines] + [x[None] for x in spare], axis=0)
    send2[...] = jnp.swapaxes(lines, 0, 1).astype(BF16)

    def second_copy(i):
        to = jnp.where(i < 8, i, i + 16)
        return to, pltpu.make_async_remote_copy(
            src_ref=send2.at[i], dst_ref=out.at[g], send_sem=s2.at[i], recv_sem=r2.at[g],
            device_id={"grid": to}, device_id_type=MESH,
        )

    def go_back(n, carry):
        i = lax.rem(n + g, A)
        to, copy = second_copy(i)

        @pl.when(to != g)
        def _():
            copy.start()

        return carry

    lax.fori_loop(0, A, go_back, 0)

    @pl.when(active)
    def _():
        own = pltpu.make_async_copy(send2.at[ai], out.at[g], self_sem)
        own.start()
        own.wait()

        def wait_sent(d, carry):
            first_copy(d).wait_send()
            return carry

        lax.fori_loop(1, G, wait_sent, 0)

        def wait_second(src, carry):
            @pl.when(src != g)
            def _():
                pltpu.make_async_remote_copy(
                    src_ref=send2.at[0], dst_ref=out.at[src], send_sem=s2.at[0], recv_sem=r2.at[src],
                    device_id={"grid": src}, device_id_type=MESH,
                ).wait_recv()

            return carry

        lax.fori_loop(0, G, wait_second, 0)

    def wait_back(i, carry):
        to, copy = second_copy(i)

        @pl.when(to != g)
        def _():
            copy.wait_send()

        return carry

    lax.fori_loop(0, A, wait_back, 0)


def last_kernel(cyt, recv, waves, out):
    g = lax.axis_index("grid")
    active = jnp.logical_or(g < 8, g >= 24)

    @pl.when(active)
    def _():
        got = recv[...].astype(F32)
        sub = lax.broadcasted_iota(jnp.int32, (G, 8, 128), 1)
        planes = [got]
        for row in (6, 7):
            spare = jnp.zeros((G, 8, 128), F32)
            for y in range(T):
                spare = jnp.where(sub == y, tile(got, y)[:, row : row + 1, :], spare)
            planes.append(spare)
        planes = jnp.concatenate(planes, axis=2).reshape(256, 1152).astype(BF16)
        fifth = dot(cyt[...], planes)
        for k in range(T):
            ksq = sphere_sq(g * T + k)
            inside = ksq < RAD2
            kinetic = ksq.astype(F32) / RAD2
            for b in range(2):
                n = (2 * k + b) * 96
                w = kept(waves[b, k, 0:48, :], waves[b, k, 144:192, :])
                total = jnp.where(inside, kinetic * w + fifth[:, n : n + 96], 0.0)
                wide = jnp.concatenate([total[:, :48], jnp.zeros((96, 96), F32), total[:, 48:]], axis=1)
                wide = wide.astype(BF16)
                out[b, k, 0:48, :] = wide[:48]
                out[b, k, 48:144, :] = jnp.zeros((96, N), BF16)
                out[b, k, 144:192, :] = wide[48:]

    @pl.when(jnp.logical_not(active))
    def _():
        out[...] = jnp.zeros(out.shape, BF16)


def shards(waves, potential, block_index, atom_of_slot, projectors, coupling):
    cy, cyt, cx, cxt, wz, wzt = (jnp.asarray(x) for x in tables())
    coup = jnp.transpose(coupling, (1, 2, 0)).reshape(64, 32)
    hbm = pl.BlockSpec(memory_space=pltpu.HBM)
    vmem = pl.BlockSpec(memory_space=pltpu.VMEM)
    dma = pltpu.SemaphoreType.DMA
    recv = pl.pallas_call(
        main_kernel,
        name="exchange_and_apply",
        out_shape=jax.ShapeDtypeStruct((G, 8, 896), BF16),
        in_specs=[hbm] * 11,
        out_specs=hbm,
        scratch_shapes=[
            pltpu.VMEM((2, T, 48, N), BF16),
            pltpu.VMEM((2, T, 48, N), BF16),
            pltpu.VMEM((256, 96), BF16),
            pltpu.VMEM((N, 96), BF16),
            pltpu.VMEM((96, N), BF16),
            pltpu.VMEM((384, 768), BF16),
            pltpu.VMEM((768, 384), BF16),
            pltpu.VMEM((T, N, N), BF16),
            pltpu.VMEM((1, 512), jnp.int32),
            pltpu.VMEM((1, 512), jnp.int32),
            pltpu.VMEM((512, 8, 128), BF16),
            pltpu.VMEM((64, 32), F32),
            pltpu.VMEM((8, 512, 128), F32),
            pltpu.VMEM((9, N, 128), F32),
            pltpu.VMEM((9, 512, N), BF16),
            pltpu.VMEM((9, N, 512), BF16),
            pltpu.VMEM((512, 128), BF16),
            pltpu.VMEM((128, 2048), BF16),
            pltpu.VMEM((G, 8, 896), BF16),
            pltpu.VMEM((A, 8, 896), BF16),
            pltpu.VMEM((9, N, 256), BF16),
            pltpu.VMEM((9, N, 256), BF16),
            pltpu.VMEM((A, 8, 896), BF16),
            pltpu.VMEM((64, 128), F32),
            pltpu.VMEM((2, 64, 128), F32),
            pltpu.VMEM((16, 128), F32),
            pltpu.VMEM((4, 16, 128), F32),
            dma((12,)),
            dma((G,)),
            dma((A,)),
            dma((A,)),
            dma((G,)),
            dma,
            dma((4,)),
            dma((4,)),
            dma((2,)),
            dma((2,)),
        ],
        compiler_params=pltpu.CompilerParams(
            collective_id=0, has_side_effects=True, vmem_limit_bytes=60 << 20
        ),
    )(
        waves, jnp.transpose(potential, (1, 0, 2)), block_index.reshape(1, -1), atom_of_slot.reshape(1, -1),
        projectors, coup, cy, cx, cxt, wz, wzt,
    )
    return pl.pallas_call(
        last_kernel,
        name="finish",
        out_shape=jax.ShapeDtypeStruct(waves.shape, BF16),
        in_specs=[vmem] * 3,
        out_specs=vmem,
        compiler_params=pltpu.CompilerParams(vmem_limit_bytes=60 << 20),
    )(cyt, recv, waves)


def solution(mesh):
    in_specs = (
        P("band", "grid", None, None),
        P(None, "grid", None),
        P("grid"),
        P("grid"),
        P("grid", None, None),
        P("grid", None, None),
    )
    out_specs = P("band", "grid", None, None)
    return jax.shard_map(shards, mesh=mesh, in_specs=in_specs, out_specs=out_specs, check_vma=False)
```

```python
import functools
import math

import jax
import jax.numpy as jnp
import ml_dtypes
import numpy as np
from jax import lax
from jax.experimental import pallas as pl
from jax.experimental.pallas import tpu as pltpu
from jax.sharding import PartitionSpec as P

MESH = pl.DeviceIdType.MESH
F32, BF16 = jnp.float32, jnp.bfloat16
N, G, T = 192, 32, 6
A = 16
RAD2 = 48 * 48
KEEP = np.concatenate([np.arange(48), np.arange(144, 192)])
OFFSETS = (1, -1, 2, -2)
FIRST = ((0, 4, 0), (4, 3, 5))
SECOND = ((0, 3, 0), (3, 4, 4))


def tables():
    k = np.arange(N)
    angles = np.float32(2.0 * math.pi / N) * ((k[:, None] * k[None, :]) % N).astype(np.float32)
    c = ((np.cos(angles) + np.sin(angles)) / np.float32(math.sqrt(N))).astype(ml_dtypes.bfloat16)
    c = c.astype(np.float32)
    cy = np.zeros((G, 8, 96), np.float32)
    cy[:, :T] = c[:, KEEP].reshape(G, T, 96)
    cy = cy.reshape(256, 96)
    cx = c[:, KEEP].reshape(N, A, T).transpose(0, 2, 1).reshape(N, 96)
    wz = np.zeros((2, 96, 2, N), np.float32)
    for par in range(2):
        wz[par, :, par, :] = c[KEEP]
    wz = wz.reshape(192, 384)
    out = [cy, cy.T, cx, cx.T, wz, wz.T]
    return [np.ascontiguousarray(x).astype(ml_dtypes.bfloat16) for x in out]


def dot(a, b):
    return jnp.dot(a, b, preferred_element_type=F32)


def folded_sq(k):
    f = jnp.minimum(k, N - k)
    return f * f


def sphere_sq(kx):
    row = lax.broadcasted_iota(jnp.int32, (96, 96), 0)
    lane = lax.broadcasted_iota(jnp.int32, (96, 96), 1)
    ky = jnp.where(row < 48, row, row + 96)
    kz = jnp.where(lane < 48, lane, lane + 96)
    return folded_sq(kx) + folded_sq(ky) + folded_sq(kz)


def kept(low, high):
    w = jnp.concatenate([low, high], axis=0).astype(F32)
    return jnp.concatenate([w[:, :48], w[:, 144:]], axis=1)


def tile(x, n):
    return x[..., n * 128 : (n + 1) * 128]


def main_kernel(
    waves, pot, idx, atom, proj, coup, cy, cx, cxt, wz, wzt, out,
    wlo, whi, cyv, cxv, cxtv, wzv, wztv, potv, idxv, atomv, projv, coupv,
    projt, potc, oh1, oh2, oha, exp_up,
    send1, recv1, rs, send2, coup_out, coup_in, coef_out, coef_in,
    load_sem, s1, r1, s2, r2, self_sem, cs, cr, ks, kr,
):
    g = lax.axis_index("grid")
    active = jnp.logical_or(g < 8, g >= 24)
    ai = jnp.where(g < 8, g, g - 16)

    def peer(d):
        return lax.rem(g + d + G, G)

    wave_loads = [
        pltpu.make_async_copy(waves.at[:, :, 0:48, :], wlo, load_sem.at[0]),
        pltpu.make_async_copy(waves.at[:, :, 144:192, :], whi, load_sem.at[1]),
        pltpu.make_async_copy(cy, cyv, load_sem.at[2]),
    ]
    pairs = (
        (coup, coupv), (idx, idxv), (atom, atomv), (proj, projv), (pot, potv),
        (cx, cxv), (wz, wzv), (wzt, wztv), (cxt, cxtv),
    )
    loads = [pltpu.make_async_copy(a, b, load_sem.at[3 + n]) for n, (a, b) in enumerate(pairs)]

    @pl.when(active)
    def _():
        for copy in wave_loads:
            copy.start()

    for copy in loads:
        copy.start()

    barrier = pltpu.get_barrier_semaphore()

    def greet(d, carry):
        pl.semaphore_signal(barrier, inc=1, device_id={"grid": peer(d)}, device_id_type=MESH)
        return carry

    lax.fori_loop(1, G, greet, 0)

    @pl.when(active)
    def _():
        for copy in wave_loads:
            copy.wait()
        parts = []
        for b in range(2):
            for k in range(T):
                inside = sphere_sq(g * T + k) < RAD2
                parts.append(jnp.where(inside, kept(wlo[b, k], whi[b, k]), 0.0))
        rhs = jnp.concatenate(parts, axis=1).astype(BF16)
        sub = lax.broadcasted_iota(jnp.int32, (G, 8, 128), 1)
        for wire, count, begin in FIRST:
            spare = dot(cyv[...], tile(rhs, begin + count)).reshape(G, 8, 128)
            for t in range(count):
                plane = dot(cyv[...], tile(rhs, begin + t)).reshape(G, 8, 128)
                for row, y in ((6, t), (7, t + count)):
                    if y < T:
                        plane = jnp.where(sub == row, spare[:, y : y + 1, :], plane)
                send1[:, :, (wire + t) * 128 : (wire + t + 1) * 128] = plane.astype(BF16)

    pl.semaphore_wait(barrier, G - 1)

    def half(ref, i, plan, h):
        return ref.at[i, :, pl.ds(plan[h][0] * 128, plan[h][1] * 128)]

    def first_copy(d, h):
        to = peer(d)
        return pltpu.make_async_remote_copy(
            src_ref=half(send1, to, FIRST, h), dst_ref=half(recv1, ai, FIRST, h),
            send_sem=s1.at[h, d], recv_sem=r1.at[h, ai],
            device_id={"grid": to}, device_id_type=MESH,
        )

    @pl.when(active)
    def _():
        for h in range(2):

            def go(d, carry):
                first_copy(d, h).start()
                return carry

            lax.fori_loop(1, G, go, 0)
        recv1[ai] = send1[g]

    for copy in loads:
        copy.wait()
    coup_out[...] = jnp.concatenate([coupv[...], jnp.zeros((64, 96), F32)], axis=1)
    coup_copies = [
        pltpu.make_async_remote_copy(
            src_ref=coup_out, dst_ref=coup_in.at[n], send_sem=ks.at[n], recv_sem=kr.at[n],
            device_id={"grid": peer(d)}, device_id_type=MESH,
        )
        for n, d in enumerate(OFFSETS[:2])
    ]
    for copy in coup_copies:
        copy.start()

    idx_row = idxv[...]
    atom_row = atomv[...]
    atom_row = ((lax.shift_right_logical(atom_row, 5) - g + 33) & 31) * 32 + (atom_row & 31)

    def column(row):
        return jnp.transpose(jnp.broadcast_to(row.astype(F32), (128, 512))).astype(jnp.int32)

    idx_col = column(idx_row)
    idx_col = jnp.concatenate([idx_col, idx_col[:, :64]], axis=1)
    lane192 = lax.broadcasted_iota(jnp.int32, (512, N), 1) * 9
    row192 = lax.broadcasted_iota(jnp.int32, (N, 512), 0) * 9
    for c in range(9):
        oh1[c] = jnp.where(lane192 + c == idx_col, 1.0, 0.0).astype(BF16)
        oh2[c] = jnp.where(row192 + c == idx_row, 1.0, 0.0).astype(BF16)
    lane128 = lax.broadcasted_iota(jnp.int32, (512, 128), 1)
    oha[...] = jnp.where(column(atom_row) == lane128, 1.0, 0.0).astype(BF16)
    up_row = lax.broadcasted_iota(jnp.int32, (128, 1024), 0)
    up_lane = lax.broadcasted_iota(jnp.int32, (128, 1024), 1)
    exp_up[...] = jnp.where(lax.shift_right_logical(up_lane, 7) == up_row, 1.0, 0.0).astype(BF16)
    projt[...] = jnp.swapaxes(projv[...].astype(F32), 0, 1)
    pt = potv[...].astype(F32)
    for j in range(3):
        e, o = pt[2 * j], pt[2 * j + 1]
        potc[3 * j] = e[:, :128]
        potc[3 * j + 1] = jnp.concatenate([e[:, 128:], o[:, :64]], axis=1)
        potc[3 * j + 2] = o[:, 64:]

    def wait_first(h):
        def body(i, carry):
            src = jnp.where(i < 8, i, i + 16)

            @pl.when(src != g)
            def _():
                pltpu.make_async_remote_copy(
                    src_ref=half(send1, 0, FIRST, h), dst_ref=half(recv1, i, FIRST, h),
                    send_sem=s1.at[h, 0], recv_sem=r1.at[h, i],
                    device_id={"grid": src}, device_id_type=MESH,
                ).wait_recv()

            return carry

        lax.fori_loop(0, A, body, 0)

    def arrived(h):
        wire, count, _ = FIRST[h]
        return jnp.swapaxes(recv1[:, :, wire * 128 : (wire + count) * 128].astype(F32), 0, 1)

    def folded(got, y, count):
        return tile(got[6 + y // count], y % count)

    def coef_copies(b):
        return [
            pltpu.make_async_remote_copy(
                src_ref=coef_out.at[b], dst_ref=coef_in.at[b, n], send_sem=cs.at[b, n], recv_sem=cr.at[b, n],
                device_id={"grid": peer(d)}, device_id_type=MESH,
            )
            for n, d in enumerate(OFFSETS)
        ]

    def project(b, lines):
        stacks = [
            jnp.concatenate([line[:, k * 96 : (k + 1) * 96] for k in range(T)], axis=0) for line in lines
        ]
        for j in range(3):
            rhs = jnp.concatenate([stacks[2 * j], stacks[2 * j + 1]], axis=1).astype(BF16)
            part = dot(cxv[...], rhs).astype(BF16)
            real = dot(part, wzv[...]).astype(BF16)
            for t in range(3):
                rs[b, 3 * j + t] = tile(real, t)
        rows = dot(oh1[0], rs[b, 0])
        for c in range(1, 9):
            rows = rows + dot(oh1[c], rs[b, c])
        prod = jnp.concatenate([(projt[p] * rows).astype(BF16) for p in range(8)], axis=1)
        inter = lax.dot_general(
            prod, exp_up[...], (((1,), (1,)), ((), ())), preferred_element_type=F32
        )
        inter = jnp.transpose(inter)[:16]
        high = inter.astype(BF16)
        low = (inter - high.astype(F32)).astype(BF16)
        coef_out[b] = (dot(high, oha[...]) + dot(low, oha[...]))[:8]
        for copy in coef_copies(b):
            copy.start()

    def apply(b, coup):
        for copy in coef_copies(b):
            copy.wait()
        lane = lax.broadcasted_iota(jnp.int32, (8, 128), 1)
        coef = coef_out[b] + pltpu.roll(coef_in[b, 0], 96, 1) + pltpu.roll(coef_in[b, 1], 32, 1)
        coef = coef + jnp.where(lane < 32, pltpu.roll(coef_in[b, 2], 64, 1), 0.0)
        coef = coef + jnp.where(
            jnp.logical_and(lane >= 64, lane < 96), pltpu.roll(coef_in[b, 3], 64, 1), 0.0
        )
        coupled = [jnp.sum(coup[8 * p : 8 * p + 8] * coef, axis=0, keepdims=True) for p in range(8)]
        coupled = jnp.concatenate(coupled + [jnp.zeros((120, 128), F32)], axis=0).astype(BF16)
        chosen = lax.dot_general(
            oha[...], coupled, (((1,), (1,)), ((), ())), preferred_element_type=F32
        ).astype(BF16)
        back = projt[0] * dot(chosen, tile(exp_up[...], 0))
        for p in range(1, 8):
            back = back + projt[p] * dot(chosen, tile(exp_up[...], p))
        back = back.astype(BF16)
        lines = []
        for j in range(3):
            row = []
            for c in range(3 * j, 3 * j + 3):
                row.append((potc[c] * rs[b, c].astype(F32) + dot(oh2[c], back)).astype(BF16))
            part = dot(jnp.concatenate(row, axis=1), wztv[...]).astype(BF16)
            part = dot(cxtv[...], part)
            for par in range(2):
                lines.append(
                    jnp.concatenate(
                        [part[k * A : (k + 1) * A, par * 96 : (par + 1) * 96] for k in range(T)], axis=1
                    )
                )
        return lines

    def second_copy(i, h):
        to = jnp.where(i < 8, i, i + 16)
        return to, pltpu.make_async_remote_copy(
            src_ref=half(send2, i, SECOND, h), dst_ref=half(out, g, SECOND, h),
            send_sem=s2.at[h, i], recv_sem=r2.at[h, g],
            device_id={"grid": to}, device_id_type=MESH,
        )

    def send_back(lines, h):
        wire, count, _ = SECOND[h]
        rows = [line[:, : count * 128] for line in lines]
        for first in (0, count):
            spare = [
                lines[y][:, count * 128 :] if y < T else jnp.zeros((A, 128), F32)
                for y in range(first, first + count)
            ]
            rows.append(jnp.concatenate(spare, axis=1))
        rows = jnp.concatenate([row[None] for row in rows], axis=0)
        send2[:, :, wire * 128 : (wire + count) * 128] = jnp.swapaxes(rows, 0, 1).astype(BF16)

        def go(n, carry):
            i = lax.rem(n + g, A)
            to, copy = second_copy(i, h)

            @pl.when(to != g)
            def _():
                copy.start()

            return carry

        lax.fori_loop(0, A, go, 0)

    wait_first(0)
    got = arrived(0)
    tails = [folded(got, y, 4) for y in range(T)]
    project(0, [jnp.concatenate([got[y], tails[y][:, :64]], axis=1) for y in range(T)])
    wait_first(1)
    got = arrived(1)
    project(1, [jnp.concatenate([tails[y][:, 64:], got[y], folded(got, y, 3)], axis=1) for y in range(T)])
    for copy in coup_copies:
        copy.wait()
    coup = coup_in[0] + pltpu.roll(coup_out[...], 32, 1) + pltpu.roll(coup_in[1], 64, 1)
    lines0 = apply(0, coup)
    send_back([line[:, :512] for line in lines0], 0)
    lines1 = apply(1, coup)
    send_back([jnp.concatenate([a[:, 512:], b], axis=1) for a, b in zip(lines0, lines1)], 1)

    @pl.when(active)
    def _():
        own = pltpu.make_async_copy(send2.at[ai], out.at[g], self_sem)
        own.start()
        own.wait()
        for h in range(2):

            def wait_sent(d, carry):
                first_copy(d, h).wait_send()
                return carry

            lax.fori_loop(1, G, wait_sent, 0)

            def wait_second(src, carry):
                @pl.when(src != g)
                def _():
                    pltpu.make_async_remote_copy(
                        src_ref=half(send2, 0, SECOND, h), dst_ref=half(out, src, SECOND, h),
                        send_sem=s2.at[h, 0], recv_sem=r2.at[h, src],
                        device_id={"grid": src}, device_id_type=MESH,
                    ).wait_recv()

                return carry

            lax.fori_loop(0, G, wait_second, 0)

    for h in range(2):

        def wait_back(i, carry):
            to, copy = second_copy(i, h)

            @pl.when(to != g)
            def _():
                copy.wait_send()

            return carry

        lax.fori_loop(0, A, wait_back, 0)


def last_kernel(cyt, recv, waves, out):
    g = lax.axis_index("grid")
    active = jnp.logical_or(g < 8, g >= 24)

    @pl.when(active)
    def _():
        got = recv[...].astype(F32)
        sub = lax.broadcasted_iota(jnp.int32, (G, 8, 128), 1)
        planes = []
        for wire, count, _ in SECOND:
            planes += [tile(got, wire + t) for t in range(count)]
            spare = jnp.zeros((G, 8, 128), F32)
            for y in range(T):
                row = 6 + y // count
                spare = jnp.where(sub == y, tile(got, wire + y % count)[:, row : row + 1, :], spare)
            planes.append(spare)
        planes = jnp.concatenate(planes, axis=2).reshape(256, 1152).astype(BF16)
        fifth = dot(cyt[...], planes)
        for k in range(T):
            ksq = sphere_sq(g * T + k)
            inside = ksq < RAD2
            kinetic = ksq.astype(F32) / RAD2
            for b in range(2):
                n = (b * T + k) * 96
                w = kept(waves[b, k, 0:48, :], waves[b, k, 144:192, :])
                total = jnp.where(inside, kinetic * w + fifth[:, n : n + 96], 0.0)
                wide = jnp.concatenate([total[:, :48], jnp.zeros((96, 96), F32), total[:, 48:]], axis=1)
                wide = wide.astype(BF16)
                out[b, k, 0:48, :] = wide[:48]
                out[b, k, 48:144, :] = jnp.zeros((96, N), BF16)
                out[b, k, 144:192, :] = wide[48:]

    @pl.when(jnp.logical_not(active))
    def _():
        out[...] = jnp.zeros(out.shape, BF16)


def shards(waves, potential, block_index, atom_of_slot, projectors, coupling):
    cy, cyt, cx, cxt, wz, wzt = (jnp.asarray(x) for x in tables())
    coup = jnp.transpose(coupling, (1, 2, 0)).reshape(64, 32)
    hbm = pl.BlockSpec(memory_space=pltpu.HBM)
    vmem = pl.BlockSpec(memory_space=pltpu.VMEM)
    dma = pltpu.SemaphoreType.DMA
    recv = pl.pallas_call(
        main_kernel,
        name="exchange_and_apply",
        out_shape=jax.ShapeDtypeStruct((G, 8, 896), BF16),
        in_specs=[hbm] * 11,
        out_specs=hbm,
        scratch_shapes=[
            pltpu.VMEM((2, T, 48, N), BF16),
            pltpu.VMEM((2, T, 48, N), BF16),
            pltpu.VMEM((256, 96), BF16),
            pltpu.VMEM((N, 96), BF16),
            pltpu.VMEM((96, N), BF16),
            pltpu.VMEM((192, 384), BF16),
            pltpu.VMEM((384, 192), BF16),
            pltpu.VMEM((T, N, N), BF16),
            pltpu.VMEM((1, 512), jnp.int32),
            pltpu.VMEM((1, 512), jnp.int32),
            pltpu.VMEM((512, 8, 128), BF16),
            pltpu.VMEM((64, 32), F32),
            pltpu.VMEM((8, 512, 128), F32),
            pltpu.VMEM((9, N, 128), F32),
            pltpu.VMEM((9, 512, N), BF16),
            pltpu.VMEM((9, N, 512), BF16),
            pltpu.VMEM((512, 128), BF16),
            pltpu.VMEM((128, 1024), BF16),
            pltpu.VMEM((G, 8, 896), BF16),
            pltpu.VMEM((A, 8, 896), BF16),
            pltpu.VMEM((2, 9, N, 128), BF16),
            pltpu.VMEM((A, 8, 896), BF16),
            pltpu.VMEM((64, 128), F32),
            pltpu.VMEM((2, 64, 128), F32),
            pltpu.VMEM((2, 8, 128), F32),
            pltpu.VMEM((2, 4, 8, 128), F32),
            dma((12,)),
            dma((2, G)),
            dma((2, A)),
            dma((2, A)),
            dma((2, G)),
            dma,
            dma((2, 4)),
            dma((2, 4)),
            dma((2,)),
            dma((2,)),
        ],
        compiler_params=pltpu.CompilerParams(
            collective_id=0, has_side_effects=True, vmem_limit_bytes=60 << 20
        ),
    )(
        waves, jnp.transpose(potential, (1, 0, 2)), block_index.reshape(1, -1), atom_of_slot.reshape(1, -1),
        projectors, coup, cy, cx, cxt, wz, wzt,
    )
    return pl.pallas_call(
        last_kernel,
        name="finish",
        out_shape=jax.ShapeDtypeStruct(waves.shape, BF16),
        in_specs=[vmem] * 3,
        out_specs=vmem,
        compiler_params=pltpu.CompilerParams(vmem_limit_bytes=60 << 20),
    )(cyt, recv, waves)


def solution(mesh):
    in_specs = (
        P("band", "grid", None, None),
        P(None, "grid", None),
        P("grid"),
        P("grid"),
        P("grid", None, None),
        P("grid", None, None),
    )
    out_specs = P("band", "grid", None, None)
    return jax.shard_map(shards, mesh=mesh, in_specs=in_specs, out_specs=out_specs, check_vma=False)
```

```python
import functools
import math

import jax
import jax.numpy as jnp
import ml_dtypes
import numpy as np
from jax import lax
from jax.experimental import pallas as pl
from jax.experimental.pallas import tpu as pltpu
from jax.sharding import PartitionSpec as P

MESH = pl.DeviceIdType.MESH
F32, BF16 = jnp.float32, jnp.bfloat16
N, G, T = 192, 32, 6
A = 16
RAD2 = 48 * 48
KEEP = np.concatenate([np.arange(48), np.arange(144, 192)])
OFFSETS = (1, -1, 2, -2)
DIRECT = 512


def tables():
    k = np.arange(N)
    angles = np.float32(2.0 * math.pi / N) * ((k[:, None] * k[None, :]) % N).astype(np.float32)
    c = ((np.cos(angles) + np.sin(angles)) / np.float32(math.sqrt(N))).astype(ml_dtypes.bfloat16)
    c = c.astype(np.float32)
    cy = np.zeros((G, 8, 96), np.float32)
    cy[:, :T] = c[:, KEEP].reshape(G, T, 96)
    cy = cy.reshape(256, 96)
    cx = c[:, KEEP].reshape(N, A, T).transpose(0, 2, 1).reshape(N, 96)
    wz = np.zeros((2, 2, 96, 2, 2, N), np.float32)
    for par in range(2):
        for b in range(2):
            wz[par, b, :, b, par, :] = c[KEEP]
    wz = wz.reshape(384, 768)
    out = [cy, cy.T, cx, cx.T, wz, wz.T]
    return [np.ascontiguousarray(x).astype(ml_dtypes.bfloat16) for x in out]


def dot(a, b):
    return jnp.dot(a, b, preferred_element_type=F32)


def folded_sq(k):
    f = jnp.minimum(k, N - k)
    return f * f


def sphere_sq(kx):
    row = lax.broadcasted_iota(jnp.int32, (96, 96), 0)
    lane = lax.broadcasted_iota(jnp.int32, (96, 96), 1)
    ky = jnp.where(row < 48, row, row + 96)
    kz = jnp.where(lane < 48, lane, lane + 96)
    return folded_sq(kx) + folded_sq(ky) + folded_sq(kz)


def kept(low, high):
    w = jnp.concatenate([low, high], axis=0).astype(F32)
    return jnp.concatenate([w[:, :48], w[:, 144:]], axis=1)


def tile(x, n):
    return x[..., n * 128 : (n + 1) * 128]


def main_kernel(
    waves, pot, idx, atom, proj, coup, cy, cx, cxt, wz, wzt, out,
    wlo, whi, cyv, cxv, cxtv, wzv, wztv, potv, idxv, atomv, projv, coupv,
    projt, potc, oh1, oh2, oha, exp_up,
    send1, recv1, rel1, rs, mx, send2, rel2, coup_out, coup_in, coef_out, coef_in,
    load_sem, s1, s1b, r1, r1b, rr1, f1, s2, s2b, r2, r2b, rr2, f2, self_sem, cs, cr, ks, kr,
):
    g = lax.axis_index("grid")
    active = jnp.logical_or(g < 8, g >= 24)
    ai = jnp.where(g < 8, g, g - 16)

    def peer(d):
        return lax.rem(g + d + G, G)

    wave_loads = [
        pltpu.make_async_copy(waves.at[:, :, 0:48, :], wlo, load_sem.at[0]),
        pltpu.make_async_copy(waves.at[:, :, 144:192, :], whi, load_sem.at[1]),
        pltpu.make_async_copy(cy, cyv, load_sem.at[2]),
    ]
    pairs = (
        (coup, coupv), (idx, idxv), (atom, atomv), (proj, projv), (pot, potv),
        (cx, cxv), (wz, wzv), (wzt, wztv), (cxt, cxtv),
    )
    loads = [pltpu.make_async_copy(a, b, load_sem.at[3 + n]) for n, (a, b) in enumerate(pairs)]

    @pl.when(active)
    def _():
        for copy in wave_loads:
            copy.start()

    for copy in loads:
        copy.start()

    barrier = pltpu.get_barrier_semaphore()

    def greet(d, carry):
        pl.semaphore_signal(barrier, inc=1, device_id={"grid": peer(d)}, device_id_type=MESH)
        return carry

    lax.fori_loop(1, G, greet, 0)

    @pl.when(active)
    def _():
        for copy in wave_loads:
            copy.wait()
        parts = []
        for k in range(T):
            inside = sphere_sq(g * T + k) < RAD2
            for b in range(2):
                parts.append(jnp.where(inside, kept(wlo[b, k], whi[b, k]), 0.0))
        rhs = jnp.concatenate(parts, axis=1).astype(BF16)
        spare = [dot(cyv[...], tile(rhs, n)).reshape(G, 8, 128) for n in (7, 8)]
        sub = lax.broadcasted_iota(jnp.int32, (G, 8, 128), 1)
        for t in range(7):
            plane = dot(cyv[...], tile(rhs, t)).reshape(G, 8, 128)
            if t < T:
                plane = jnp.where(sub == 6, spare[0][:, t : t + 1, :], plane)
                plane = jnp.where(sub == 7, spare[1][:, t : t + 1, :], plane)
            send1[:, :, t * 128 : (t + 1) * 128] = plane.astype(BF16)

    pl.semaphore_wait(barrier, G - 1)

    my_row = g // A
    partner = lax.rem(g + A, G)
    head = (slice(None), pl.ds(0, DIRECT))
    tail = (slice(None), pl.ds(DIRECT, 896 - DIRECT))

    def remote(src, dst, send, recv, to):
        return pltpu.make_async_remote_copy(
            src_ref=src, dst_ref=dst, send_sem=send, recv_sem=recv,
            device_id={"grid": to}, device_id_type=MESH,
        )

    def owner(i):
        return jnp.where(i < 8, i, i + 16)

    def is_whole(a):
        return jnp.logical_or(a // A == my_row, a == partner)

    def each(low, high, start, skip, body):
        def step(n, carry):
            i = low + lax.rem(n + start, high - low)

            @pl.when(jnp.logical_not(skip(i)))
            def _():
                body(i)

            return carry

        lax.fori_loop(0, high - low, step, 0)

    def itself(a):
        return a == g

    def forwarded1(to):
        return remote(
            send1.at[(to, *tail)], rel1.at[lax.rem(ai, 8)], s1b.at[to], rr1.at[lax.rem(ai, 8)],
            lax.rem(to + A, G),
        )

    def whole1(to):
        return remote(send1.at[to], recv1.at[ai], s1.at[to], r1.at[ai], to)

    def part1(to):
        return remote(send1.at[(to, *head)], recv1.at[(ai, *head)], s1.at[to], r1.at[ai], to)

    def either(test, yes, no):
        pl.when(test)(yes)
        pl.when(jnp.logical_not(test))(no)

    @pl.when(active)
    def _():
        each(0, G, g, is_whole, lambda to: forwarded1(to).start())
        each(
            0, G, g, itself,
            lambda to: either(is_whole(to), lambda: whole1(to).start(), lambda: part1(to).start()),
        )
        recv1[ai] = send1[g]

    for copy in loads:
        copy.wait()
    coup_out[...] = jnp.concatenate([coupv[...], jnp.zeros((64, 96), F32)], axis=1)
    coup_copies = [
        pltpu.make_async_remote_copy(
            src_ref=coup_out, dst_ref=coup_in.at[n], send_sem=ks.at[n], recv_sem=kr.at[n],
            device_id={"grid": peer(d)}, device_id_type=MESH,
        )
        for n, d in enumerate(OFFSETS[:2])
    ]
    for copy in coup_copies:
        copy.start()

    idx_row = idxv[...]
    atom_row = atomv[...]
    atom_row = ((lax.shift_right_logical(atom_row, 5) - g + 33) & 31) * 32 + (atom_row & 31)

    def column(row):
        return jnp.transpose(jnp.broadcast_to(row.astype(F32), (128, 512))).astype(jnp.int32)

    idx_col = column(idx_row)
    idx_col = jnp.concatenate([idx_col, idx_col[:, :64]], axis=1)
    lane192 = lax.broadcasted_iota(jnp.int32, (512, N), 1) * 9
    row192 = lax.broadcasted_iota(jnp.int32, (N, 512), 0) * 9
    for c in range(9):
        oh1[c] = jnp.where(lane192 + c == idx_col, 1.0, 0.0).astype(BF16)
        oh2[c] = jnp.where(row192 + c == idx_row, 1.0, 0.0).astype(BF16)
    lane128 = lax.broadcasted_iota(jnp.int32, (512, 128), 1)
    oha[...] = jnp.where(column(atom_row) == lane128, 1.0, 0.0).astype(BF16)
    up_row = lax.broadcasted_iota(jnp.int32, (128, 2048), 0)
    up_lane = lax.broadcasted_iota(jnp.int32, (128, 2048), 1)
    exp_up[...] = jnp.where(lax.shift_right_logical(up_lane, 7) == up_row, 1.0, 0.0).astype(BF16)
    projt[...] = jnp.swapaxes(projv[...].astype(F32), 0, 1)
    pt = potv[...].astype(F32)
    for j in range(3):
        e, o = pt[2 * j], pt[2 * j + 1]
        potc[3 * j] = e[:, :128]
        potc[3 * j + 1] = jnp.concatenate([e[:, 128:], o[:, :64]], axis=1)
        potc[3 * j + 2] = o[:, 64:]

    def pass1(k):
        i = my_row * 8 + k
        return remote(rel1.at[k], recv1.at[(i, *tail)], f1.at[k], r1b.at[i], partner)

    def relay1(k):
        remote(send1.at[(0, *tail)], rel1.at[k], s1b.at[0], rr1.at[k], partner).wait_recv()
        pass1(k).start()

    def own_row(k):
        return owner(my_row * 8 + k) == g

    each(0, 8, 0, own_row, relay1)

    def wait1(i):
        src = owner(i)

        def parts():
            remote(send1.at[(0, *head)], recv1.at[(i, *head)], s1.at[0], r1.at[i], src).wait_recv()
            remote(rel1.at[0], recv1.at[(i, *tail)], f1.at[0], r1b.at[i], partner).wait_recv()

        either(
            is_whole(src),
            lambda: remote(send1.at[0], recv1.at[i], s1.at[0], r1.at[i], src).wait_recv(),
            parts,
        )

    each(0, A, 0, lambda i: owner(i) == g, wait1)

    got = jnp.swapaxes(recv1[...].astype(F32), 0, 1)
    stacks = []
    for y in range(T):
        line = jnp.concatenate([got[y], tile(got[6], y), tile(got[7], y)], axis=1)
        stacks.append(jnp.concatenate([line[:, k * N : (k + 1) * N] for k in range(T)], axis=0))
    for j in range(3):
        rhs = jnp.concatenate([stacks[2 * j], stacks[2 * j + 1]], axis=1).astype(BF16)
        part = dot(cxv[...], rhs).astype(BF16)
        real = dot(part, wzv[...]).astype(BF16)
        for t in range(3):
            rs[3 * j + t] = jnp.concatenate([tile(real, t), tile(real, 3 + t)], axis=1)

    rows = dot(oh1[0], rs[0])
    for c in range(1, 9):
        rows = rows + dot(oh1[c], rs[c])
    inter = None
    for b in range(2):
        prod = jnp.concatenate(
            [(projt[p] * rows[:, b * 128 : (b + 1) * 128]).astype(BF16) for p in range(8)], axis=1
        )
        term = lax.dot_general(
            prod, exp_up[:, b * 1024 : (b + 1) * 1024], (((1,), (1,)), ((), ())), preferred_element_type=F32
        )
        inter = term if inter is None else inter + term
    inter_t = jnp.transpose(inter)[:16]
    high = inter_t.astype(BF16)
    low = (inter_t - high.astype(F32)).astype(BF16)
    coef_out[...] = dot(high, oha[...]) + dot(low, oha[...])
    coef_copies = [
        pltpu.make_async_remote_copy(
            src_ref=coef_out, dst_ref=coef_in.at[n], send_sem=cs.at[n], recv_sem=cr.at[n],
            device_id={"grid": peer(d)}, device_id_type=MESH,
        )
        for n, d in enumerate(OFFSETS)
    ]
    for copy in coef_copies:
        copy.start()
    for copy in coup_copies:
        copy.wait()
    coup = coup_in[0] + pltpu.roll(coup_out[...], 32, 1) + pltpu.roll(coup_in[1], 64, 1)
    for copy in coef_copies:
        copy.wait()
    lane16 = lax.broadcasted_iota(jnp.int32, (16, 128), 1)
    coef = coef_out[...] + pltpu.roll(coef_in[0], 96, 1) + pltpu.roll(coef_in[1], 32, 1)
    coef = coef + jnp.where(lane16 < 32, pltpu.roll(coef_in[2], 64, 1), 0.0)
    coef = coef + jnp.where(
        jnp.logical_and(lane16 >= 64, lane16 < 96), pltpu.roll(coef_in[3], 64, 1), 0.0
    )
    mixed_rows = []
    for b in range(2):
        for p in range(8):
            mixed_rows.append(
                jnp.sum(coup[8 * p : 8 * p + 8] * coef[8 * b : 8 * b + 8], axis=0, keepdims=True)
            )
    coupled = jnp.concatenate(mixed_rows, axis=0).astype(BF16)
    coupled = jnp.concatenate([coupled, jnp.zeros((112, 128), BF16)], axis=0)
    chosen = lax.dot_general(
        oha[...], coupled, (((1,), (1,)), ((), ())), preferred_element_type=F32
    ).astype(BF16)
    backs = []
    for b in range(2):
        back = None
        for p in range(8):
            n = (b * 8 + p) * 128
            term = projt[p] * dot(chosen, exp_up[:, n : n + 128])
            back = term if back is None else back + term
        backs.append(back)
    back = jnp.concatenate(backs, axis=1).astype(BF16)

    for c in range(9):
        spread = dot(oh2[c], back)
        local = potc[c]
        local = jnp.concatenate([local, local], axis=1)
        mx[c] = (local * rs[c].astype(F32) + spread).astype(BF16)
    lines = []
    for j in range(3):
        row = jnp.concatenate([tile(mx[3 * j + t], b) for b in range(2) for t in range(3)], axis=1)
        part = dot(row, wztv[...]).astype(BF16)
        back = dot(cxtv[...], part)
        for par in range(2):
            lines.append(
                jnp.concatenate(
                    [back[k * A : (k + 1) * A, par * N : (par + 1) * N] for k in range(T)], axis=1
                )
            )
    spare = [
        jnp.concatenate([tile(line, n) for line in lines] + [jnp.zeros((A, 128), F32)], axis=1)
        for n in (7, 8)
    ]
    lines = jnp.concatenate([line[None, :, :896] for line in lines] + [x[None] for x in spare], axis=0)
    send2[...] = jnp.swapaxes(lines, 0, 1).astype(BF16)

    slot = lax.rem(g, A)

    def forwarded2(i):
        return remote(
            send2.at[(i, *tail)], rel2.at[slot], s2b.at[i], rr2.at[slot], lax.rem(owner(i) + A, G)
        )

    def whole2(i):
        return remote(send2.at[i], out.at[g], s2.at[i], r2.at[g], owner(i))

    def part2(i):
        return remote(send2.at[(i, *head)], out.at[(g, *head)], s2.at[i], r2.at[g], owner(i))

    each(0, A, slot, lambda i: is_whole(owner(i)), lambda i: forwarded2(i).start())
    each(
        0, A, slot, lambda i: owner(i) == g,
        lambda i: either(is_whole(owner(i)), lambda: whole2(i).start(), lambda: part2(i).start()),
    )

    def pass2(k):
        src = my_row * A + k
        return remote(rel2.at[k], out.at[(src, *tail)], f2.at[k], r2b.at[src], partner)

    def relay2(k):
        remote(send2.at[(0, *tail)], rel2.at[k], s2b.at[0], rr2.at[k], partner).wait_recv()
        pass2(k).start()

    @pl.when(jnp.logical_not(active))
    def _():
        each(0, A, 0, lambda k: k == slot, relay2)
        each(0, A, 0, lambda k: k == slot, lambda k: pass2(k).wait_send())

    def wait2(src):
        def parts():
            remote(send2.at[(0, *head)], out.at[(src, *head)], s2.at[0], r2.at[src], src).wait_recv()
            remote(rel2.at[0], out.at[(src, *tail)], f2.at[0], r2b.at[src], partner).wait_recv()

        either(
            is_whole(src),
            lambda: remote(send2.at[0], out.at[src], s2.at[0], r2.at[src], src).wait_recv(),
            parts,
        )

    each(0, 8, 0, own_row, lambda k: pass1(k).wait_send())

    @pl.when(active)
    def _():
        own = pltpu.make_async_copy(send2.at[ai], out.at[g], self_sem)
        own.start()
        own.wait()
        each(0, G, 0, is_whole, lambda to: forwarded1(to).wait_send())
        each(
            0, G, 0, itself,
            lambda to: either(is_whole(to), lambda: whole1(to).wait_send(), lambda: part1(to).wait_send()),
        )
        each(0, G, 0, itself, wait2)

    each(0, A, 0, lambda i: is_whole(owner(i)), lambda i: forwarded2(i).wait_send())
    each(
        0, A, 0, lambda i: owner(i) == g,
        lambda i: either(
            is_whole(owner(i)), lambda: whole2(i).wait_send(), lambda: part2(i).wait_send()
        ),
    )


def last_kernel(cyt, recv, waves, out):
    g = lax.axis_index("grid")
    active = jnp.logical_or(g < 8, g >= 24)

    @pl.when(active)
    def _():
        got = recv[...].astype(F32)
        sub = lax.broadcasted_iota(jnp.int32, (G, 8, 128), 1)
        planes = [got]
        for row in (6, 7):
            spare = jnp.zeros((G, 8, 128), F32)
            for y in range(T):
                spare = jnp.where(sub == y, tile(got, y)[:, row : row + 1, :], spare)
            planes.append(spare)
        planes = jnp.concatenate(planes, axis=2).reshape(256, 1152).astype(BF16)
        fifth = dot(cyt[...], planes)
        for k in range(T):
            ksq = sphere_sq(g * T + k)
            inside = ksq < RAD2
            kinetic = ksq.astype(F32) / RAD2
            for b in range(2):
                n = (2 * k + b) * 96
                w = kept(waves[b, k, 0:48, :], waves[b, k, 144:192, :])
                total = jnp.where(inside, kinetic * w + fifth[:, n : n + 96], 0.0)
                wide = jnp.concatenate([total[:, :48], jnp.zeros((96, 96), F32), total[:, 48:]], axis=1)
                wide = wide.astype(BF16)
                out[b, k, 0:48, :] = wide[:48]
                out[b, k, 48:144, :] = jnp.zeros((96, N), BF16)
                out[b, k, 144:192, :] = wide[48:]

    @pl.when(jnp.logical_not(active))
    def _():
        out[...] = jnp.zeros(out.shape, BF16)


def shards(waves, potential, block_index, atom_of_slot, projectors, coupling):
    cy, cyt, cx, cxt, wz, wzt = (jnp.asarray(x) for x in tables())
    coup = jnp.transpose(coupling, (1, 2, 0)).reshape(64, 32)
    hbm = pl.BlockSpec(memory_space=pltpu.HBM)
    vmem = pl.BlockSpec(memory_space=pltpu.VMEM)
    dma = pltpu.SemaphoreType.DMA
    recv = pl.pallas_call(
        main_kernel,
        name="exchange_and_apply",
        out_shape=jax.ShapeDtypeStruct((G, 8, 896), BF16),
        in_specs=[hbm] * 11,
        out_specs=hbm,
        scratch_shapes=[
            pltpu.VMEM((2, T, 48, N), BF16),
            pltpu.VMEM((2, T, 48, N), BF16),
            pltpu.VMEM((256, 96), BF16),
            pltpu.VMEM((N, 96), BF16),
            pltpu.VMEM((96, N), BF16),
            pltpu.VMEM((384, 768), BF16),
            pltpu.VMEM((768, 384), BF16),
            pltpu.VMEM((T, N, N), BF16),
            pltpu.VMEM((1, 512), jnp.int32),
            pltpu.VMEM((1, 512), jnp.int32),
            pltpu.VMEM((512, 8, 128), BF16),
            pltpu.VMEM((64, 32), F32),
            pltpu.VMEM((8, 512, 128), F32),
            pltpu.VMEM((9, N, 128), F32),
            pltpu.VMEM((9, 512, N), BF16),
            pltpu.VMEM((9, N, 512), BF16),
            pltpu.VMEM((512, 128), BF16),
            pltpu.VMEM((128, 2048), BF16),
            pltpu.VMEM((G, 8, 896), BF16),
            pltpu.VMEM((A, 8, 896), BF16),
            pltpu.VMEM((8, 8, 896 - DIRECT), BF16),
            pltpu.VMEM((9, N, 256), BF16),
            pltpu.VMEM((9, N, 256), BF16),
            pltpu.VMEM((A, 8, 896), BF16),
            pltpu.VMEM((A, 8, 896 - DIRECT), BF16),
            pltpu.VMEM((64, 128), F32),
            pltpu.VMEM((2, 64, 128), F32),
            pltpu.VMEM((16, 128), F32),
            pltpu.VMEM((4, 16, 128), F32),
            dma((12,)),
            dma((G,)),
            dma((G,)),
            dma((A,)),
            dma((A,)),
            dma((8,)),
            dma((8,)),
            dma((A,)),
            dma((A,)),
            dma((G,)),
            dma((G,)),
            dma((A,)),
            dma((A,)),
            dma,
            dma((4,)),
            dma((4,)),
            dma((2,)),
            dma((2,)),
        ],
        compiler_params=pltpu.CompilerParams(
            collective_id=0, has_side_effects=True, vmem_limit_bytes=60 << 20
        ),
    )(
        waves, jnp.transpose(potential, (1, 0, 2)), block_index.reshape(1, -1), atom_of_slot.reshape(1, -1),
        projectors, coup, cy, cx, cxt, wz, wzt,
    )
    return pl.pallas_call(
        last_kernel,
        name="finish",
        out_shape=jax.ShapeDtypeStruct(waves.shape, BF16),
        in_specs=[vmem] * 3,
        out_specs=vmem,
        compiler_params=pltpu.CompilerParams(vmem_limit_bytes=60 << 20),
    )(cyt, recv, waves)


def solution(mesh):
    in_specs = (
        P("band", "grid", None, None),
        P(None, "grid", None),
        P("grid"),
        P("grid"),
        P("grid", None, None),
        P("grid", None, None),
    )
    out_specs = P("band", "grid", None, None)
    return jax.shard_map(shards, mesh=mesh, in_specs=in_specs, out_specs=out_specs, check_vma=False)
```

```python
import functools
import math

import jax
import jax.numpy as jnp
import ml_dtypes
import numpy as np
from jax import lax
from jax.experimental import pallas as pl
from jax.experimental.pallas import tpu as pltpu
from jax.sharding import PartitionSpec as P

MESH = pl.DeviceIdType.MESH
F32, BF16 = jnp.float32, jnp.bfloat16
N, G, T = 192, 32, 6
A = 16
RAD2 = 48 * 48
KEEP = np.concatenate([np.arange(48), np.arange(144, 192)])
OFFSETS = (1, -1, 2, -2)
FIRST = ((0, 4, 0), (4, 3, 5))
SECOND = ((0, 3, 0), (3, 4, 4))


def tables():
    k = np.arange(N)
    angles = np.float32(2.0 * math.pi / N) * ((k[:, None] * k[None, :]) % N).astype(np.float32)
    c = ((np.cos(angles) + np.sin(angles)) / np.float32(math.sqrt(N))).astype(ml_dtypes.bfloat16)
    c = c.astype(np.float32)
    cy = np.zeros((G, 8, 96), np.float32)
    cy[:, :T] = c[:, KEEP].reshape(G, T, 96)
    cy = cy.reshape(256, 96)
    cx = c[:, KEEP].reshape(N, A, T).transpose(0, 2, 1).reshape(N, 96)
    wz = np.zeros((2, 96, 2, N), np.float32)
    for par in range(2):
        wz[par, :, par, :] = c[KEEP]
    wz = wz.reshape(192, 384)
    out = [cy, cy.T, cx, cx.T, wz, wz.T]
    return [np.ascontiguousarray(x).astype(ml_dtypes.bfloat16) for x in out]


def dot(a, b):
    return jnp.dot(a, b, preferred_element_type=F32)


def folded_sq(k):
    f = jnp.minimum(k, N - k)
    return f * f


def sphere_sq(kx):
    row = lax.broadcasted_iota(jnp.int32, (96, 96), 0)
    lane = lax.broadcasted_iota(jnp.int32, (96, 96), 1)
    ky = jnp.where(row < 48, row, row + 96)
    kz = jnp.where(lane < 48, lane, lane + 96)
    return folded_sq(kx) + folded_sq(ky) + folded_sq(kz)


def kept(low, high):
    w = jnp.concatenate([low, high], axis=0).astype(F32)
    return jnp.concatenate([w[:, :48], w[:, 144:]], axis=1)


def tile(x, n):
    return x[..., n * 128 : (n + 1) * 128]


def main_kernel(
    waves, pot, idx, atom, proj, coup, cy, cx, cxt, wz, wzt, out,
    wlo, whi, cyv, cxv, cxtv, wzv, wztv, potv, idxv, atomv, projv, coupv,
    projt, potc, oh1, oh2, oha, exp_up,
    send1, recv1, rs, send2, coup_out, coup_in, coef_out, coef_in,
    load_sem, s1, r1, s2, r2, self_sem, cs, cr, ks, kr,
):
    g = lax.axis_index("grid")
    active = jnp.logical_or(g < 8, g >= 24)
    ai = jnp.where(g < 8, g, g - 16)

    def peer(d):
        return lax.rem(g + d + G, G)

    wave_loads = [
        pltpu.make_async_copy(waves.at[:, :, 0:48, :], wlo, load_sem.at[0]),
        pltpu.make_async_copy(waves.at[:, :, 144:192, :], whi, load_sem.at[1]),
        pltpu.make_async_copy(cy, cyv, load_sem.at[2]),
    ]
    pairs = (
        (coup, coupv), (idx, idxv), (atom, atomv), (proj, projv), (pot, potv),
        (cx, cxv), (wz, wzv), (wzt, wztv), (cxt, cxtv),
    )
    loads = [pltpu.make_async_copy(a, b, load_sem.at[3 + n]) for n, (a, b) in enumerate(pairs)]

    @pl.when(active)
    def _():
        for copy in wave_loads:
            copy.start()

    for copy in loads:
        copy.start()

    barrier = pltpu.get_barrier_semaphore()

    for d in range(1, G):
        pl.semaphore_signal(barrier, inc=1, device_id={"grid": peer(d)}, device_id_type=MESH)

    @pl.when(active)
    def _():
        for copy in wave_loads:
            copy.wait()
        parts = []
        for b in range(2):
            for k in range(T):
                inside = sphere_sq(g * T + k) < RAD2
                parts.append(jnp.where(inside, kept(wlo[b, k], whi[b, k]), 0.0))
        rhs = jnp.concatenate(parts, axis=1).astype(BF16)
        sub = lax.broadcasted_iota(jnp.int32, (G, 8, 128), 1)
        for wire, count, begin in FIRST:
            spare = dot(cyv[...], tile(rhs, begin + count)).reshape(G, 8, 128)
            for t in range(count):
                plane = dot(cyv[...], tile(rhs, begin + t)).reshape(G, 8, 128)
                for row, y in ((6, t), (7, t + count)):
                    if y < T:
                        plane = jnp.where(sub == row, spare[:, y : y + 1, :], plane)
                send1[:, :, (wire + t) * 128 : (wire + t + 1) * 128] = plane.astype(BF16)

    pl.semaphore_wait(barrier, G - 1)

    my_row, place = g // A, lax.rem(g, A)
    partner = lax.rem(g + A, G)

    def half(ref, i, plan, h):
        return ref.at[i, :, pl.ds(plan[h][0] * 128, plan[h][1] * 128)]

    def remote(src, dst, send, recv, to):
        return pltpu.make_async_remote_copy(
            src_ref=src, dst_ref=dst, send_sem=send, recv_sem=recv,
            device_id={"grid": to}, device_id_type=MESH,
        )

    def whole(ref, count, plan, h, send, recv):
        chunks = half(ref, pl.ds(0, count), plan, h)
        return remote(chunks, chunks, send.at[h], recv.at[h], partner)

    def first_copy(row, n, h):
        to = row * A + lax.rem(place + n, A)
        remote(
            half(send1, to, FIRST, h), half(recv1, ai, FIRST, h), s1.at[h], r1.at[h], to
        ).start()

    @pl.when(active)
    def _():
        for h in range(2):

            def across(n, carry):
                first_copy(1 - my_row, n, h)
                return carry

            def along(n, carry):
                first_copy(my_row, n, h)
                return carry

            lax.fori_loop(0, A, across, 0)
            lax.fori_loop(1, A, along, 0)
        recv1[ai] = send1[g]

    for copy in loads:
        copy.wait()
    coup_out[...] = jnp.concatenate([coupv[...], jnp.zeros((64, 96), F32)], axis=1)
    coup_copies = [
        pltpu.make_async_remote_copy(
            src_ref=coup_out, dst_ref=coup_in.at[n], send_sem=ks.at[n], recv_sem=kr.at[n],
            device_id={"grid": peer(d)}, device_id_type=MESH,
        )
        for n, d in enumerate(OFFSETS[:2])
    ]
    for copy in coup_copies:
        copy.start()

    idx_row = idxv[...]
    atom_row = atomv[...]
    atom_row = ((lax.shift_right_logical(atom_row, 5) - g + 33) & 31) * 32 + (atom_row & 31)

    def column(row):
        return jnp.transpose(jnp.broadcast_to(row.astype(F32), (128, 512))).astype(jnp.int32)

    idx_col = column(idx_row)
    idx_col = jnp.concatenate([idx_col, idx_col[:, :64]], axis=1)
    lane192 = lax.broadcasted_iota(jnp.int32, (512, N), 1) * 9
    row192 = lax.broadcasted_iota(jnp.int32, (N, 512), 0) * 9
    for c in range(9):
        oh1[c] = jnp.where(lane192 + c == idx_col, 1.0, 0.0).astype(BF16)
        oh2[c] = jnp.where(row192 + c == idx_row, 1.0, 0.0).astype(BF16)
    lane128 = lax.broadcasted_iota(jnp.int32, (512, 128), 1)
    oha[...] = jnp.where(column(atom_row) == lane128, 1.0, 0.0).astype(BF16)
    up_row = lax.broadcasted_iota(jnp.int32, (128, 1024), 0)
    up_lane = lax.broadcasted_iota(jnp.int32, (128, 1024), 1)
    exp_up[...] = jnp.where(lax.shift_right_logical(up_lane, 7) == up_row, 1.0, 0.0).astype(BF16)
    projt[...] = jnp.swapaxes(projv[...].astype(F32), 0, 1)
    pt = potv[...].astype(F32)
    for j in range(3):
        e, o = pt[2 * j], pt[2 * j + 1]
        potc[3 * j] = e[:, :128]
        potc[3 * j + 1] = jnp.concatenate([e[:, 128:], o[:, :64]], axis=1)
        potc[3 * j + 2] = o[:, 64:]

    def wait_first(h):
        @pl.when(active)
        def _():
            whole(recv1, A - 1, FIRST, h, s1, r1).wait_recv()

        @pl.when(jnp.logical_not(active))
        def _():
            whole(recv1, A, FIRST, h, s1, r1).wait_recv()

    def arrived(h):
        wire, count, _ = FIRST[h]
        return jnp.swapaxes(recv1[:, :, wire * 128 : (wire + count) * 128].astype(F32), 0, 1)

    def folded(got, y, count):
        return tile(got[6 + y // count], y % count)

    def coef_copies(b):
        return [
            pltpu.make_async_remote_copy(
                src_ref=coef_out.at[b], dst_ref=coef_in.at[b, n], send_sem=cs.at[b, n], recv_sem=cr.at[b, n],
                device_id={"grid": peer(d)}, device_id_type=MESH,
            )
            for n, d in enumerate(OFFSETS)
        ]

    def project(b, lines):
        stacks = [
            jnp.concatenate([line[:, k * 96 : (k + 1) * 96] for k in range(T)], axis=0) for line in lines
        ]
        for j in range(3):
            rhs = jnp.concatenate([stacks[2 * j], stacks[2 * j + 1]], axis=1).astype(BF16)
            part = dot(cxv[...], rhs).astype(BF16)
            real = dot(part, wzv[...]).astype(BF16)
            for t in range(3):
                rs[b, 3 * j + t] = tile(real, t)
        rows = dot(oh1[0], rs[b, 0])
        for c in range(1, 9):
            rows = rows + dot(oh1[c], rs[b, c])
        prod = jnp.concatenate([(projt[p] * rows).astype(BF16) for p in range(8)], axis=1)
        inter = lax.dot_general(
            prod, exp_up[...], (((1,), (1,)), ((), ())), preferred_element_type=F32
        )
        inter = jnp.transpose(inter)[:16]
        high = inter.astype(BF16)
        low = (inter - high.astype(F32)).astype(BF16)
        coef_out[b] = (dot(high, oha[...]) + dot(low, oha[...]))[:8]
        for copy in coef_copies(b):
            copy.start()

    def apply(b, coup):
        for copy in coef_copies(b):
            copy.wait()
        lane = lax.broadcasted_iota(jnp.int32, (8, 128), 1)
        coef = coef_out[b] + pltpu.roll(coef_in[b, 0], 96, 1) + pltpu.roll(coef_in[b, 1], 32, 1)
        coef = coef + jnp.where(lane < 32, pltpu.roll(coef_in[b, 2], 64, 1), 0.0)
        coef = coef + jnp.where(
            jnp.logical_and(lane >= 64, lane < 96), pltpu.roll(coef_in[b, 3], 64, 1), 0.0
        )
        coupled = [jnp.sum(coup[8 * p : 8 * p + 8] * coef, axis=0, keepdims=True) for p in range(8)]
        coupled = jnp.concatenate(coupled + [jnp.zeros((120, 128), F32)], axis=0).astype(BF16)
        chosen = lax.dot_general(
            oha[...], coupled, (((1,), (1,)), ((), ())), preferred_element_type=F32
        ).astype(BF16)
        back = projt[0] * dot(chosen, tile(exp_up[...], 0))
        for p in range(1, 8):
            back = back + projt[p] * dot(chosen, tile(exp_up[...], p))
        back = back.astype(BF16)
        lines = []
        for j in range(3):
            row = []
            for c in range(3 * j, 3 * j + 3):
                row.append((potc[c] * rs[b, c].astype(F32) + dot(oh2[c], back)).astype(BF16))
            part = dot(jnp.concatenate(row, axis=1), wztv[...]).astype(BF16)
            part = dot(cxtv[...], part)
            for par in range(2):
                lines.append(
                    jnp.concatenate(
                        [part[k * A : (k + 1) * A, par * 96 : (par + 1) * 96] for k in range(T)], axis=1
                    )
                )
        return lines

    def send_back(lines, h):
        wire, count, _ = SECOND[h]
        rows = [line[:, : count * 128] for line in lines]
        for first in (0, count):
            spare = [
                lines[y][:, count * 128 :] if y < T else jnp.zeros((A, 128), F32)
                for y in range(first, first + count)
            ]
            rows.append(jnp.concatenate(spare, axis=1))
        rows = jnp.concatenate([row[None] for row in rows], axis=0)
        send2[:, :, wire * 128 : (wire + count) * 128] = jnp.swapaxes(rows, 0, 1).astype(BF16)

        def go(n, carry):
            i = lax.rem(n + place, A)
            to = jnp.where(i < 8, i, i + A)

            @pl.when(to != g)
            def _():
                remote(
                    half(send2, i, SECOND, h), half(out, g, SECOND, h), s2.at[h], r2.at[h], to
                ).start()

            return carry

        lax.fori_loop(0, A, go, 0)

    wait_first(0)
    got = arrived(0)
    tails = [folded(got, y, 4) for y in range(T)]
    project(0, [jnp.concatenate([got[y], tails[y][:, :64]], axis=1) for y in range(T)])
    wait_first(1)
    got = arrived(1)
    project(1, [jnp.concatenate([tails[y][:, 64:], got[y], folded(got, y, 3)], axis=1) for y in range(T)])
    for copy in coup_copies:
        copy.wait()
    coup = coup_in[0] + pltpu.roll(coup_out[...], 32, 1) + pltpu.roll(coup_in[1], 64, 1)
    lines0 = apply(0, coup)
    send_back([line[:, :512] for line in lines0], 0)
    lines1 = apply(1, coup)
    send_back([jnp.concatenate([a[:, 512:], b], axis=1) for a, b in zip(lines0, lines1)], 1)

    @pl.when(active)
    def _():
        own = pltpu.make_async_copy(send2.at[ai], out.at[g], self_sem)
        own.start()
        for h in range(2):
            whole(send1, G - 1, FIRST, h, s1, r1).wait_send()
            whole(send2, A - 1, SECOND, h, s2, r2).wait_send()
        own.wait()
        for h in range(2):
            whole(out, G - 1, SECOND, h, s2, r2).wait_recv()

    @pl.when(jnp.logical_not(active))
    def _():
        for h in range(2):
            whole(send2, A, SECOND, h, s2, r2).wait_send()


def last_kernel(cyt, recv, waves, out, cyv, got_ref, wlo, whi, zero, low, high, load_sem, store_sem):
    g = lax.axis_index("grid")
    active = jnp.logical_or(g < 8, g >= 24)

    @pl.when(active)
    def _():
        loads = [
            pltpu.make_async_copy(a, b, load_sem.at[n])
            for n, (a, b) in enumerate(
                (
                    (recv, got_ref), (cyt, cyv),
                    (waves.at[:, :, 0:48, :], wlo), (waves.at[:, :, 144:192, :], whi),
                )
            )
        ]
        for copy in loads:
            copy.start()
        zero[...] = jnp.zeros(zero.shape, BF16)
        stores = [pltpu.make_async_copy(zero, out.at[:, :, 48:144, :], store_sem.at[0])]
        stores[0].start()
        for copy in loads:
            copy.wait()
        got = got_ref[...].astype(F32)
        sub = lax.broadcasted_iota(jnp.int32, (G, 8, 128), 1)
        planes = []
        for wire, count, _ in SECOND:
            planes += [tile(got, wire + t) for t in range(count)]
            spare = jnp.zeros((G, 8, 128), F32)
            for y in range(T):
                row = 6 + y // count
                spare = jnp.where(sub == y, tile(got, wire + y % count)[:, row : row + 1, :], spare)
            planes.append(spare)
        planes = jnp.concatenate(planes, axis=2).reshape(256, 1152).astype(BF16)
        fifth = dot(cyv[...], planes)
        for b in range(2):
            for k in range(T):
                ksq = sphere_sq(g * T + k)
                n = (b * T + k) * 96
                total = ksq.astype(F32) / RAD2 * kept(wlo[b, k], whi[b, k]) + fifth[:, n : n + 96]
                total = jnp.where(ksq < RAD2, total, 0.0)
                total = jnp.concatenate([total[:, :48], jnp.zeros((96, 96), F32), total[:, 48:]], axis=1)
                total = total.astype(BF16)
                low[b, k] = total[:48]
                high[b, k] = total[48:]
            stores += [
                pltpu.make_async_copy(low.at[b], out.at[b, :, 0:48, :], store_sem.at[1 + 2 * b]),
                pltpu.make_async_copy(high.at[b], out.at[b, :, 144:192, :], store_sem.at[2 + 2 * b]),
            ]
            stores[-2].start()
            stores[-1].start()
        for copy in stores:
            copy.wait()

    @pl.when(jnp.logical_not(active))
    def _():
        zero[...] = jnp.zeros(zero.shape, BF16)
        stores = [
            pltpu.make_async_copy(zero, out.at[:, :, n * 96 : (n + 1) * 96, :], store_sem.at[n])
            for n in range(2)
        ]
        for copy in stores:
            copy.start()
        for copy in stores:
            copy.wait()


def shards(waves, potential, block_index, atom_of_slot, projectors, coupling):
    cy, cyt, cx, cxt, wz, wzt = (jnp.asarray(x) for x in tables())
    coup = jnp.transpose(coupling, (1, 2, 0)).reshape(64, 32)
    hbm = pl.BlockSpec(memory_space=pltpu.HBM)
    dma = pltpu.SemaphoreType.DMA
    recv = pl.pallas_call(
        main_kernel,
        name="exchange_and_apply",
        out_shape=jax.ShapeDtypeStruct((G, 8, 896), BF16),
        in_specs=[hbm] * 11,
        out_specs=hbm,
        scratch_shapes=[
            pltpu.VMEM((2, T, 48, N), BF16),
            pltpu.VMEM((2, T, 48, N), BF16),
            pltpu.VMEM((256, 96), BF16),
            pltpu.VMEM((N, 96), BF16),
            pltpu.VMEM((96, N), BF16),
            pltpu.VMEM((192, 384), BF16),
            pltpu.VMEM((384, 192), BF16),
            pltpu.VMEM((T, N, N), BF16),
            pltpu.VMEM((1, 512), jnp.int32),
            pltpu.VMEM((1, 512), jnp.int32),
            pltpu.VMEM((512, 8, 128), BF16),
            pltpu.VMEM((64, 32), F32),
            pltpu.VMEM((8, 512, 128), F32),
            pltpu.VMEM((9, N, 128), F32),
            pltpu.VMEM((9, 512, N), BF16),
            pltpu.VMEM((9, N, 512), BF16),
            pltpu.VMEM((512, 128), BF16),
            pltpu.VMEM((128, 1024), BF16),
            pltpu.VMEM((G, 8, 896), BF16),
            pltpu.VMEM((A, 8, 896), BF16),
            pltpu.VMEM((2, 9, N, 128), BF16),
            pltpu.VMEM((A, 8, 896), BF16),
            pltpu.VMEM((64, 128), F32),
            pltpu.VMEM((2, 64, 128), F32),
            pltpu.VMEM((2, 8, 128), F32),
            pltpu.VMEM((2, 4, 8, 128), F32),
            dma((12,)),
            dma((2,)),
            dma((2,)),
            dma((2,)),
            dma((2,)),
            dma,
            dma((2, 4)),
            dma((2, 4)),
            dma((2,)),
            dma((2,)),
        ],
        compiler_params=pltpu.CompilerParams(
            collective_id=0, has_side_effects=True, vmem_limit_bytes=60 << 20
        ),
    )(
        waves, jnp.transpose(potential, (1, 0, 2)), block_index.reshape(1, -1), atom_of_slot.reshape(1, -1),
        projectors, coup, cy, cx, cxt, wz, wzt,
    )
    return pl.pallas_call(
        last_kernel,
        name="finish",
        out_shape=jax.ShapeDtypeStruct(waves.shape, BF16),
        in_specs=[hbm] * 3,
        out_specs=hbm,
        scratch_shapes=[
            pltpu.VMEM((96, 256), BF16),
            pltpu.VMEM((G, 8, 896), BF16),
            pltpu.VMEM((2, T, 48, N), BF16),
            pltpu.VMEM((2, T, 48, N), BF16),
            pltpu.VMEM((2, T, 96, N), BF16),
            pltpu.VMEM((2, T, 48, N), BF16),
            pltpu.VMEM((2, T, 48, N), BF16),
            dma((4,)),
            dma((5,)),
        ],
        compiler_params=pltpu.CompilerParams(vmem_limit_bytes=60 << 20),
    )(cyt, recv, waves)


def solution(mesh):
    in_specs = (
        P("band", "grid", None, None),
        P(None, "grid", None),
        P("grid"),
        P("grid"),
        P("grid", None, None),
        P("grid", None, None),
    )
    out_specs = P("band", "grid", None, None)
    return jax.shard_map(shards, mesh=mesh, in_specs=in_specs, out_specs=out_specs, check_vma=False)
```

```python
import functools
import math

import jax
import jax.numpy as jnp
import ml_dtypes
import numpy as np
from jax import lax
from jax.experimental import pallas as pl
from jax.experimental.pallas import tpu as pltpu
from jax.sharding import PartitionSpec as P

MESH = pl.DeviceIdType.MESH
F32, BF16 = jnp.float32, jnp.bfloat16
N, G, T = 192, 32, 6
A = 16
RAD2 = 48 * 48
KEEP = np.concatenate([np.arange(48), np.arange(144, 192)])
OFFSETS = (1, -1, 2, -2)
FIRST = ((0, 4, 0), (4, 3, 5))
SECOND = ((0, 3, 0), (3, 4, 4))


def tables():
    k = np.arange(N)
    angles = np.float32(2.0 * math.pi / N) * ((k[:, None] * k[None, :]) % N).astype(np.float32)
    c = ((np.cos(angles) + np.sin(angles)) / np.float32(math.sqrt(N))).astype(ml_dtypes.bfloat16)
    c = c.astype(np.float32)
    cy = np.zeros((G, 8, 96), np.float32)
    cy[:, :T] = c[:, KEEP].reshape(G, T, 96)
    cy = cy.reshape(256, 96)
    cx = c[:, KEEP].reshape(N, A, T).transpose(0, 2, 1).reshape(N, 96)
    wz = np.zeros((2, 96, 2, N), np.float32)
    for par in range(2):
        wz[par, :, par, :] = c[KEEP]
    wz = wz.reshape(192, 384)
    out = [cy, cy.T, cx, cx.T, wz, wz.T]
    return [np.ascontiguousarray(x).astype(ml_dtypes.bfloat16) for x in out]


def dot(a, b):
    return jnp.dot(a, b, preferred_element_type=F32)


def folded_sq(k):
    f = jnp.minimum(k, N - k)
    return f * f


def sphere_sq(kx):
    row = lax.broadcasted_iota(jnp.int32, (96, 96), 0)
    lane = lax.broadcasted_iota(jnp.int32, (96, 96), 1)
    ky = jnp.where(row < 48, row, row + 96)
    kz = jnp.where(lane < 48, lane, lane + 96)
    return folded_sq(kx) + folded_sq(ky) + folded_sq(kz)


def kept(low, high):
    w = jnp.concatenate([low, high], axis=0).astype(F32)
    return jnp.concatenate([w[:, :48], w[:, 144:]], axis=1)


def tile(x, n):
    return x[..., n * 128 : (n + 1) * 128]


def main_kernel(
    waves, pot, idx, atom, proj, coup, cy, cx, cxt, wz, wzt, out,
    wlo, whi, cyv, cxv, cxtv, wzv, wztv, potv, idxv, atomv, projv, coupv,
    projt, potc, oh1, oh2, oha, exp_up,
    send1, recv1, rs, send2, coup_out, coup_in, coef_out, coef_in,
    load_sem, s1, r1, s2, r2, self_sem, cs, cr, ks, kr,
):
    g = lax.axis_index("grid")
    active = jnp.logical_or(g < 8, g >= 24)
    ai = jnp.where(g < 8, g, g - 16)

    def peer(d):
        return lax.rem(g + d + G, G)

    wave_loads = [
        pltpu.make_async_copy(waves.at[:, :, 0:48, :], wlo, load_sem.at[0]),
        pltpu.make_async_copy(waves.at[:, :, 144:192, :], whi, load_sem.at[1]),
        pltpu.make_async_copy(cy, cyv, load_sem.at[2]),
    ]
    pairs = (
        (coup, coupv), (idx, idxv), (atom, atomv), (proj, projv), (pot, potv),
        (cx, cxv), (wz, wzv), (wzt, wztv), (cxt, cxtv),
    )
    loads = [pltpu.make_async_copy(a, b, load_sem.at[3 + n]) for n, (a, b) in enumerate(pairs)]

    @pl.when(active)
    def _():
        for copy in wave_loads:
            copy.start()

    for copy in loads:
        copy.start()

    barrier = pltpu.get_barrier_semaphore()

    for d in range(1, G):
        pl.semaphore_signal(barrier, inc=1, device_id={"grid": peer(d)}, device_id_type=MESH)

    def transform(h):
        parts = []
        wire, count, begin = FIRST[h]
        first, last = begin * 128 // 96, (begin + count + 1) * 128
        for n in range(first, -(-last // 96)):
            b, k = n // T, n % T
            inside = sphere_sq(g * T + k) < RAD2
            parts.append(jnp.where(inside, kept(wlo[b, k], whi[b, k]), 0.0))
        rhs = jnp.concatenate(parts, axis=1)
        skip = begin * 128 - first * 96
        rhs = rhs[:, skip : skip + (count + 1) * 128].astype(BF16)
        sub = lax.broadcasted_iota(jnp.int32, (G, 8, 128), 1)
        spare = dot(cyv[...], tile(rhs, count)).reshape(G, 8, 128)
        for t in range(count):
            plane = dot(cyv[...], tile(rhs, t)).reshape(G, 8, 128)
            for row, y in ((6, t), (7, t + count)):
                if y < T:
                    plane = jnp.where(sub == row, spare[:, y : y + 1, :], plane)
            send1[:, :, (wire + t) * 128 : (wire + t + 1) * 128] = plane.astype(BF16)

    @pl.when(active)
    def _():
        for copy in wave_loads:
            copy.wait()
        transform(0)

    pl.semaphore_wait(barrier, G - 1)

    my_row, place = g // A, lax.rem(g, A)
    partner = lax.rem(g + A, G)

    def half(ref, i, plan, h):
        return ref.at[i, :, pl.ds(plan[h][0] * 128, plan[h][1] * 128)]

    def remote(src, dst, send, recv, to):
        return pltpu.make_async_remote_copy(
            src_ref=src, dst_ref=dst, send_sem=send, recv_sem=recv,
            device_id={"grid": to}, device_id_type=MESH,
        )

    def whole(ref, count, plan, h, send, recv):
        chunks = half(ref, pl.ds(0, count), plan, h)
        return remote(chunks, chunks, send.at[h], recv.at[h], partner)

    def first_copy(row, n, h):
        to = row * A + lax.rem(place + n, A)
        remote(
            half(send1, to, FIRST, h), half(recv1, ai, FIRST, h), s1.at[h], r1.at[h], to
        ).start()

    @pl.when(active)
    def _():
        for h in range(2):
            if h == 1:
                transform(1)

            def across(n, carry):
                first_copy(1 - my_row, n, h)
                return carry

            def along(n, carry):
                first_copy(my_row, n, h)
                return carry

            lax.fori_loop(0, A, across, 0)
            lax.fori_loop(1, A, along, 0)
        recv1[ai] = send1[g]

    for copy in loads:
        copy.wait()
    coup_out[...] = jnp.concatenate([coupv[...], jnp.zeros((64, 96), F32)], axis=1)
    coup_copies = [
        pltpu.make_async_remote_copy(
            src_ref=coup_out, dst_ref=coup_in.at[n], send_sem=ks.at[n], recv_sem=kr.at[n],
            device_id={"grid": peer(d)}, device_id_type=MESH,
        )
        for n, d in enumerate(OFFSETS[:2])
    ]
    for copy in coup_copies:
        copy.start()

    idx_row = idxv[...]
    atom_row = atomv[...]
    atom_row = ((lax.shift_right_logical(atom_row, 5) - g + 33) & 31) * 32 + (atom_row & 31)

    def column(row):
        return jnp.transpose(jnp.broadcast_to(row.astype(F32), (128, 512))).astype(jnp.int32)

    idx_col = column(idx_row)[:, :1]
    lane = lax.broadcasted_iota(jnp.int32, (1, 9 * N), 1)
    ninth = lax.shift_right_logical(lane * 43691, 23)
    oh1[...] = jnp.where((lane - ninth * N) * 9 + ninth == idx_col, 1.0, 0.0).astype(BF16)
    row192 = lax.broadcasted_iota(jnp.int32, (N, 512), 0) * 9
    for c in range(9):
        oh2[c * N : (c + 1) * N] = jnp.where(row192 + c == idx_row, 1.0, 0.0).astype(BF16)
    lane128 = lax.broadcasted_iota(jnp.int32, (512, 128), 1)
    oha[...] = jnp.where(column(atom_row) == lane128, 1.0, 0.0).astype(BF16)
    up_row = lax.broadcasted_iota(jnp.int32, (128, 1024), 0)
    up_lane = lax.broadcasted_iota(jnp.int32, (128, 1024), 1)
    exp_up[...] = jnp.where(lax.shift_right_logical(up_lane, 7) == up_row, 1.0, 0.0).astype(BF16)
    projt[...] = jnp.swapaxes(projv[...].astype(F32), 0, 1)
    pt = potv[...].astype(F32)
    for j in range(3):
        e, o = pt[2 * j], pt[2 * j + 1]
        potc[3 * j] = e[:, :128]
        potc[3 * j + 1] = jnp.concatenate([e[:, 128:], o[:, :64]], axis=1)
        potc[3 * j + 2] = o[:, 64:]

    def wait_first(h):
        @pl.when(active)
        def _():
            whole(recv1, A - 1, FIRST, h, s1, r1).wait_recv()

        @pl.when(jnp.logical_not(active))
        def _():
            whole(recv1, A, FIRST, h, s1, r1).wait_recv()

    def arrived(h):
        wire, count, _ = FIRST[h]
        return jnp.swapaxes(recv1[:, :, wire * 128 : (wire + count) * 128].astype(F32), 0, 1)

    def folded(got, y, count):
        return tile(got[6 + y // count], y % count)

    def coef_copies(b):
        return [
            pltpu.make_async_remote_copy(
                src_ref=coef_out.at[b], dst_ref=coef_in.at[b, n], send_sem=cs.at[b, n], recv_sem=cr.at[b, n],
                device_id={"grid": peer(d)}, device_id_type=MESH,
            )
            for n, d in enumerate(OFFSETS)
        ]

    def project(b, lines):
        stacks = [
            jnp.concatenate([line[:, k * 96 : (k + 1) * 96] for k in range(T)], axis=0) for line in lines
        ]
        for j in range(3):
            rhs = jnp.concatenate([stacks[2 * j], stacks[2 * j + 1]], axis=1).astype(BF16)
            part = dot(cxv[...], rhs).astype(BF16)
            real = dot(part, wzv[...]).astype(BF16)
            for t in range(3):
                c = 3 * j + t
                rs[b, c * N : (c + 1) * N] = tile(real, t)
        rows = dot(oh1[...], rs[b])
        prod = jnp.concatenate([(projt[p] * rows).astype(BF16) for p in range(8)], axis=1)
        inter = lax.dot_general(
            prod, exp_up[...], (((1,), (1,)), ((), ())), preferred_element_type=F32
        )
        inter = jnp.transpose(inter)[:16]
        high = inter.astype(BF16)
        low = (inter - high.astype(F32)).astype(BF16)
        coef_out[b] = (dot(high, oha[...]) + dot(low, oha[...]))[:8]
        for copy in coef_copies(b):
            copy.start()

    def apply(b, coup):
        for copy in coef_copies(b):
            copy.wait()
        lane = lax.broadcasted_iota(jnp.int32, (8, 128), 1)
        coef = coef_out[b] + pltpu.roll(coef_in[b, 0], 96, 1) + pltpu.roll(coef_in[b, 1], 32, 1)
        coef = coef + jnp.where(lane < 32, pltpu.roll(coef_in[b, 2], 64, 1), 0.0)
        coef = coef + jnp.where(
            jnp.logical_and(lane >= 64, lane < 96), pltpu.roll(coef_in[b, 3], 64, 1), 0.0
        )
        coupled = [jnp.sum(coup[8 * p : 8 * p + 8] * coef, axis=0, keepdims=True) for p in range(8)]
        coupled = jnp.concatenate(coupled + [jnp.zeros((120, 128), F32)], axis=0).astype(BF16)
        chosen = lax.dot_general(
            oha[...], coupled, (((1,), (1,)), ((), ())), preferred_element_type=F32
        ).astype(BF16)
        back = projt[0] * dot(chosen, tile(exp_up[...], 0))
        for p in range(1, 8):
            back = back + projt[p] * dot(chosen, tile(exp_up[...], p))
        back = back.astype(BF16)
        spread = dot(oh2[...], back)
        lines = []
        for j in range(3):
            row = []
            for c in range(3 * j, 3 * j + 3):
                cut = slice(c * N, (c + 1) * N)
                row.append((potc[c] * rs[b, cut].astype(F32) + spread[cut]).astype(BF16))
            part = dot(jnp.concatenate(row, axis=1), wztv[...]).astype(BF16)
            part = dot(cxtv[...], part)
            for par in range(2):
                lines.append(
                    jnp.concatenate(
                        [part[k * A : (k + 1) * A, par * 96 : (par + 1) * 96] for k in range(T)], axis=1
                    )
                )
        return lines

    def send_back(lines, h):
        wire, count, _ = SECOND[h]
        rows = [line[:, : count * 128] for line in lines]
        for first in (0, count):
            spare = [
                lines[y][:, count * 128 :] if y < T else jnp.zeros((A, 128), F32)
                for y in range(first, first + count)
            ]
            rows.append(jnp.concatenate(spare, axis=1))
        rows = jnp.concatenate([row[None] for row in rows], axis=0)
        send2[:, :, wire * 128 : (wire + count) * 128] = jnp.swapaxes(rows, 0, 1).astype(BF16)

        def go(n, carry):
            i = lax.rem(n + place, A)
            to = jnp.where(i < 8, i, i + A)

            @pl.when(to != g)
            def _():
                remote(
                    half(send2, i, SECOND, h), half(out, g, SECOND, h), s2.at[h], r2.at[h], to
                ).start()

            return carry

        lax.fori_loop(0, A, go, 0)

    wait_first(0)
    got = arrived(0)
    tails = [folded(got, y, 4) for y in range(T)]
    project(0, [jnp.concatenate([got[y], tails[y][:, :64]], axis=1) for y in range(T)])
    wait_first(1)
    got = arrived(1)
    project(1, [jnp.concatenate([tails[y][:, 64:], got[y], folded(got, y, 3)], axis=1) for y in range(T)])
    for copy in coup_copies:
        copy.wait()
    coup = coup_in[0] + pltpu.roll(coup_out[...], 32, 1) + pltpu.roll(coup_in[1], 64, 1)
    lines0 = apply(0, coup)
    send_back([line[:, :512] for line in lines0], 0)
    lines1 = apply(1, coup)
    send_back([jnp.concatenate([a[:, 512:], b], axis=1) for a, b in zip(lines0, lines1)], 1)

    @pl.when(active)
    def _():
        own = pltpu.make_async_copy(send2.at[ai], out.at[g], self_sem)
        own.start()
        for h in range(2):
            whole(send1, G - 1, FIRST, h, s1, r1).wait_send()
            whole(send2, A - 1, SECOND, h, s2, r2).wait_send()
        own.wait()
        for h in range(2):
            whole(out, G - 1, SECOND, h, s2, r2).wait_recv()

    @pl.when(jnp.logical_not(active))
    def _():
        for h in range(2):
            whole(send2, A, SECOND, h, s2, r2).wait_send()


def last_kernel(cyt, recv, waves, out, cyv, got_ref, wlo, whi, zero, low, high, load_sem, store_sem):
    g = lax.axis_index("grid")
    active = jnp.logical_or(g < 8, g >= 24)

    @pl.when(active)
    def _():
        loads = [
            pltpu.make_async_copy(a, b, load_sem.at[n])
            for n, (a, b) in enumerate(
                (
                    (recv, got_ref), (cyt, cyv),
                    (waves.at[:, :, 0:48, :], wlo), (waves.at[:, :, 144:192, :], whi),
                )
            )
        ]
        for copy in loads:
            copy.start()
        zero[...] = jnp.zeros(zero.shape, BF16)
        stores = [pltpu.make_async_copy(zero, out.at[:, :, 48:144, :], store_sem.at[0])]
        stores[0].start()
        for copy in loads:
            copy.wait()
        got = got_ref[...].astype(F32)
        sub = lax.broadcasted_iota(jnp.int32, (G, 8, 128), 1)
        planes = []
        for wire, count, _ in SECOND:
            planes += [tile(got, wire + t) for t in range(count)]
            spare = jnp.zeros((G, 8, 128), F32)
            for y in range(T):
                row = 6 + y // count
                spare = jnp.where(sub == y, tile(got, wire + y % count)[:, row : row + 1, :], spare)
            planes.append(spare)
        planes = jnp.concatenate(planes, axis=2).reshape(256, 1152).astype(BF16)
        fifth = dot(cyv[...], planes)
        for b in range(2):
            for k in range(T):
                ksq = sphere_sq(g * T + k)
                n = (b * T + k) * 96
                total = ksq.astype(F32) / RAD2 * kept(wlo[b, k], whi[b, k]) + fifth[:, n : n + 96]
                total = jnp.where(ksq < RAD2, total, 0.0)
                total = jnp.concatenate([total[:, :48], jnp.zeros((96, 96), F32), total[:, 48:]], axis=1)
                total = total.astype(BF16)
                low[b, k] = total[:48]
                high[b, k] = total[48:]
            stores += [
                pltpu.make_async_copy(low.at[b], out.at[b, :, 0:48, :], store_sem.at[1 + 2 * b]),
                pltpu.make_async_copy(high.at[b], out.at[b, :, 144:192, :], store_sem.at[2 + 2 * b]),
            ]
            stores[-2].start()
            stores[-1].start()
        for copy in stores:
            copy.wait()

    @pl.when(jnp.logical_not(active))
    def _():
        zero[...] = jnp.zeros(zero.shape, BF16)
        stores = [
            pltpu.make_async_copy(zero, out.at[:, :, n * 96 : (n + 1) * 96, :], store_sem.at[n])
            for n in range(2)
        ]
        for copy in stores:
            copy.start()
        for copy in stores:
            copy.wait()


def shards(waves, potential, block_index, atom_of_slot, projectors, coupling):
    cy, cyt, cx, cxt, wz, wzt = (jnp.asarray(x) for x in tables())
    coup = jnp.transpose(coupling, (1, 2, 0)).reshape(64, 32)
    hbm = pl.BlockSpec(memory_space=pltpu.HBM)
    dma = pltpu.SemaphoreType.DMA
    recv = pl.pallas_call(
        main_kernel,
        name="exchange_and_apply",
        out_shape=jax.ShapeDtypeStruct((G, 8, 896), BF16),
        in_specs=[hbm] * 11,
        out_specs=hbm,
        scratch_shapes=[
            pltpu.VMEM((2, T, 48, N), BF16),
            pltpu.VMEM((2, T, 48, N), BF16),
            pltpu.VMEM((256, 96), BF16),
            pltpu.VMEM((N, 96), BF16),
            pltpu.VMEM((96, N), BF16),
            pltpu.VMEM((192, 384), BF16),
            pltpu.VMEM((384, 192), BF16),
            pltpu.VMEM((T, N, N), BF16),
            pltpu.VMEM((1, 512), jnp.int32),
            pltpu.VMEM((1, 512), jnp.int32),
            pltpu.VMEM((512, 8, 128), BF16),
            pltpu.VMEM((64, 32), F32),
            pltpu.VMEM((8, 512, 128), F32),
            pltpu.VMEM((9, N, 128), F32),
            pltpu.VMEM((512, 9 * N), BF16),
            pltpu.VMEM((9 * N, 512), BF16),
            pltpu.VMEM((512, 128), BF16),
            pltpu.VMEM((128, 1024), BF16),
            pltpu.VMEM((G, 8, 896), BF16),
            pltpu.VMEM((A, 8, 896), BF16),
            pltpu.VMEM((2, 9 * N, 128), BF16),
            pltpu.VMEM((A, 8, 896), BF16),
            pltpu.VMEM((64, 128), F32),
            pltpu.VMEM((2, 64, 128), F32),
            pltpu.VMEM((2, 8, 128), F32),
            pltpu.VMEM((2, 4, 8, 128), F32),
            dma((12,)),
            dma((2,)),
            dma((2,)),
            dma((2,)),
            dma((2,)),
            dma,
            dma((2, 4)),
            dma((2, 4)),
            dma((2,)),
            dma((2,)),
        ],
        compiler_params=pltpu.CompilerParams(
            collective_id=0, has_side_effects=True, vmem_limit_bytes=60 << 20
        ),
    )(
        waves, jnp.transpose(potential, (1, 0, 2)), block_index.reshape(1, -1), atom_of_slot.reshape(1, -1),
        projectors, coup, cy, cx, cxt, wz, wzt,
    )
    return pl.pallas_call(
        last_kernel,
        name="finish",
        out_shape=jax.ShapeDtypeStruct(waves.shape, BF16),
        in_specs=[hbm] * 3,
        out_specs=hbm,
        scratch_shapes=[
            pltpu.VMEM((96, 256), BF16),
            pltpu.VMEM((G, 8, 896), BF16),
            pltpu.VMEM((2, T, 48, N), BF16),
            pltpu.VMEM((2, T, 48, N), BF16),
            pltpu.VMEM((2, T, 96, N), BF16),
            pltpu.VMEM((2, T, 48, N), BF16),
            pltpu.VMEM((2, T, 48, N), BF16),
            dma((4,)),
            dma((5,)),
        ],
        compiler_params=pltpu.CompilerParams(vmem_limit_bytes=60 << 20),
    )(cyt, recv, waves)


def solution(mesh):
    in_specs = (
        P("band", "grid", None, None),
        P(None, "grid", None),
        P("grid"),
        P("grid"),
        P("grid", None, None),
        P("grid", None, None),
    )
    out_specs = P("band", "grid", None, None)
    return jax.shard_map(shards, mesh=mesh, in_specs=in_specs, out_specs=out_specs, check_vma=False)
```

```python
import functools
import math

import jax
import jax.numpy as jnp
import ml_dtypes
import numpy as np
from jax import lax
from jax.experimental import pallas as pl
from jax.experimental.pallas import tpu as pltpu
from jax.sharding import PartitionSpec as P

MESH = pl.DeviceIdType.MESH
F32, BF16 = jnp.float32, jnp.bfloat16
N, G, T = 192, 32, 6
A = 16
RAD2 = 48 * 48
KEEP = np.concatenate([np.arange(48), np.arange(144, 192)])
OFFSETS = (1, -1, 2, -2)
FIRST = ((0, 4, 0), (4, 3, 5))
SECOND = ((0, 3, 0), (3, 4, 4))


def tables():
    k = np.arange(N)
    angles = np.float32(2.0 * math.pi / N) * ((k[:, None] * k[None, :]) % N).astype(np.float32)
    c = ((np.cos(angles) + np.sin(angles)) / np.float32(math.sqrt(N))).astype(ml_dtypes.bfloat16)
    c = c.astype(np.float32)
    cy = np.zeros((G, 8, 96), np.float32)
    cy[:, :T] = c[:, KEEP].reshape(G, T, 96)
    cy = cy.reshape(256, 96)
    cx = c[:, KEEP].reshape(N, A, T).transpose(0, 2, 1).reshape(N, 96)
    wz = np.zeros((2, 96, 2, N), np.float32)
    for par in range(2):
        wz[par, :, par, :] = c[KEEP]
    wz = wz.reshape(192, 384)
    out = [cy, cy.T, cx, cx.T, wz, wz.T]
    return [np.ascontiguousarray(x).astype(ml_dtypes.bfloat16) for x in out]


def dot(a, b):
    return jnp.dot(a, b, preferred_element_type=F32)


def folded_sq(k):
    f = jnp.minimum(k, N - k)
    return f * f


def sphere_sq(kx):
    row = lax.broadcasted_iota(jnp.int32, (96, 96), 0)
    lane = lax.broadcasted_iota(jnp.int32, (96, 96), 1)
    ky = jnp.where(row < 48, row, row + 96)
    kz = jnp.where(lane < 48, lane, lane + 96)
    return folded_sq(kx) + folded_sq(ky) + folded_sq(kz)


def kept(low, high):
    w = jnp.concatenate([low, high], axis=0).astype(F32)
    return jnp.concatenate([w[:, :48], w[:, 144:]], axis=1)


def tile(x, n):
    return x[..., n * 128 : (n + 1) * 128]


def main_kernel(
    waves, pot, idx, atom, proj, coup, cy, cx, cxt, wz, wzt, out,
    wlo, whi, cyv, cxv, cxtv, wzv, wztv, potv, idxv, atomv, projv, coupv,
    projt, potc, oh1, oh2, oha, exp_up,
    send1, recv1, rs, send2, coup_out, coup_in, coef_out, coef_in,
    load_sem, s1, r1, s2, r2, self_sem, cs, cr, ks, kr,
):
    g = lax.axis_index("grid")
    active = jnp.logical_or(g < 8, g >= 24)
    ai = jnp.where(g < 8, g, g - 16)

    def peer(d):
        return lax.rem(g + d + G, G)

    wave_loads = [
        pltpu.make_async_copy(waves.at[:, :, 0:48, :], wlo, load_sem.at[0]),
        pltpu.make_async_copy(waves.at[:, :, 144:192, :], whi, load_sem.at[1]),
        pltpu.make_async_copy(cy, cyv, load_sem.at[2]),
    ]
    pairs = (
        (coup, coupv), (idx, idxv), (atom, atomv), (proj, projv), (pot, potv),
        (cx, cxv), (wz, wzv), (wzt, wztv), (cxt, cxtv),
    )
    loads = [pltpu.make_async_copy(a, b, load_sem.at[3 + n]) for n, (a, b) in enumerate(pairs)]

    @pl.when(active)
    def _():
        for copy in wave_loads:
            copy.start()

    barrier = pltpu.get_barrier_semaphore()
    for d in range(1, G):
        pl.semaphore_signal(barrier, inc=1, device_id={"grid": peer(d)}, device_id_type=MESH)

    for copy in loads:
        copy.start()

    def transform(h):
        parts = []
        wire, count, begin = FIRST[h]
        first, last = begin * 128 // 96, (begin + count + 1) * 128
        for n in range(first, -(-last // 96)):
            b, k = n // T, n % T
            inside = sphere_sq(g * T + k) < RAD2
            parts.append(jnp.where(inside, kept(wlo[b, k], whi[b, k]), 0.0))
        rhs = jnp.concatenate(parts, axis=1)
        skip = begin * 128 - first * 96
        rhs = rhs[:, skip : skip + (count + 1) * 128].astype(BF16)
        sub = lax.broadcasted_iota(jnp.int32, (G, 8, 128), 1)
        spare = dot(cyv[...], tile(rhs, count)).reshape(G, 8, 128)
        for t in range(count):
            plane = dot(cyv[...], tile(rhs, t)).reshape(G, 8, 128)
            for row, y in ((6, t), (7, t + count)):
                if y < T:
                    plane = jnp.where(sub == row, spare[:, y : y + 1, :], plane)
            send1[:, :, (wire + t) * 128 : (wire + t + 1) * 128] = plane.astype(BF16)

    @pl.when(active)
    def _():
        for copy in wave_loads:
            copy.wait()
        transform(0)

    pl.semaphore_wait(barrier, G - 1)

    my_row, place = g // A, lax.rem(g, A)
    partner = lax.rem(g + A, G)

    def half(ref, i, plan, h):
        return ref.at[i, :, pl.ds(plan[h][0] * 128, plan[h][1] * 128)]

    def remote(src, dst, send, recv, to):
        return pltpu.make_async_remote_copy(
            src_ref=src, dst_ref=dst, send_sem=send, recv_sem=recv,
            device_id={"grid": to}, device_id_type=MESH,
        )

    def whole(ref, count, plan, h, send, recv):
        chunks = half(ref, pl.ds(0, count), plan, h)
        return remote(chunks, chunks, send.at[h], recv.at[h], partner)

    def first_copy(row, n, h):
        to = row * A + lax.rem(place + n, A)
        remote(
            half(send1, to, FIRST, h), half(recv1, ai, FIRST, h), s1.at[h], r1.at[h], to
        ).start()

    @pl.when(active)
    def _():
        for h in range(2):
            if h == 1:
                transform(1)

            def across(n, carry):
                first_copy(1 - my_row, n, h)
                return carry

            def along(n, carry):
                first_copy(my_row, n, h)
                return carry

            lax.fori_loop(0, A, across, 0)
            lax.fori_loop(1, A, along, 0)
        recv1[ai] = send1[g]

    for copy in loads:
        copy.wait()
    coup_out[...] = jnp.concatenate([coupv[...], jnp.zeros((64, 96), F32)], axis=1)
    coup_copies = [
        pltpu.make_async_remote_copy(
            src_ref=coup_out, dst_ref=coup_in.at[n], send_sem=ks.at[n], recv_sem=kr.at[n],
            device_id={"grid": peer(d)}, device_id_type=MESH,
        )
        for n, d in enumerate(OFFSETS[:2])
    ]
    for copy in coup_copies:
        copy.start()

    idx_row = idxv[...]
    atom_row = atomv[...]
    atom_row = ((lax.shift_right_logical(atom_row, 5) - g + 33) & 31) * 32 + (atom_row & 31)

    def column(row):
        return jnp.transpose(jnp.broadcast_to(row.astype(F32), (128, 512))).astype(jnp.int32)

    idx_col = column(idx_row)[:, :1]
    lane = lax.broadcasted_iota(jnp.int32, (1, 9 * N), 1)
    ninth = lax.shift_right_logical(lane * 43691, 23)
    oh1[...] = jnp.where((lane - ninth * N) * 9 + ninth == idx_col, 1.0, 0.0).astype(BF16)
    row192 = lax.broadcasted_iota(jnp.int32, (N, 512), 0) * 9
    for c in range(9):
        oh2[c * N : (c + 1) * N] = jnp.where(row192 + c == idx_row, 1.0, 0.0).astype(BF16)
    lane128 = lax.broadcasted_iota(jnp.int32, (512, 128), 1)
    oha[...] = jnp.where(column(atom_row) == lane128, 1.0, 0.0).astype(BF16)
    up_row = lax.broadcasted_iota(jnp.int32, (128, 1024), 0)
    up_lane = lax.broadcasted_iota(jnp.int32, (128, 1024), 1)
    exp_up[...] = jnp.where(lax.shift_right_logical(up_lane, 7) == up_row, 1.0, 0.0).astype(BF16)
    projt[...] = jnp.swapaxes(projv[...].astype(F32), 0, 1)
    pt = potv[...].astype(F32)
    for j in range(3):
        e, o = pt[2 * j], pt[2 * j + 1]
        potc[3 * j] = e[:, :128]
        potc[3 * j + 1] = jnp.concatenate([e[:, 128:], o[:, :64]], axis=1)
        potc[3 * j + 2] = o[:, 64:]

    def wait_first(h):
        @pl.when(active)
        def _():
            whole(recv1, A - 1, FIRST, h, s1, r1).wait_recv()

        @pl.when(jnp.logical_not(active))
        def _():
            whole(recv1, A, FIRST, h, s1, r1).wait_recv()

    def arrived(h):
        wire, count, _ = FIRST[h]
        return jnp.swapaxes(recv1[:, :, wire * 128 : (wire + count) * 128].astype(F32), 0, 1)

    def folded(got, y, count):
        return tile(got[6 + y // count], y % count)

    def coef_copies(b):
        return [
            pltpu.make_async_remote_copy(
                src_ref=coef_out.at[b], dst_ref=coef_in.at[b, n], send_sem=cs.at[b, n], recv_sem=cr.at[b, n],
                device_id={"grid": peer(d)}, device_id_type=MESH,
            )
            for n, d in enumerate(OFFSETS)
        ]

    def project(b, lines):
        stacks = [
            jnp.concatenate([line[:, k * 96 : (k + 1) * 96] for k in range(T)], axis=0) for line in lines
        ]
        for j in range(3):
            rhs = jnp.concatenate([stacks[2 * j], stacks[2 * j + 1]], axis=1).astype(BF16)
            part = dot(cxv[...], rhs).astype(BF16)
            real = dot(part, wzv[...]).astype(BF16)
            for t in range(3):
                c = 3 * j + t
                rs[b, c * N : (c + 1) * N] = tile(real, t)
        rows = dot(oh1[...], rs[b])
        prod = jnp.concatenate([(projt[p] * rows).astype(BF16) for p in range(8)], axis=1)
        inter = lax.dot_general(
            prod, exp_up[...], (((1,), (1,)), ((), ())), preferred_element_type=F32
        )
        inter = jnp.transpose(inter)[:16]
        high = inter.astype(BF16)
        low = (inter - high.astype(F32)).astype(BF16)
        coef_out[b] = (dot(high, oha[...]) + dot(low, oha[...]))[:8]
        for copy in coef_copies(b):
            copy.start()

    def apply(b, coup):
        for copy in coef_copies(b):
            copy.wait()
        lane = lax.broadcasted_iota(jnp.int32, (8, 128), 1)
        coef = coef_out[b] + pltpu.roll(coef_in[b, 0], 96, 1) + pltpu.roll(coef_in[b, 1], 32, 1)
        coef = coef + jnp.where(lane < 32, pltpu.roll(coef_in[b, 2], 64, 1), 0.0)
        coef = coef + jnp.where(
            jnp.logical_and(lane >= 64, lane < 96), pltpu.roll(coef_in[b, 3], 64, 1), 0.0
        )
        coupled = [jnp.sum(coup[8 * p : 8 * p + 8] * coef, axis=0, keepdims=True) for p in range(8)]
        coupled = jnp.concatenate(coupled + [jnp.zeros((120, 128), F32)], axis=0).astype(BF16)
        chosen = lax.dot_general(
            oha[...], coupled, (((1,), (1,)), ((), ())), preferred_element_type=F32
        ).astype(BF16)
        back = projt[0] * dot(chosen, tile(exp_up[...], 0))
        for p in range(1, 8):
            back = back + projt[p] * dot(chosen, tile(exp_up[...], p))
        back = back.astype(BF16)
        spread = dot(oh2[...], back)
        lines = []
        for j in range(3):
            row = []
            for c in range(3 * j, 3 * j + 3):
                cut = slice(c * N, (c + 1) * N)
                row.append((potc[c] * rs[b, cut].astype(F32) + spread[cut]).astype(BF16))
            part = dot(jnp.concatenate(row, axis=1), wztv[...]).astype(BF16)
            part = dot(cxtv[...], part)
            for par in range(2):
                lines.append(
                    jnp.concatenate(
                        [part[k * A : (k + 1) * A, par * 96 : (par + 1) * 96] for k in range(T)], axis=1
                    )
                )
        return lines

    def send_back(lines, h):
        wire, count, _ = SECOND[h]
        rows = [line[:, : count * 128] for line in lines]
        for first in (0, count):
            spare = [
                lines[y][:, count * 128 :] if y < T else jnp.zeros((A, 128), F32)
                for y in range(first, first + count)
            ]
            rows.append(jnp.concatenate(spare, axis=1))
        rows = jnp.concatenate([row[None] for row in rows], axis=0)
        send2[:, :, wire * 128 : (wire + count) * 128] = jnp.swapaxes(rows, 0, 1).astype(BF16)

        def go(n, carry):
            i = jnp.where(n < 8, 1 - my_row, my_row) * 8 + lax.rem(n + place, 8)
            to = jnp.where(i < 8, i, i + A)

            @pl.when(to != g)
            def _():
                remote(
                    half(send2, i, SECOND, h), half(out, g, SECOND, h), s2.at[h], r2.at[h], to
                ).start()

            return carry

        lax.fori_loop(0, A, go, 0)

    wait_first(0)
    got = arrived(0)
    tails = [folded(got, y, 4) for y in range(T)]
    project(0, [jnp.concatenate([got[y], tails[y][:, :64]], axis=1) for y in range(T)])
    wait_first(1)
    got = arrived(1)
    project(1, [jnp.concatenate([tails[y][:, 64:], got[y], folded(got, y, 3)], axis=1) for y in range(T)])
    for copy in coup_copies:
        copy.wait()
    coup = coup_in[0] + pltpu.roll(coup_out[...], 32, 1) + pltpu.roll(coup_in[1], 64, 1)
    lines0 = apply(0, coup)
    send_back([line[:, :512] for line in lines0], 0)
    lines1 = apply(1, coup)
    send_back([jnp.concatenate([a[:, 512:], b], axis=1) for a, b in zip(lines0, lines1)], 1)

    @pl.when(active)
    def _():
        own = pltpu.make_async_copy(send2.at[ai], out.at[g], self_sem)
        own.start()
        for h in range(2):
            whole(send1, G - 1, FIRST, h, s1, r1).wait_send()
            whole(send2, A - 1, SECOND, h, s2, r2).wait_send()
        own.wait()
        for h in range(2):
            whole(out, G - 1, SECOND, h, s2, r2).wait_recv()

    @pl.when(jnp.logical_not(active))
    def _():
        for h in range(2):
            whole(send2, A, SECOND, h, s2, r2).wait_send()


def last_kernel(cyt, recv, waves, out, cyv, got_ref, wlo, whi, zero, low, high, load_sem, store_sem):
    g = lax.axis_index("grid")
    active = jnp.logical_or(g < 8, g >= 24)

    @pl.when(active)
    def _():
        loads = [
            pltpu.make_async_copy(a, b, load_sem.at[n])
            for n, (a, b) in enumerate(
                (
                    (recv, got_ref), (cyt, cyv),
                    (waves.at[:, :, 0:48, :], wlo), (waves.at[:, :, 144:192, :], whi),
                )
            )
        ]
        for copy in loads:
            copy.start()
        zero[...] = jnp.zeros(zero.shape, BF16)
        stores = [pltpu.make_async_copy(zero, out.at[:, :, 48:144, :], store_sem.at[0])]
        stores[0].start()
        for copy in loads[:2]:
            copy.wait()
        got = got_ref[...].astype(F32)
        sub = lax.broadcasted_iota(jnp.int32, (G, 8, 128), 1)
        planes = []
        for wire, count, _ in SECOND:
            planes += [tile(got, wire + t) for t in range(count)]
            spare = jnp.zeros((G, 8, 128), F32)
            for y in range(T):
                row = 6 + y // count
                spare = jnp.where(sub == y, tile(got, wire + y % count)[:, row : row + 1, :], spare)
            planes.append(spare)
        planes = jnp.concatenate(planes, axis=2).reshape(256, 1152).astype(BF16)
        fifth = dot(cyv[...], planes)
        for copy in loads[2:]:
            copy.wait()
        for b in range(2):
            for k in range(T):
                ksq = sphere_sq(g * T + k)
                n = (b * T + k) * 96
                total = ksq.astype(F32) / RAD2 * kept(wlo[b, k], whi[b, k]) + fifth[:, n : n + 96]
                total = jnp.where(ksq < RAD2, total, 0.0)
                total = jnp.concatenate([total[:, :48], jnp.zeros((96, 96), F32), total[:, 48:]], axis=1)
                total = total.astype(BF16)
                low[b, k] = total[:48]
                high[b, k] = total[48:]
            stores += [
                pltpu.make_async_copy(low.at[b], out.at[b, :, 0:48, :], store_sem.at[1 + 2 * b]),
                pltpu.make_async_copy(high.at[b], out.at[b, :, 144:192, :], store_sem.at[2 + 2 * b]),
            ]
            stores[-2].start()
            stores[-1].start()
        for copy in stores:
            copy.wait()

    @pl.when(jnp.logical_not(active))
    def _():
        zero[...] = jnp.zeros(zero.shape, BF16)
        stores = [
            pltpu.make_async_copy(zero, out.at[:, :, n * 96 : (n + 1) * 96, :], store_sem.at[n])
            for n in range(2)
        ]
        for copy in stores:
            copy.start()
        for copy in stores:
            copy.wait()


def shards(waves, potential, block_index, atom_of_slot, projectors, coupling):
    cy, cyt, cx, cxt, wz, wzt = (jnp.asarray(x) for x in tables())
    coup = jnp.transpose(coupling, (1, 2, 0)).reshape(64, 32)
    hbm = pl.BlockSpec(memory_space=pltpu.HBM)
    dma = pltpu.SemaphoreType.DMA
    recv = pl.pallas_call(
        main_kernel,
        name="exchange_and_apply",
        out_shape=jax.ShapeDtypeStruct((G, 8, 896), BF16),
        in_specs=[hbm] * 11,
        out_specs=hbm,
        scratch_shapes=[
            pltpu.VMEM((2, T, 48, N), BF16),
            pltpu.VMEM((2, T, 48, N), BF16),
            pltpu.VMEM((256, 96), BF16),
            pltpu.VMEM((N, 96), BF16),
            pltpu.VMEM((96, N), BF16),
            pltpu.VMEM((192, 384), BF16),
            pltpu.VMEM((384, 192), BF16),
            pltpu.VMEM((T, N, N), BF16),
            pltpu.VMEM((1, 512), jnp.int32),
            pltpu.VMEM((1, 512), jnp.int32),
            pltpu.VMEM((512, 8, 128), BF16),
            pltpu.VMEM((64, 32), F32),
            pltpu.VMEM((8, 512, 128), F32),
            pltpu.VMEM((9, N, 128), F32),
            pltpu.VMEM((512, 9 * N), BF16),
            pltpu.VMEM((9 * N, 512), BF16),
            pltpu.VMEM((512, 128), BF16),
            pltpu.VMEM((128, 1024), BF16),
            pltpu.VMEM((G, 8, 896), BF16),
            pltpu.VMEM((A, 8, 896), BF16),
            pltpu.VMEM((2, 9 * N, 128), BF16),
            pltpu.VMEM((A, 8, 896), BF16),
            pltpu.VMEM((64, 128), F32),
            pltpu.VMEM((2, 64, 128), F32),
            pltpu.VMEM((2, 8, 128), F32),
            pltpu.VMEM((2, 4, 8, 128), F32),
            dma((12,)),
            dma((2,)),
            dma((2,)),
            dma((2,)),
            dma((2,)),
            dma,
            dma((2, 4)),
            dma((2, 4)),
            dma((2,)),
            dma((2,)),
        ],
        compiler_params=pltpu.CompilerParams(
            collective_id=0, has_side_effects=True, vmem_limit_bytes=60 << 20
        ),
    )(
        waves, jnp.transpose(potential, (1, 0, 2)), block_index.reshape(1, -1), atom_of_slot.reshape(1, -1),
        projectors, coup, cy, cx, cxt, wz, wzt,
    )
    return pl.pallas_call(
        last_kernel,
        name="finish",
        out_shape=jax.ShapeDtypeStruct(waves.shape, BF16),
        in_specs=[hbm] * 3,
        out_specs=hbm,
        scratch_shapes=[
            pltpu.VMEM((96, 256), BF16),
            pltpu.VMEM((G, 8, 896), BF16),
            pltpu.VMEM((2, T, 48, N), BF16),
            pltpu.VMEM((2, T, 48, N), BF16),
            pltpu.VMEM((2, T, 96, N), BF16),
            pltpu.VMEM((2, T, 48, N), BF16),
            pltpu.VMEM((2, T, 48, N), BF16),
            dma((4,)),
            dma((5,)),
        ],
        compiler_params=pltpu.CompilerParams(vmem_limit_bytes=60 << 20),
    )(cyt, recv, waves)


def solution(mesh):
    in_specs = (
        P("band", "grid", None, None),
        P(None, "grid", None),
        P("grid"),
        P("grid"),
        P("grid", None, None),
        P("grid", None, None),
    )
    out_specs = P("band", "grid", None, None)
    return jax.shard_map(shards, mesh=mesh, in_specs=in_specs, out_specs=out_specs, check_vma=False)
```

```python
import functools
import math

import jax
import jax.numpy as jnp
import ml_dtypes
import numpy as np
from jax import lax
from jax.experimental import pallas as pl
from jax.experimental.pallas import tpu as pltpu
from jax.sharding import PartitionSpec as P

MESH = pl.DeviceIdType.MESH
F32, BF16 = jnp.float32, jnp.bfloat16
N, G, T = 192, 32, 6
A = 16
RAD2 = 48 * 48
KEEP = np.concatenate([np.arange(48), np.arange(144, 192)])
OFFSETS = (1, -1, 2, -2)
FIRST = ((0, 4, 0), (4, 3, 5))
SECOND = ((0, 3, 0), (3, 4, 4))


def tables():
    k = np.arange(N)
    angles = np.float32(2.0 * math.pi / N) * ((k[:, None] * k[None, :]) % N).astype(np.float32)
    c = ((np.cos(angles) + np.sin(angles)) / np.float32(math.sqrt(N))).astype(ml_dtypes.bfloat16)
    c = c.astype(np.float32)
    cy = np.zeros((G, 8, 96), np.float32)
    cy[:, :T] = c[:, KEEP].reshape(G, T, 96)
    cy = cy.reshape(256, 96)
    cx = c[:, KEEP].reshape(N, A, T).transpose(0, 2, 1).reshape(N, 96)
    wz = np.zeros((2, 96, 2, N), np.float32)
    for par in range(2):
        wz[par, :, par, :] = c[KEEP]
    wz = wz.reshape(192, 384)
    out = [cy, cy.T, cx, cx.T, wz, wz.T]
    return [np.ascontiguousarray(x).astype(ml_dtypes.bfloat16) for x in out]


def dot(a, b):
    return jnp.dot(a, b, preferred_element_type=F32)


def folded_sq(k):
    f = jnp.minimum(k, N - k)
    return f * f


def sphere_sq(kx):
    row = lax.broadcasted_iota(jnp.int32, (96, 96), 0)
    lane = lax.broadcasted_iota(jnp.int32, (96, 96), 1)
    ky = jnp.where(row < 48, row, row + 96)
    kz = jnp.where(lane < 48, lane, lane + 96)
    return folded_sq(kx) + folded_sq(ky) + folded_sq(kz)


def kept(low, high):
    w = jnp.concatenate([low, high], axis=0).astype(F32)
    return jnp.concatenate([w[:, :48], w[:, 144:]], axis=1)


def tile(x, n):
    return x[..., n * 128 : (n + 1) * 128]


def main_kernel(
    waves, pot, idx, atom, proj, coup, cy, cx, cxt, wz, wzt, out,
    wlo, whi, cyv, cxv, cxtv, wzv, wztv, potv, idxv, atomv, projv, coupv,
    projt, potc, oh1, oh2, oha, exp_up,
    send1, recv1, rs, send2, coup_out, coup_in, coef_out, coef_in,
    load_sem, s1, r1, s2, r2, self_sem, cs, cr, ks, kr,
):
    g = lax.axis_index("grid")
    active = jnp.logical_or(g < 8, g >= 24)
    ai = jnp.where(g < 8, g, g - 16)

    def peer(d):
        return lax.rem(g + d + G, G)

    wave_loads = [
        pltpu.make_async_copy(waves.at[:, :, 0:48, :], wlo, load_sem.at[0]),
        pltpu.make_async_copy(waves.at[:, :, 144:192, :], whi, load_sem.at[1]),
        pltpu.make_async_copy(cy, cyv, load_sem.at[2]),
    ]
    pairs = (
        (coup, coupv), (idx, idxv), (atom, atomv), (proj, projv), (pot, potv),
        (cx, cxv), (wz, wzv), (wzt, wztv), (cxt, cxtv),
    )
    loads = [pltpu.make_async_copy(a, b, load_sem.at[3 + n]) for n, (a, b) in enumerate(pairs)]

    @pl.when(active)
    def _():
        for copy in wave_loads:
            copy.start()

    barrier = pltpu.get_barrier_semaphore()
    for d in range(1, G):
        pl.semaphore_signal(barrier, inc=1, device_id={"grid": peer(d)}, device_id_type=MESH)

    for copy in loads:
        copy.start()

    def transform(h):
        parts = []
        wire, count, begin = FIRST[h]
        first, last = begin * 128 // 96, (begin + count + 1) * 128
        for n in range(first, -(-last // 96)):
            b, k = n // T, n % T
            inside = sphere_sq(g * T + k) < RAD2
            parts.append(jnp.where(inside, kept(wlo[b, k], whi[b, k]), 0.0))
        rhs = jnp.concatenate(parts, axis=1)
        skip = begin * 128 - first * 96
        rhs = rhs[:, skip : skip + (count + 1) * 128].astype(BF16)
        sub = lax.broadcasted_iota(jnp.int32, (G, 8, 128), 1)
        spare = dot(cyv[...], tile(rhs, count)).reshape(G, 8, 128)
        for t in range(count):
            plane = dot(cyv[...], tile(rhs, t)).reshape(G, 8, 128)
            for row, y in ((6, t), (7, t + count)):
                if y < T:
                    plane = jnp.where(sub == row, spare[:, y : y + 1, :], plane)
            send1[:, :, (wire + t) * 128 : (wire + t + 1) * 128] = plane.astype(BF16)

    @pl.when(active)
    def _():
        for copy in wave_loads:
            copy.wait()
        transform(0)

    pl.semaphore_wait(barrier, G - 1)

    my_row, place = g // A, lax.rem(g, A)
    partner = lax.rem(g + A, G)

    def half(ref, i, plan, h):
        return ref.at[i, :, pl.ds(plan[h][0] * 128, plan[h][1] * 128)]

    def remote(src, dst, send, recv, to):
        return pltpu.make_async_remote_copy(
            src_ref=src, dst_ref=dst, send_sem=send, recv_sem=recv,
            device_id={"grid": to}, device_id_type=MESH,
        )

    def whole(ref, count, plan, h, send, recv):
        chunks = half(ref, pl.ds(0, count), plan, h)
        return remote(chunks, chunks, send.at[h], recv.at[h], partner)

    def first_copy(row, n, h):
        to = row * A + lax.rem(place + n, A)
        remote(
            half(send1, to, FIRST, h), half(recv1, ai, FIRST, h), s1.at[h], r1.at[h], to
        ).start()

    @pl.when(active)
    def _():
        for h in range(2):
            if h == 1:
                transform(1)

            def across(n, carry):
                first_copy(1 - my_row, n, h)
                return carry

            def along(n, carry):
                first_copy(my_row, n, h)
                return carry

            lax.fori_loop(0, A, across, 0)
            lax.fori_loop(1, A, along, 0)
        recv1[ai] = send1[g]

    for copy in loads:
        copy.wait()
    coup_out[...] = jnp.concatenate([coupv[...], jnp.zeros((64, 96), F32)], axis=1)
    coup_copies = [
        pltpu.make_async_remote_copy(
            src_ref=coup_out, dst_ref=coup_in.at[n], send_sem=ks.at[n], recv_sem=kr.at[n],
            device_id={"grid": peer(d)}, device_id_type=MESH,
        )
        for n, d in enumerate(OFFSETS[:2])
    ]
    for copy in coup_copies:
        copy.start()

    idx_row = idxv[...]
    atom_row = atomv[...]
    atom_row = ((lax.shift_right_logical(atom_row, 5) - g + 33) & 31) * 32 + (atom_row & 31)

    def column(row):
        return jnp.transpose(jnp.broadcast_to(row.astype(F32), (128, 512))).astype(jnp.int32)

    idx_col = column(idx_row)[:, :1]
    lane = lax.broadcasted_iota(jnp.int32, (1, 9 * N), 1)
    ninth = lax.shift_right_logical(lane * 43691, 23)
    oh1[...] = jnp.where((lane - ninth * N) * 9 + ninth == idx_col, 1.0, 0.0).astype(BF16)
    row192 = lax.broadcasted_iota(jnp.int32, (N, 512), 0) * 9
    for c in range(9):
        oh2[c * N : (c + 1) * N] = jnp.where(row192 + c == idx_row, 1.0, 0.0).astype(BF16)
    lane128 = lax.broadcasted_iota(jnp.int32, (512, 128), 1)
    oha[...] = jnp.where(column(atom_row) == lane128, 1.0, 0.0).astype(BF16)
    up_row = lax.broadcasted_iota(jnp.int32, (128, 1024), 0)
    up_lane = lax.broadcasted_iota(jnp.int32, (128, 1024), 1)
    exp_up[...] = jnp.where(lax.shift_right_logical(up_lane, 7) == up_row, 1.0, 0.0).astype(BF16)
    projt[...] = jnp.swapaxes(projv[...].astype(F32), 0, 1)
    pt = potv[...].astype(F32)
    for j in range(3):
        e, o = pt[2 * j], pt[2 * j + 1]
        potc[3 * j] = e[:, :128]
        potc[3 * j + 1] = jnp.concatenate([e[:, 128:], o[:, :64]], axis=1)
        potc[3 * j + 2] = o[:, 64:]

    def wait_first(h):
        @pl.when(active)
        def _():
            whole(recv1, A - 1, FIRST, h, s1, r1).wait_recv()

        @pl.when(jnp.logical_not(active))
        def _():
            whole(recv1, A, FIRST, h, s1, r1).wait_recv()

    def arrived(h):
        wire, count, _ = FIRST[h]
        return jnp.swapaxes(recv1[:, :, wire * 128 : (wire + count) * 128].astype(F32), 0, 1)

    def folded(got, y, count):
        return tile(got[6 + y // count], y % count)

    def coef_copies(b):
        return [
            pltpu.make_async_remote_copy(
                src_ref=coef_out.at[b], dst_ref=coef_in.at[b, n], send_sem=cs.at[b, n], recv_sem=cr.at[b, n],
                device_id={"grid": peer(d)}, device_id_type=MESH,
            )
            for n, d in enumerate(OFFSETS)
        ]

    def project(b, lines):
        stacks = [
            jnp.concatenate([line[:, k * 96 : (k + 1) * 96] for k in range(T)], axis=0) for line in lines
        ]
        for j in range(3):
            rhs = jnp.concatenate([stacks[2 * j], stacks[2 * j + 1]], axis=1).astype(BF16)
            part = dot(cxv[...], rhs).astype(BF16)
            real = dot(part, wzv[...]).astype(BF16)
            for t in range(3):
                c = 3 * j + t
                rs[b, c * N : (c + 1) * N] = tile(real, t)
        rows = dot(oh1[...], rs[b])
        prod = jnp.concatenate([(projt[p] * rows).astype(BF16) for p in range(8)], axis=1)
        inter = lax.dot_general(
            prod, exp_up[...], (((1,), (1,)), ((), ())), preferred_element_type=F32
        )
        inter = jnp.transpose(inter)[:16]
        high = inter.astype(BF16)
        low = (inter - high.astype(F32)).astype(BF16)
        coef_out[b] = (dot(high, oha[...]) + dot(low, oha[...]))[:8]
        for copy in coef_copies(b):
            copy.start()

    def apply(b, coup):
        for copy in coef_copies(b):
            copy.wait()
        lane = lax.broadcasted_iota(jnp.int32, (8, 128), 1)
        coef = coef_out[b] + pltpu.roll(coef_in[b, 0], 96, 1) + pltpu.roll(coef_in[b, 1], 32, 1)
        coef = coef + jnp.where(lane < 32, pltpu.roll(coef_in[b, 2], 64, 1), 0.0)
        coef = coef + jnp.where(
            jnp.logical_and(lane >= 64, lane < 96), pltpu.roll(coef_in[b, 3], 64, 1), 0.0
        )
        coupled = [jnp.sum(coup[8 * p : 8 * p + 8] * coef, axis=0, keepdims=True) for p in range(8)]
        coupled = jnp.concatenate(coupled + [jnp.zeros((120, 128), F32)], axis=0).astype(BF16)
        chosen = lax.dot_general(
            oha[...], coupled, (((1,), (1,)), ((), ())), preferred_element_type=F32
        ).astype(BF16)
        back = projt[0] * dot(chosen, tile(exp_up[...], 0))
        for p in range(1, 8):
            back = back + projt[p] * dot(chosen, tile(exp_up[...], p))
        back = back.astype(BF16)
        spread = dot(oh2[...], back)
        lines = []
        for j in range(3):
            row = []
            for c in range(3 * j, 3 * j + 3):
                cut = slice(c * N, (c + 1) * N)
                row.append((potc[c] * rs[b, cut].astype(F32) + spread[cut]).astype(BF16))
            part = dot(jnp.concatenate(row, axis=1), wztv[...]).astype(BF16)
            part = dot(cxtv[...], part)
            for par in range(2):
                lines.append(
                    jnp.concatenate(
                        [part[k * A : (k + 1) * A, par * 96 : (par + 1) * 96] for k in range(T)], axis=1
                    )
                )
        return lines

    def send_back(lines, h):
        wire, count, _ = SECOND[h]
        rows = [line[:, : count * 128] for line in lines]
        for first in (0, count):
            spare = [
                lines[y][:, count * 128 :] if y < T else jnp.zeros((A, 128), F32)
                for y in range(first, first + count)
            ]
            rows.append(jnp.concatenate(spare, axis=1))
        rows = jnp.concatenate([row[None] for row in rows], axis=0)
        send2[:, :, wire * 128 : (wire + count) * 128] = jnp.swapaxes(rows, 0, 1).astype(BF16)

        def go(n, carry):
            i = lax.rem(n + place, A)
            to = jnp.where(i < 8, i, i + A)

            @pl.when(to != g)
            def _():
                remote(
                    half(send2, i, SECOND, h), half(out, g, SECOND, h), s2.at[h], r2.at[h], to
                ).start()

            return carry

        lax.fori_loop(0, A, go, 0)

    wait_first(0)
    got = arrived(0)
    tails = [folded(got, y, 4) for y in range(T)]
    project(0, [jnp.concatenate([got[y], tails[y][:, :64]], axis=1) for y in range(T)])
    wait_first(1)
    got = arrived(1)
    project(1, [jnp.concatenate([tails[y][:, 64:], got[y], folded(got, y, 3)], axis=1) for y in range(T)])
    for copy in coup_copies:
        copy.wait()
    coup = coup_in[0] + pltpu.roll(coup_out[...], 32, 1) + pltpu.roll(coup_in[1], 64, 1)
    lines0 = apply(0, coup)
    send_back([line[:, :512] for line in lines0], 0)
    lines1 = apply(1, coup)
    send_back([jnp.concatenate([a[:, 512:], b], axis=1) for a, b in zip(lines0, lines1)], 1)

    @pl.when(active)
    def _():
        own = pltpu.make_async_copy(send2.at[ai], out.at[g], self_sem)
        own.start()
        for h in range(2):
            whole(send1, G - 1, FIRST, h, s1, r1).wait_send()
            whole(send2, A - 1, SECOND, h, s2, r2).wait_send()
        own.wait()
        for h in range(2):
            whole(out, G - 1, SECOND, h, s2, r2).wait_recv()

    @pl.when(jnp.logical_not(active))
    def _():
        for h in range(2):
            whole(send2, A, SECOND, h, s2, r2).wait_send()


def last_kernel(cyt, recv, waves, out, cyv, got_ref, wlo, whi, zero, low, high, load_sem, store_sem):
    g = lax.axis_index("grid")
    active = jnp.logical_or(g < 8, g >= 24)

    @pl.when(active)
    def _():
        loads = [
            pltpu.make_async_copy(a, b, load_sem.at[n])
            for n, (a, b) in enumerate(
                (
                    (recv, got_ref), (cyt, cyv),
                    (waves.at[:, :, 0:48, :], wlo), (waves.at[:, :, 144:192, :], whi),
                )
            )
        ]
        for copy in loads:
            copy.start()
        zero[...] = jnp.zeros(zero.shape, BF16)
        stores = [pltpu.make_async_copy(zero, out.at[:, :, 48:144, :], store_sem.at[0])]
        stores[0].start()
        for copy in loads[:2]:
            copy.wait()
        got = got_ref[...].astype(F32)
        sub = lax.broadcasted_iota(jnp.int32, (G, 8, 128), 1)
        planes = []
        for wire, count, _ in SECOND:
            planes += [tile(got, wire + t) for t in range(count)]
            spare = jnp.zeros((G, 8, 128), F32)
            for y in range(T):
                row = 6 + y // count
                spare = jnp.where(sub == y, tile(got, wire + y % count)[:, row : row + 1, :], spare)
            planes.append(spare)
        planes = jnp.concatenate(planes, axis=2).reshape(256, 1152).astype(BF16)
        fifth = dot(cyv[...], planes)
        for copy in loads[2:]:
            copy.wait()
        for b in range(2):
            for k in range(T):
                ksq = sphere_sq(g * T + k)
                n = (b * T + k) * 96
                total = ksq.astype(F32) / RAD2 * kept(wlo[b, k], whi[b, k]) + fifth[:, n : n + 96]
                total = jnp.where(ksq < RAD2, total, 0.0)
                total = jnp.concatenate([total[:, :48], jnp.zeros((96, 96), F32), total[:, 48:]], axis=1)
                total = total.astype(BF16)
                low[b, k] = total[:48]
                high[b, k] = total[48:]
            stores += [
                pltpu.make_async_copy(low.at[b], out.at[b, :, 0:48, :], store_sem.at[1 + 2 * b]),
                pltpu.make_async_copy(high.at[b], out.at[b, :, 144:192, :], store_sem.at[2 + 2 * b]),
            ]
            stores[-2].start()
            stores[-1].start()
        for copy in stores:
            copy.wait()

    @pl.when(jnp.logical_not(active))
    def _():
        zero[...] = jnp.zeros(zero.shape, BF16)
        stores = [
            pltpu.make_async_copy(zero, out.at[:, :, n * 96 : (n + 1) * 96, :], store_sem.at[n])
            for n in range(2)
        ]
        for copy in stores:
            copy.start()
        for copy in stores:
            copy.wait()


def shards(waves, potential, block_index, atom_of_slot, projectors, coupling):
    cy, cyt, cx, cxt, wz, wzt = (jnp.asarray(x) for x in tables())
    coup = jnp.transpose(coupling, (1, 2, 0)).reshape(64, 32)
    hbm = pl.BlockSpec(memory_space=pltpu.HBM)
    dma = pltpu.SemaphoreType.DMA
    recv = pl.pallas_call(
        main_kernel,
        name="exchange_and_apply",
        out_shape=jax.ShapeDtypeStruct((G, 8, 896), BF16),
        in_specs=[hbm] * 11,
        out_specs=hbm,
        scratch_shapes=[
            pltpu.VMEM((2, T, 48, N), BF16),
            pltpu.VMEM((2, T, 48, N), BF16),
            pltpu.VMEM((256, 96), BF16),
            pltpu.VMEM((N, 96), BF16),
            pltpu.VMEM((96, N), BF16),
            pltpu.VMEM((192, 384), BF16),
            pltpu.VMEM((384, 192), BF16),
            pltpu.VMEM((T, N, N), BF16),
            pltpu.VMEM((1, 512), jnp.int32),
            pltpu.VMEM((1, 512), jnp.int32),
            pltpu.VMEM((512, 8, 128), BF16),
            pltpu.VMEM((64, 32), F32),
            pltpu.VMEM((8, 512, 128), F32),
            pltpu.VMEM((9, N, 128), F32),
            pltpu.VMEM((512, 9 * N), BF16),
            pltpu.VMEM((9 * N, 512), BF16),
            pltpu.VMEM((512, 128), BF16),
            pltpu.VMEM((128, 1024), BF16),
            pltpu.VMEM((G, 8, 896), BF16),
            pltpu.VMEM((A, 8, 896), BF16),
            pltpu.VMEM((2, 9 * N, 128), BF16),
            pltpu.VMEM((A, 8, 896), BF16),
            pltpu.VMEM((64, 128), F32),
            pltpu.VMEM((2, 64, 128), F32),
            pltpu.VMEM((2, 8, 128), F32),
            pltpu.VMEM((2, 4, 8, 128), F32),
            dma((12,)),
            dma((2,)),
            dma((2,)),
            dma((2,)),
            dma((2,)),
            dma,
            dma((2, 4)),
            dma((2, 4)),
            dma((2,)),
            dma((2,)),
        ],
        compiler_params=pltpu.CompilerParams(
            collective_id=0, has_side_effects=True, vmem_limit_bytes=60 << 20
        ),
    )(
        waves, jnp.transpose(potential, (1, 0, 2)), block_index.reshape(1, -1), atom_of_slot.reshape(1, -1),
        projectors, coup, cy, cx, cxt, wz, wzt,
    )
    return pl.pallas_call(
        last_kernel,
        name="finish",
        out_shape=jax.ShapeDtypeStruct(waves.shape, BF16),
        in_specs=[hbm] * 3,
        out_specs=hbm,
        scratch_shapes=[
            pltpu.VMEM((96, 256), BF16),
            pltpu.VMEM((G, 8, 896), BF16),
            pltpu.VMEM((2, T, 48, N), BF16),
            pltpu.VMEM((2, T, 48, N), BF16),
            pltpu.VMEM((2, T, 96, N), BF16),
            pltpu.VMEM((2, T, 48, N), BF16),
            pltpu.VMEM((2, T, 48, N), BF16),
            dma((4,)),
            dma((5,)),
        ],
        compiler_params=pltpu.CompilerParams(vmem_limit_bytes=60 << 20),
    )(cyt, recv, waves)


def solution(mesh):
    in_specs = (
        P("band", "grid", None, None),
        P(None, "grid", None),
        P("grid"),
        P("grid"),
        P("grid", None, None),
        P("grid", None, None),
    )
    out_specs = P("band", "grid", None, None)
    return jax.shard_map(shards, mesh=mesh, in_specs=in_specs, out_specs=out_specs, check_vma=False)
```

```python
import functools
import math

import jax
import jax.numpy as jnp
import ml_dtypes
import numpy as np
from jax import lax
from jax.experimental import pallas as pl
from jax.experimental.pallas import tpu as pltpu
from jax.sharding import PartitionSpec as P

MESH = pl.DeviceIdType.MESH
F32, BF16 = jnp.float32, jnp.bfloat16
N, G, T = 192, 32, 6
A = 16
RAD2 = 48 * 48
KEEP = np.concatenate([np.arange(48), np.arange(144, 192)])
OFFSETS = (1, -1, 2, -2)
FIRST = ((0, 4, 0), (4, 3, 5))
SECOND = ((0, 3, 0), (3, 4, 4))


def tables():
    k = np.arange(N)
    angles = np.float32(2.0 * math.pi / N) * ((k[:, None] * k[None, :]) % N).astype(np.float32)
    c = ((np.cos(angles) + np.sin(angles)) / np.float32(math.sqrt(N))).astype(ml_dtypes.bfloat16)
    c = c.astype(np.float32)
    cy = np.zeros((G, 8, 96), np.float32)
    cy[:, :T] = c[:, KEEP].reshape(G, T, 96)
    cy = cy.reshape(256, 96)
    cx = c[:, KEEP].reshape(N, A, T).transpose(0, 2, 1).reshape(N, 96)
    wz = np.zeros((2, 96, 2, N), np.float32)
    for par in range(2):
        wz[par, :, par, :] = c[KEEP]
    wz = wz.reshape(192, 384)
    out = [cy, cy.T, cx, cx.T, wz, wz.T]
    return [np.ascontiguousarray(x).astype(ml_dtypes.bfloat16) for x in out]


def dot(a, b):
    return jnp.dot(a, b, preferred_element_type=F32)


def folded_sq(k):
    f = jnp.minimum(k, N - k)
    return f * f


def sphere_sq(kx):
    row = lax.broadcasted_iota(jnp.int32, (96, 96), 0)
    lane = lax.broadcasted_iota(jnp.int32, (96, 96), 1)
    ky = jnp.where(row < 48, row, row + 96)
    kz = jnp.where(lane < 48, lane, lane + 96)
    return folded_sq(kx) + folded_sq(ky) + folded_sq(kz)


def kept(low, high):
    w = jnp.concatenate([low, high], axis=0).astype(F32)
    return jnp.concatenate([w[:, :48], w[:, 144:]], axis=1)


def tile(x, n):
    return x[..., n * 128 : (n + 1) * 128]


def main_kernel(
    waves, pot, idx, atom, proj, coup, cy, cx, cxt, wz, wzt, out,
    wlo, whi, cyv, cxv, cxtv, wzv, wztv, potv, idxv, atomv, projv, coupv,
    projt, potc, oh1, oh2, oha, exp_up,
    send1, recv1, rs, send2, coup_out, coup_in, coef_out, coef_in,
    load_sem, s1, r1, s2, r2, self_sem, cs, cr, ks, kr,
):
    g = lax.axis_index("grid")
    active = jnp.logical_or(g < 8, g >= 24)
    ai = jnp.where(g < 8, g, g - 16)

    def peer(d):
        return lax.rem(g + d + G, G)

    wave_loads = [
        pltpu.make_async_copy(waves.at[:, :, 0:48, :], wlo, load_sem.at[0]),
        pltpu.make_async_copy(waves.at[:, :, 144:192, :], whi, load_sem.at[1]),
        pltpu.make_async_copy(cy, cyv, load_sem.at[2]),
    ]
    pairs = (
        (coup, coupv), (idx, idxv), (atom, atomv), (proj, projv), (pot, potv),
        (cx, cxv), (wz, wzv), (wzt, wztv), (cxt, cxtv),
    )
    loads = [pltpu.make_async_copy(a, b, load_sem.at[3 + n]) for n, (a, b) in enumerate(pairs)]

    @pl.when(active)
    def _():
        for copy in wave_loads:
            copy.start()

    for copy in loads:
        copy.start()

    barrier = pltpu.get_barrier_semaphore()

    for d in range(1, G):
        pl.semaphore_signal(barrier, inc=1, device_id={"grid": peer(d)}, device_id_type=MESH)

    def transform(h):
        parts = []
        wire, count, begin = FIRST[h]
        first, last = begin * 128 // 96, (begin + count + 1) * 128
        for n in range(first, -(-last // 96)):
            b, k = n // T, n % T
            inside = sphere_sq(g * T + k) < RAD2
            parts.append(jnp.where(inside, kept(wlo[b, k], whi[b, k]), 0.0))
        rhs = jnp.concatenate(parts, axis=1)
        skip = begin * 128 - first * 96
        rhs = rhs[:, skip : skip + (count + 1) * 128].astype(BF16)
        sub = lax.broadcasted_iota(jnp.int32, (G, 8, 128), 1)
        spare = dot(cyv[...], tile(rhs, count)).reshape(G, 8, 128)
        for t in range(count):
            plane = dot(cyv[...], tile(rhs, t)).reshape(G, 8, 128)
            for row, y in ((6, t), (7, t + count)):
                if y < T:
                    plane = jnp.where(sub == row, spare[:, y : y + 1, :], plane)
            send1[:, :, (wire + t) * 128 : (wire + t + 1) * 128] = plane.astype(BF16)

    @pl.when(active)
    def _():
        for copy in wave_loads:
            copy.wait()
        transform(0)

    pl.semaphore_wait(barrier, G - 1)

    my_row, place = g // A, lax.rem(g, A)
    partner = lax.rem(g + A, G)

    def half(ref, i, plan, h):
        return ref.at[i, :, pl.ds(plan[h][0] * 128, plan[h][1] * 128)]

    def remote(src, dst, send, recv, to):
        return pltpu.make_async_remote_copy(
            src_ref=src, dst_ref=dst, send_sem=send, recv_sem=recv,
            device_id={"grid": to}, device_id_type=MESH,
        )

    def whole(ref, count, plan, h, send, recv):
        chunks = half(ref, pl.ds(0, count), plan, h)
        return remote(chunks, chunks, send.at[h], recv.at[h], partner)

    def first_copy(row, n, h):
        to = row * A + lax.rem(place + n, A)
        remote(
            half(send1, to, FIRST, h), half(recv1, ai, FIRST, h), s1.at[h], r1.at[h], to
        ).start()

    @pl.when(active)
    def _():
        for h in range(2):
            if h == 1:
                transform(1)

            def across(n, carry):
                first_copy(1 - my_row, n, h)
                return carry

            def along(n, carry):
                first_copy(my_row, n, h)
                return carry

            lax.fori_loop(0, A, across, 0)
            lax.fori_loop(1, A, along, 0)
        recv1[ai] = send1[g]

    for copy in loads:
        copy.wait()
    coup_out[...] = jnp.concatenate([coupv[...], jnp.zeros((64, 96), F32)], axis=1)
    coup_copies = [
        pltpu.make_async_remote_copy(
            src_ref=coup_out, dst_ref=coup_in.at[n], send_sem=ks.at[n], recv_sem=kr.at[n],
            device_id={"grid": peer(d)}, device_id_type=MESH,
        )
        for n, d in enumerate(OFFSETS[:2])
    ]
    for copy in coup_copies:
        copy.start()

    idx_row = idxv[...]
    atom_row = atomv[...]
    atom_row = ((lax.shift_right_logical(atom_row, 5) - g + 33) & 31) * 32 + (atom_row & 31)

    def column(row):
        return jnp.transpose(jnp.broadcast_to(row.astype(F32), (128, 512))).astype(jnp.int32)

    idx_col = column(idx_row)[:, :1]
    lane = lax.broadcasted_iota(jnp.int32, (1, 9 * N), 1)
    ninth = lax.shift_right_logical(lane * 43691, 23)
    oh1[...] = jnp.where((lane - ninth * N) * 9 + ninth == idx_col, 1.0, 0.0).astype(BF16)
    row192 = lax.broadcasted_iota(jnp.int32, (N, 512), 0) * 9
    for c in range(9):
        oh2[c * N : (c + 1) * N] = jnp.where(row192 + c == idx_row, 1.0, 0.0).astype(BF16)
    lane128 = lax.broadcasted_iota(jnp.int32, (512, 128), 1)
    oha[...] = jnp.where(column(atom_row) == lane128, 1.0, 0.0).astype(BF16)
    up_row = lax.broadcasted_iota(jnp.int32, (128, 1024), 0)
    up_lane = lax.broadcasted_iota(jnp.int32, (128, 1024), 1)
    exp_up[...] = jnp.where(lax.shift_right_logical(up_lane, 7) == up_row, 1.0, 0.0).astype(BF16)
    projt[...] = jnp.swapaxes(projv[...].astype(F32), 0, 1)
    pt = potv[...].astype(F32)
    for j in range(3):
        e, o = pt[2 * j], pt[2 * j + 1]
        potc[3 * j] = e[:, :128]
        potc[3 * j + 1] = jnp.concatenate([e[:, 128:], o[:, :64]], axis=1)
        potc[3 * j + 2] = o[:, 64:]

    def wait_first(h):
        @pl.when(active)
        def _():
            whole(recv1, A - 1, FIRST, h, s1, r1).wait_recv()

        @pl.when(jnp.logical_not(active))
        def _():
            whole(recv1, A, FIRST, h, s1, r1).wait_recv()

    def arrived(h):
        wire, count, _ = FIRST[h]
        return jnp.swapaxes(recv1[:, :, wire * 128 : (wire + count) * 128].astype(F32), 0, 1)

    def folded(got, y, count):
        return tile(got[6 + y // count], y % count)

    def coef_copies(b):
        return [
            pltpu.make_async_remote_copy(
                src_ref=coef_out.at[b], dst_ref=coef_in.at[b, n], send_sem=cs.at[b, n], recv_sem=cr.at[b, n],
                device_id={"grid": peer(d)}, device_id_type=MESH,
            )
            for n, d in enumerate(OFFSETS)
        ]

    def project(b, lines):
        stacks = [
            jnp.concatenate([line[:, k * 96 : (k + 1) * 96] for k in range(T)], axis=0) for line in lines
        ]
        for j in range(3):
            rhs = jnp.concatenate([stacks[2 * j], stacks[2 * j + 1]], axis=1).astype(BF16)
            part = dot(cxv[...], rhs).astype(BF16)
            real = dot(part, wzv[...]).astype(BF16)
            for t in range(3):
                c = 3 * j + t
                rs[b, c * N : (c + 1) * N] = tile(real, t)
        rows = dot(oh1[...], rs[b])
        prod = jnp.concatenate([(projt[p] * rows).astype(BF16) for p in range(8)], axis=1)
        inter = lax.dot_general(
            prod, exp_up[...], (((1,), (1,)), ((), ())), preferred_element_type=F32
        )
        inter = jnp.transpose(inter)[:16]
        high = inter.astype(BF16)
        low = (inter - high.astype(F32)).astype(BF16)
        coef_out[b] = (dot(high, oha[...]) + dot(low, oha[...]))[:8]
        for copy in coef_copies(b):
            copy.start()

    def apply(b, coup):
        for copy in coef_copies(b):
            copy.wait()
        lane = lax.broadcasted_iota(jnp.int32, (8, 128), 1)
        coef = coef_out[b] + pltpu.roll(coef_in[b, 0], 96, 1) + pltpu.roll(coef_in[b, 1], 32, 1)
        coef = coef + jnp.where(lane < 32, pltpu.roll(coef_in[b, 2], 64, 1), 0.0)
        coef = coef + jnp.where(
            jnp.logical_and(lane >= 64, lane < 96), pltpu.roll(coef_in[b, 3], 64, 1), 0.0
        )
        coupled = [jnp.sum(coup[8 * p : 8 * p + 8] * coef, axis=0, keepdims=True) for p in range(8)]
        coupled = jnp.concatenate(coupled + [jnp.zeros((120, 128), F32)], axis=0).astype(BF16)
        chosen = lax.dot_general(
            oha[...], coupled, (((1,), (1,)), ((), ())), preferred_element_type=F32
        ).astype(BF16)
        back = projt[0] * dot(chosen, tile(exp_up[...], 0))
        for p in range(1, 8):
            back = back + projt[p] * dot(chosen, tile(exp_up[...], p))
        back = back.astype(BF16)
        spread = dot(oh2[...], back)
        lines = []
        for j in range(3):
            row = []
            for c in range(3 * j, 3 * j + 3):
                cut = slice(c * N, (c + 1) * N)
                row.append((potc[c] * rs[b, cut].astype(F32) + spread[cut]).astype(BF16))
            part = dot(jnp.concatenate(row, axis=1), wztv[...]).astype(BF16)
            part = dot(cxtv[...], part)
            for par in range(2):
                lines.append(
                    jnp.concatenate(
                        [part[k * A : (k + 1) * A, par * 96 : (par + 1) * 96] for k in range(T)], axis=1
                    )
                )
        return lines

    def send_back(lines, h):
        wire, count, _ = SECOND[h]
        rows = [line[:, : count * 128] for line in lines]
        for first in (0, count):
            spare = [
                lines[y][:, count * 128 :] if y < T else jnp.zeros((A, 128), F32)
                for y in range(first, first + count)
            ]
            rows.append(jnp.concatenate(spare, axis=1))
        rows = jnp.concatenate([row[None] for row in rows], axis=0)
        send2[:, :, wire * 128 : (wire + count) * 128] = jnp.swapaxes(rows, 0, 1).astype(BF16)

        def go(n, carry):
            i = jnp.where(n < 8, 1 - my_row, my_row) * 8 + lax.rem(n + place, 8)
            to = jnp.where(i < 8, i, i + A)

            @pl.when(to != g)
            def _():
                remote(
                    half(send2, i, SECOND, h), half(out, g, SECOND, h), s2.at[h], r2.at[h], to
                ).start()

            return carry

        lax.fori_loop(0, A, go, 0)

    wait_first(0)
    got = arrived(0)
    tails = [folded(got, y, 4) for y in range(T)]
    project(0, [jnp.concatenate([got[y], tails[y][:, :64]], axis=1) for y in range(T)])
    wait_first(1)
    got = arrived(1)
    project(1, [jnp.concatenate([tails[y][:, 64:], got[y], folded(got, y, 3)], axis=1) for y in range(T)])
    for copy in coup_copies:
        copy.wait()
    coup = coup_in[0] + pltpu.roll(coup_out[...], 32, 1) + pltpu.roll(coup_in[1], 64, 1)
    lines0 = apply(0, coup)
    send_back([line[:, :512] for line in lines0], 0)
    lines1 = apply(1, coup)
    send_back([jnp.concatenate([a[:, 512:], b], axis=1) for a, b in zip(lines0, lines1)], 1)

    @pl.when(active)
    def _():
        own = pltpu.make_async_copy(send2.at[ai], out.at[g], self_sem)
        own.start()
        for h in range(2):
            whole(send1, G - 1, FIRST, h, s1, r1).wait_send()
            whole(send2, A - 1, SECOND, h, s2, r2).wait_send()
        own.wait()
        for h in range(2):
            whole(out, G - 1, SECOND, h, s2, r2).wait_recv()

    @pl.when(jnp.logical_not(active))
    def _():
        for h in range(2):
            whole(send2, A, SECOND, h, s2, r2).wait_send()


def last_kernel(cyt, recv, waves, out, cyv, got_ref, wlo, whi, zero, low, high, load_sem, store_sem):
    g = lax.axis_index("grid")
    active = jnp.logical_or(g < 8, g >= 24)

    @pl.when(active)
    def _():
        loads = [
            pltpu.make_async_copy(a, b, load_sem.at[n])
            for n, (a, b) in enumerate(
                (
                    (recv, got_ref), (cyt, cyv),
                    (waves.at[:, :, 0:48, :], wlo), (waves.at[:, :, 144:192, :], whi),
                )
            )
        ]
        for copy in loads:
            copy.start()
        zero[...] = jnp.zeros(zero.shape, BF16)
        stores = [pltpu.make_async_copy(zero, out.at[:, :, 48:144, :], store_sem.at[0])]
        stores[0].start()
        for copy in loads:
            copy.wait()
        got = got_ref[...].astype(F32)
        sub = lax.broadcasted_iota(jnp.int32, (G, 8, 128), 1)
        planes = []
        for wire, count, _ in SECOND:
            planes += [tile(got, wire + t) for t in range(count)]
            spare = jnp.zeros((G, 8, 128), F32)
            for y in range(T):
                row = 6 + y // count
                spare = jnp.where(sub == y, tile(got, wire + y % count)[:, row : row + 1, :], spare)
            planes.append(spare)
        planes = jnp.concatenate(planes, axis=2).reshape(256, 1152).astype(BF16)
        fifth = dot(cyv[...], planes)
        for b in range(2):
            for k in range(T):
                ksq = sphere_sq(g * T + k)
                n = (b * T + k) * 96
                total = ksq.astype(F32) / RAD2 * kept(wlo[b, k], whi[b, k]) + fifth[:, n : n + 96]
                total = jnp.where(ksq < RAD2, total, 0.0)
                total = jnp.concatenate([total[:, :48], jnp.zeros((96, 96), F32), total[:, 48:]], axis=1)
                total = total.astype(BF16)
                low[b, k] = total[:48]
                high[b, k] = total[48:]
            stores += [
                pltpu.make_async_copy(low.at[b], out.at[b, :, 0:48, :], store_sem.at[1 + 2 * b]),
                pltpu.make_async_copy(high.at[b], out.at[b, :, 144:192, :], store_sem.at[2 + 2 * b]),
            ]
            stores[-2].start()
            stores[-1].start()
        for copy in stores:
            copy.wait()

    @pl.when(jnp.logical_not(active))
    def _():
        zero[...] = jnp.zeros(zero.shape, BF16)
        stores = [
            pltpu.make_async_copy(zero, out.at[:, :, n * 96 : (n + 1) * 96, :], store_sem.at[n])
            for n in range(2)
        ]
        for copy in stores:
            copy.start()
        for copy in stores:
            copy.wait()


def shards(waves, potential, block_index, atom_of_slot, projectors, coupling):
    cy, cyt, cx, cxt, wz, wzt = (jnp.asarray(x) for x in tables())
    coup = jnp.transpose(coupling, (1, 2, 0)).reshape(64, 32)
    hbm = pl.BlockSpec(memory_space=pltpu.HBM)
    dma = pltpu.SemaphoreType.DMA
    recv = pl.pallas_call(
        main_kernel,
        name="exchange_and_apply",
        out_shape=jax.ShapeDtypeStruct((G, 8, 896), BF16),
        in_specs=[hbm] * 11,
        out_specs=hbm,
        scratch_shapes=[
            pltpu.VMEM((2, T, 48, N), BF16),
            pltpu.VMEM((2, T, 48, N), BF16),
            pltpu.VMEM((256, 96), BF16),
            pltpu.VMEM((N, 96), BF16),
            pltpu.VMEM((96, N), BF16),
            pltpu.VMEM((192, 384), BF16),
            pltpu.VMEM((384, 192), BF16),
            pltpu.VMEM((T, N, N), BF16),
            pltpu.VMEM((1, 512), jnp.int32),
            pltpu.VMEM((1, 512), jnp.int32),
            pltpu.VMEM((512, 8, 128), BF16),
            pltpu.VMEM((64, 32), F32),
            pltpu.VMEM((8, 512, 128), F32),
            pltpu.VMEM((9, N, 128), F32),
            pltpu.VMEM((512, 9 * N), BF16),
            pltpu.VMEM((9 * N, 512), BF16),
            pltpu.VMEM((512, 128), BF16),
            pltpu.VMEM((128, 1024), BF16),
            pltpu.VMEM((G, 8, 896), BF16),
            pltpu.VMEM((A, 8, 896), BF16),
            pltpu.VMEM((2, 9 * N, 128), BF16),
            pltpu.VMEM((A, 8, 896), BF16),
            pltpu.VMEM((64, 128), F32),
            pltpu.VMEM((2, 64, 128), F32),
            pltpu.VMEM((2, 8, 128), F32),
            pltpu.VMEM((2, 4, 8, 128), F32),
            dma((12,)),
            dma((2,)),
            dma((2,)),
            dma((2,)),
            dma((2,)),
            dma,
            dma((2, 4)),
            dma((2, 4)),
            dma((2,)),
            dma((2,)),
        ],
        compiler_params=pltpu.CompilerParams(
            collective_id=0, has_side_effects=True, vmem_limit_bytes=60 << 20
        ),
    )(
        waves, jnp.transpose(potential, (1, 0, 2)), block_index.reshape(1, -1), atom_of_slot.reshape(1, -1),
        projectors, coup, cy, cx, cxt, wz, wzt,
    )
    return pl.pallas_call(
        last_kernel,
        name="finish",
        out_shape=jax.ShapeDtypeStruct(waves.shape, BF16),
        in_specs=[hbm] * 3,
        out_specs=hbm,
        scratch_shapes=[
            pltpu.VMEM((96, 256), BF16),
            pltpu.VMEM((G, 8, 896), BF16),
            pltpu.VMEM((2, T, 48, N), BF16),
            pltpu.VMEM((2, T, 48, N), BF16),
            pltpu.VMEM((2, T, 96, N), BF16),
            pltpu.VMEM((2, T, 48, N), BF16),
            pltpu.VMEM((2, T, 48, N), BF16),
            dma((4,)),
            dma((5,)),
        ],
        compiler_params=pltpu.CompilerParams(vmem_limit_bytes=60 << 20),
    )(cyt, recv, waves)


def solution(mesh):
    in_specs = (
        P("band", "grid", None, None),
        P(None, "grid", None),
        P("grid"),
        P("grid"),
        P("grid", None, None),
        P("grid", None, None),
    )
    out_specs = P("band", "grid", None, None)
    return jax.shard_map(shards, mesh=mesh, in_specs=in_specs, out_specs=out_specs, check_vma=False)
```

```python
import functools
import math

import jax
import jax.numpy as jnp
import ml_dtypes
import numpy as np
from jax import lax
from jax.experimental import pallas as pl
from jax.experimental.pallas import tpu as pltpu
from jax.sharding import PartitionSpec as P

MESH = pl.DeviceIdType.MESH
F32, BF16 = jnp.float32, jnp.bfloat16
N, G, T = 192, 32, 6
A = 16
RAD2 = 48 * 48
KEEP = np.concatenate([np.arange(48), np.arange(144, 192)])
OFFSETS = (1, -1, 2, -2)
FIRST = ((0, 4, 0), (4, 3, 5))
SECOND = ((0, 3, 0), (3, 4, 4))


def tables():
    k = np.arange(N)
    angles = np.float32(2.0 * math.pi / N) * ((k[:, None] * k[None, :]) % N).astype(np.float32)
    c = ((np.cos(angles) + np.sin(angles)) / np.float32(math.sqrt(N))).astype(ml_dtypes.bfloat16)
    c = c.astype(np.float32)
    cy = np.zeros((G, 8, 96), np.float32)
    cy[:, :T] = c[:, KEEP].reshape(G, T, 96)
    cy = cy.reshape(256, 96)
    cx = c[:, KEEP].reshape(N, A, T).transpose(0, 2, 1).reshape(N, 96)
    wz = np.zeros((2, 96, 2, N), np.float32)
    for par in range(2):
        wz[par, :, par, :] = c[KEEP]
    wz = wz.reshape(192, 384)
    out = [cy, cy.T, cx, cx.T, wz, wz.T]
    return [np.ascontiguousarray(x).astype(ml_dtypes.bfloat16) for x in out]


def dot(a, b):
    return jnp.dot(a, b, preferred_element_type=F32)


def folded_sq(k):
    f = jnp.minimum(k, N - k)
    return f * f


def sphere_sq(kx):
    row = lax.broadcasted_iota(jnp.int32, (96, 96), 0)
    lane = lax.broadcasted_iota(jnp.int32, (96, 96), 1)
    ky = jnp.where(row < 48, row, row + 96)
    kz = jnp.where(lane < 48, lane, lane + 96)
    return folded_sq(kx) + folded_sq(ky) + folded_sq(kz)


def kept(low, high):
    w = jnp.concatenate([low, high], axis=0).astype(F32)
    return jnp.concatenate([w[:, :48], w[:, 144:]], axis=1)


def tile(x, n):
    return x[..., n * 128 : (n + 1) * 128]


def main_kernel(
    waves, pot, idx, atom, proj, coup, cy, cx, cxt, wz, wzt, out,
    wlo, whi, cyv, cxv, cxtv, wzv, wztv, potv, idxv, atomv, projv, coupv,
    projt, potc, oh1, oh2, oha, exp_up,
    send1, recv1, rs, send2, coup_out, coup_in, coef_out, coef_in,
    load_sem, s1, r1, s2, r2, self_sem, cs, cr, ks, kr,
):
    g = lax.axis_index("grid")
    active = jnp.logical_or(g < 8, g >= 24)
    ai = jnp.where(g < 8, g, g - 16)

    def peer(d):
        return lax.rem(g + d + G, G)

    wave_loads = [
        pltpu.make_async_copy(waves.at[:, :, 0:48, :], wlo, load_sem.at[0]),
        pltpu.make_async_copy(waves.at[:, :, 144:192, :], whi, load_sem.at[1]),
        pltpu.make_async_copy(cy, cyv, load_sem.at[2]),
    ]
    pairs = (
        (coup, coupv), (idx, idxv), (atom, atomv), (proj, projv), (pot, potv),
        (cx, cxv), (wz, wzv), (wzt, wztv), (cxt, cxtv),
    )
    loads = [pltpu.make_async_copy(a, b, load_sem.at[3 + n]) for n, (a, b) in enumerate(pairs)]

    @pl.when(active)
    def _():
        for copy in wave_loads:
            copy.start()

    for copy in loads:
        copy.start()

    barrier = pltpu.get_barrier_semaphore()

    for d in range(1, G):
        pl.semaphore_signal(barrier, inc=1, device_id={"grid": peer(d)}, device_id_type=MESH)

    def transform(h):
        parts = []
        wire, count, begin = FIRST[h]
        first, last = begin * 128 // 96, (begin + count + 1) * 128
        for n in range(first, -(-last // 96)):
            b, k = n // T, n % T
            inside = sphere_sq(g * T + k) < RAD2
            parts.append(jnp.where(inside, kept(wlo[b, k], whi[b, k]), 0.0))
        rhs = jnp.concatenate(parts, axis=1)
        skip = begin * 128 - first * 96
        rhs = rhs[:, skip : skip + (count + 1) * 128].astype(BF16)
        sub = lax.broadcasted_iota(jnp.int32, (G, 8, 128), 1)
        spare = dot(cyv[...], tile(rhs, count)).reshape(G, 8, 128)
        for t in range(count):
            plane = dot(cyv[...], tile(rhs, t)).reshape(G, 8, 128)
            for row, y in ((6, t), (7, t + count)):
                if y < T:
                    plane = jnp.where(sub == row, spare[:, y : y + 1, :], plane)
            send1[:, :, (wire + t) * 128 : (wire + t + 1) * 128] = plane.astype(BF16)

    @pl.when(active)
    def _():
        for copy in wave_loads:
            copy.wait()
        transform(0)

    pl.semaphore_wait(barrier, G - 1)

    place = lax.rem(g, A)
    partner = lax.rem(g + A, G)

    def half(ref, i, plan, h):
        return ref.at[i, :, pl.ds(plan[h][0] * 128, plan[h][1] * 128)]

    def remote(src, dst, send, recv, to):
        return pltpu.make_async_remote_copy(
            src_ref=src, dst_ref=dst, send_sem=send, recv_sem=recv,
            device_id={"grid": to}, device_id_type=MESH,
        )

    def whole(ref, count, plan, h, send, recv):
        chunks = half(ref, pl.ds(0, count), plan, h)
        return remote(chunks, chunks, send.at[h], recv.at[h], partner)

    def first_copy(d, h):
        to = peer(d)
        remote(
            half(send1, to, FIRST, h), half(recv1, ai, FIRST, h), s1.at[h], r1.at[h], to
        ).start()

    @pl.when(active)
    def _():
        for h in range(2):
            if h == 1:
                transform(1)

            def go(d, carry):
                first_copy(d, h)
                return carry

            lax.fori_loop(1, G, go, 0)
        recv1[ai] = send1[g]

    for copy in loads:
        copy.wait()
    coup_out[...] = jnp.concatenate([coupv[...], jnp.zeros((64, 96), F32)], axis=1)
    coup_copies = [
        pltpu.make_async_remote_copy(
            src_ref=coup_out, dst_ref=coup_in.at[n], send_sem=ks.at[n], recv_sem=kr.at[n],
            device_id={"grid": peer(d)}, device_id_type=MESH,
        )
        for n, d in enumerate(OFFSETS[:2])
    ]
    for copy in coup_copies:
        copy.start()

    idx_row = idxv[...]
    atom_row = atomv[...]
    atom_row = ((lax.shift_right_logical(atom_row, 5) - g + 33) & 31) * 32 + (atom_row & 31)

    def column(row):
        return jnp.transpose(jnp.broadcast_to(row.astype(F32), (128, 512))).astype(jnp.int32)

    idx_col = column(idx_row)[:, :1]
    lane = lax.broadcasted_iota(jnp.int32, (1, 9 * N), 1)
    ninth = lax.shift_right_logical(lane * 43691, 23)
    oh1[...] = jnp.where((lane - ninth * N) * 9 + ninth == idx_col, 1.0, 0.0).astype(BF16)
    row192 = lax.broadcasted_iota(jnp.int32, (N, 512), 0) * 9
    for c in range(9):
        oh2[c * N : (c + 1) * N] = jnp.where(row192 + c == idx_row, 1.0, 0.0).astype(BF16)
    lane128 = lax.broadcasted_iota(jnp.int32, (512, 128), 1)
    oha[...] = jnp.where(column(atom_row) == lane128, 1.0, 0.0).astype(BF16)
    up_row = lax.broadcasted_iota(jnp.int32, (128, 1024), 0)
    up_lane = lax.broadcasted_iota(jnp.int32, (128, 1024), 1)
    exp_up[...] = jnp.where(lax.shift_right_logical(up_lane, 7) == up_row, 1.0, 0.0).astype(BF16)
    projt[...] = jnp.swapaxes(projv[...].astype(F32), 0, 1)
    pt = potv[...].astype(F32)
    for j in range(3):
        e, o = pt[2 * j], pt[2 * j + 1]
        potc[3 * j] = e[:, :128]
        potc[3 * j + 1] = jnp.concatenate([e[:, 128:], o[:, :64]], axis=1)
        potc[3 * j + 2] = o[:, 64:]

    def wait_first(h):
        @pl.when(active)
        def _():
            whole(recv1, A - 1, FIRST, h, s1, r1).wait_recv()

        @pl.when(jnp.logical_not(active))
        def _():
            whole(recv1, A, FIRST, h, s1, r1).wait_recv()

    def arrived(h):
        wire, count, _ = FIRST[h]
        return jnp.swapaxes(recv1[:, :, wire * 128 : (wire + count) * 128].astype(F32), 0, 1)

    def folded(got, y, count):
        return tile(got[6 + y // count], y % count)

    def coef_copies(b):
        return [
            pltpu.make_async_remote_copy(
                src_ref=coef_out.at[b], dst_ref=coef_in.at[b, n], send_sem=cs.at[b, n], recv_sem=cr.at[b, n],
                device_id={"grid": peer(d)}, device_id_type=MESH,
            )
            for n, d in enumerate(OFFSETS)
        ]

    def project(b, lines):
        stacks = [
            jnp.concatenate([line[:, k * 96 : (k + 1) * 96] for k in range(T)], axis=0) for line in lines
        ]
        for j in range(3):
            rhs = jnp.concatenate([stacks[2 * j], stacks[2 * j + 1]], axis=1).astype(BF16)
            part = dot(cxv[...], rhs).astype(BF16)
            real = dot(part, wzv[...]).astype(BF16)
            for t in range(3):
                c = 3 * j + t
                rs[b, c * N : (c + 1) * N] = tile(real, t)
        rows = dot(oh1[...], rs[b])
        prod = jnp.concatenate([(projt[p] * rows).astype(BF16) for p in range(8)], axis=1)
        inter = lax.dot_general(
            prod, exp_up[...], (((1,), (1,)), ((), ())), preferred_element_type=F32
        )
        inter = jnp.transpose(inter)[:16]
        high = inter.astype(BF16)
        low = (inter - high.astype(F32)).astype(BF16)
        coef_out[b] = (dot(high, oha[...]) + dot(low, oha[...]))[:8]
        for copy in coef_copies(b):
            copy.start()

    def apply(b, coup):
        for copy in coef_copies(b):
            copy.wait()
        lane = lax.broadcasted_iota(jnp.int32, (8, 128), 1)
        coef = coef_out[b] + pltpu.roll(coef_in[b, 0], 96, 1) + pltpu.roll(coef_in[b, 1], 32, 1)
        coef = coef + jnp.where(lane < 32, pltpu.roll(coef_in[b, 2], 64, 1), 0.0)
        coef = coef + jnp.where(
            jnp.logical_and(lane >= 64, lane < 96), pltpu.roll(coef_in[b, 3], 64, 1), 0.0
        )
        coupled = [jnp.sum(coup[8 * p : 8 * p + 8] * coef, axis=0, keepdims=True) for p in range(8)]
        coupled = jnp.concatenate(coupled + [jnp.zeros((120, 128), F32)], axis=0).astype(BF16)
        chosen = lax.dot_general(
            oha[...], coupled, (((1,), (1,)), ((), ())), preferred_element_type=F32
        ).astype(BF16)
        back = projt[0] * dot(chosen, tile(exp_up[...], 0))
        for p in range(1, 8):
            back = back + projt[p] * dot(chosen, tile(exp_up[...], p))
        back = back.astype(BF16)
        spread = dot(oh2[...], back)
        lines = []
        for j in range(3):
            row = []
            for c in range(3 * j, 3 * j + 3):
                cut = slice(c * N, (c + 1) * N)
                row.append((potc[c] * rs[b, cut].astype(F32) + spread[cut]).astype(BF16))
            part = dot(jnp.concatenate(row, axis=1), wztv[...]).astype(BF16)
            part = dot(cxtv[...], part)
            for par in range(2):
                lines.append(
                    jnp.concatenate(
                        [part[k * A : (k + 1) * A, par * 96 : (par + 1) * 96] for k in range(T)], axis=1
                    )
                )
        return lines

    def send_back(lines, h):
        wire, count, _ = SECOND[h]
        rows = [line[:, : count * 128] for line in lines]
        for first in (0, count):
            spare = [
                lines[y][:, count * 128 :] if y < T else jnp.zeros((A, 128), F32)
                for y in range(first, first + count)
            ]
            rows.append(jnp.concatenate(spare, axis=1))
        rows = jnp.concatenate([row[None] for row in rows], axis=0)
        send2[:, :, wire * 128 : (wire + count) * 128] = jnp.swapaxes(rows, 0, 1).astype(BF16)

        def go(n, carry):
            i = lax.rem(n + place, A)
            to = jnp.where(i < 8, i, i + A)

            @pl.when(to != g)
            def _():
                remote(
                    half(send2, i, SECOND, h), half(out, g, SECOND, h), s2.at[h], r2.at[h], to
                ).start()

            return carry

        lax.fori_loop(0, A, go, 0)

    wait_first(0)
    got = arrived(0)
    tails = [folded(got, y, 4) for y in range(T)]
    project(0, [jnp.concatenate([got[y], tails[y][:, :64]], axis=1) for y in range(T)])
    wait_first(1)
    got = arrived(1)
    project(1, [jnp.concatenate([tails[y][:, 64:], got[y], folded(got, y, 3)], axis=1) for y in range(T)])
    for copy in coup_copies:
        copy.wait()
    coup = coup_in[0] + pltpu.roll(coup_out[...], 32, 1) + pltpu.roll(coup_in[1], 64, 1)
    lines0 = apply(0, coup)
    send_back([line[:, :512] for line in lines0], 0)
    lines1 = apply(1, coup)
    send_back([jnp.concatenate([a[:, 512:], b], axis=1) for a, b in zip(lines0, lines1)], 1)

    @pl.when(active)
    def _():
        own = pltpu.make_async_copy(send2.at[ai], out.at[g], self_sem)
        own.start()
        for h in range(2):
            whole(send1, G - 1, FIRST, h, s1, r1).wait_send()
            whole(send2, A - 1, SECOND, h, s2, r2).wait_send()
        own.wait()
        for h in range(2):
            whole(out, G - 1, SECOND, h, s2, r2).wait_recv()

    @pl.when(jnp.logical_not(active))
    def _():
        for h in range(2):
            whole(send2, A, SECOND, h, s2, r2).wait_send()


def last_kernel(cyt, recv, waves, out, cyv, got_ref, wlo, whi, zero, low, high, load_sem, store_sem):
    g = lax.axis_index("grid")
    active = jnp.logical_or(g < 8, g >= 24)

    @pl.when(active)
    def _():
        loads = [
            pltpu.make_async_copy(a, b, load_sem.at[n])
            for n, (a, b) in enumerate(
                (
                    (recv, got_ref), (cyt, cyv),
                    (waves.at[:, :, 0:48, :], wlo), (waves.at[:, :, 144:192, :], whi),
                )
            )
        ]
        for copy in loads:
            copy.start()
        zero[...] = jnp.zeros(zero.shape, BF16)
        stores = [pltpu.make_async_copy(zero, out.at[:, :, 48:144, :], store_sem.at[0])]
        stores[0].start()
        for copy in loads:
            copy.wait()
        got = got_ref[...].astype(F32)
        sub = lax.broadcasted_iota(jnp.int32, (G, 8, 128), 1)
        planes = []
        for wire, count, _ in SECOND:
            planes += [tile(got, wire + t) for t in range(count)]
            spare = jnp.zeros((G, 8, 128), F32)
            for y in range(T):
                row = 6 + y // count
                spare = jnp.where(sub == y, tile(got, wire + y % count)[:, row : row + 1, :], spare)
            planes.append(spare)
        planes = jnp.concatenate(planes, axis=2).reshape(256, 1152).astype(BF16)
        fifth = dot(cyv[...], planes)
        for b in range(2):
            for k in range(T):
                ksq = sphere_sq(g * T + k)
                n = (b * T + k) * 96
                total = ksq.astype(F32) / RAD2 * kept(wlo[b, k], whi[b, k]) + fifth[:, n : n + 96]
                total = jnp.where(ksq < RAD2, total, 0.0)
                total = jnp.concatenate([total[:, :48], jnp.zeros((96, 96), F32), total[:, 48:]], axis=1)
                total = total.astype(BF16)
                low[b, k] = total[:48]
                high[b, k] = total[48:]
            stores += [
                pltpu.make_async_copy(low.at[b], out.at[b, :, 0:48, :], store_sem.at[1 + 2 * b]),
                pltpu.make_async_copy(high.at[b], out.at[b, :, 144:192, :], store_sem.at[2 + 2 * b]),
            ]
            stores[-2].start()
            stores[-1].start()
        for copy in stores:
            copy.wait()

    @pl.when(jnp.logical_not(active))
    def _():
        zero[...] = jnp.zeros(zero.shape, BF16)
        stores = [
            pltpu.make_async_copy(zero, out.at[:, :, n * 96 : (n + 1) * 96, :], store_sem.at[n])
            for n in range(2)
        ]
        for copy in stores:
            copy.start()
        for copy in stores:
            copy.wait()


def shards(waves, potential, block_index, atom_of_slot, projectors, coupling):
    cy, cyt, cx, cxt, wz, wzt = (jnp.asarray(x) for x in tables())
    coup = jnp.transpose(coupling, (1, 2, 0)).reshape(64, 32)
    hbm = pl.BlockSpec(memory_space=pltpu.HBM)
    dma = pltpu.SemaphoreType.DMA
    recv = pl.pallas_call(
        main_kernel,
        name="exchange_and_apply",
        out_shape=jax.ShapeDtypeStruct((G, 8, 896), BF16),
        in_specs=[hbm] * 11,
        out_specs=hbm,
        scratch_shapes=[
            pltpu.VMEM((2, T, 48, N), BF16),
            pltpu.VMEM((2, T, 48, N), BF16),
            pltpu.VMEM((256, 96), BF16),
            pltpu.VMEM((N, 96), BF16),
            pltpu.VMEM((96, N), BF16),
            pltpu.VMEM((192, 384), BF16),
            pltpu.VMEM((384, 192), BF16),
            pltpu.VMEM((T, N, N), BF16),
            pltpu.VMEM((1, 512), jnp.int32),
            pltpu.VMEM((1, 512), jnp.int32),
            pltpu.VMEM((512, 8, 128), BF16),
            pltpu.VMEM((64, 32), F32),
            pltpu.VMEM((8, 512, 128), F32),
            pltpu.VMEM((9, N, 128), F32),
            pltpu.VMEM((512, 9 * N), BF16),
            pltpu.VMEM((9 * N, 512), BF16),
            pltpu.VMEM((512, 128), BF16),
            pltpu.VMEM((128, 1024), BF16),
            pltpu.VMEM((G, 8, 896), BF16),
            pltpu.VMEM((A, 8, 896), BF16),
            pltpu.VMEM((2, 9 * N, 128), BF16),
            pltpu.VMEM((A, 8, 896), BF16),
            pltpu.VMEM((64, 128), F32),
            pltpu.VMEM((2, 64, 128), F32),
            pltpu.VMEM((2, 8, 128), F32),
            pltpu.VMEM((2, 4, 8, 128), F32),
            dma((12,)),
            dma((2,)),
            dma((2,)),
            dma((2,)),
            dma((2,)),
            dma,
            dma((2, 4)),
            dma((2, 4)),
            dma((2,)),
            dma((2,)),
        ],
        compiler_params=pltpu.CompilerParams(
            collective_id=0, has_side_effects=True, vmem_limit_bytes=60 << 20
        ),
    )(
        waves, jnp.transpose(potential, (1, 0, 2)), block_index.reshape(1, -1), atom_of_slot.reshape(1, -1),
        projectors, coup, cy, cx, cxt, wz, wzt,
    )
    return pl.pallas_call(
        last_kernel,
        name="finish",
        out_shape=jax.ShapeDtypeStruct(waves.shape, BF16),
        in_specs=[hbm] * 3,
        out_specs=hbm,
        scratch_shapes=[
            pltpu.VMEM((96, 256), BF16),
            pltpu.VMEM((G, 8, 896), BF16),
            pltpu.VMEM((2, T, 48, N), BF16),
            pltpu.VMEM((2, T, 48, N), BF16),
            pltpu.VMEM((2, T, 96, N), BF16),
            pltpu.VMEM((2, T, 48, N), BF16),
            pltpu.VMEM((2, T, 48, N), BF16),
            dma((4,)),
            dma((5,)),
        ],
        compiler_params=pltpu.CompilerParams(vmem_limit_bytes=60 << 20),
    )(cyt, recv, waves)


def solution(mesh):
    in_specs = (
        P("band", "grid", None, None),
        P(None, "grid", None),
        P("grid"),
        P("grid"),
        P("grid", None, None),
        P("grid", None, None),
    )
    out_specs = P("band", "grid", None, None)
    return jax.shard_map(shards, mesh=mesh, in_specs=in_specs, out_specs=out_specs, check_vma=False)
```
